32 devices in a mesh: dp: 4 (over z), tensor: 8 (over y, x, core).
Axes of the slice: x: 2, y: 2, z: 4, core: 2. Of those that a mesh axis runs over, the one named last changes fastest.
Arguments:
- block_input: bfloat16 [8192, 2048], P(('dp', 'tensor')), may hold values from -6 to 6
- segments: int32 [4, 2048], P('dp'), may hold values from 0 to 15, never falling along the last dimension, each value on 1 to 1024 neighbouring positions
- routes: int32 [8192, 8], P('dp'), may hold values from 0 to 15, all different within a row
- w_query: bfloat16 [2048, 2048], P(None, 'tensor'), as said below
- w_key: bfloat16 [2048, 2048], P(None, 'tensor'), as said below
- w_value: bfloat16 [2048, 2048], P(None, 'tensor'), may hold values from -0.125 to 0.125
- w_output: bfloat16 [2048, 2048], P('tensor'), may hold values from -0.5 to 0.5
- attn_gain: float32 [2048], replicated, may hold values from 0.5 to 1.5
- query_gain: float32 [2048], P('tensor'), may hold values from 0.5 to 1.5
- key_gain: float32 [2048], P('tensor'), may hold values from 0.5 to 1.5
- moe_gain: float32 [2048], replicated, may hold values from 0.5 to 1.5
- router: bfloat16 [2048, 16], replicated, may hold values from -0.06591797 to 0.06591797
- w_gate: bfloat16 [16, 2048, 1024], P(None, None, 'tensor'), may hold values from -0.125 to 0.125
- w_up: bfloat16 [16, 2048, 1024], P(None, None, 'tensor'), may hold values from -0.125 to 0.125
- w_down: bfloat16 [16, 1024, 2048], P(None, 'tensor'), may hold values from -1.5 to 1.5
- cotangent: bfloat16 [8192, 2048], P(('dp', 'tensor')), may hold values from -6 to 6
Outputs:
- block_output: bfloat16 [8192, 2048], P(('dp', 'tensor'))
- grad_input: float32 [8192, 2048], P(('dp', 'tensor'))
- grad_query: float32 [2048, 2048], P('dp', 'tensor')
- grad_key: float32 [2048, 2048], P('dp', 'tensor')
- grad_value: float32 [2048, 2048], P('dp', 'tensor')
- grad_output_proj: float32 [2048, 2048], P('tensor', 'dp')
- grad_attn_gain: float32 [2048], replicated
- grad_query_gain: float32 [2048], replicated
- grad_key_gain: float32 [2048], replicated
- grad_moe_gain: float32 [2048], replicated
- grad_router: float32 [2048, 16], replicated
- grad_gate: float32 [16, 2048, 1024], P(None, 'dp', 'tensor')
- grad_up: float32 [16, 2048, 1024], P(None, 'dp', 'tensor')
- grad_down: float32 [16, 1024, 2048], P(None, 'tensor', 'dp')
The draws below stay inside these ranges and needn't reach their ends.
Inputs may be any that keep to these rules, and one draw needn't show every extreme that they name: `w_query`: entries are of order one over the root of 2048. `w_key`: entries are of order one over the root of 2048.
All inputs are finite; a program needn't handle non-finite values.
Results may differ from the reference program's by a relative error of at most 0.02.
Values may be sent and summed in bfloat16 or wider, within the bound.
A program may use at most 1.1875 GiB of HBM per device.

```python
import math
import jax
import jax.numpy as jnp
import numpy as np
from jax import lax

D = 2048
HEADS = 16
HEAD_DIM = 128
EXPERT_FF = 1024
TOPK = 8
EXPERTS = 16
SEQ_LEN = 2048
SEQ_DP = 1
TOK_DP = 2048
SEQS = 4
TOKENS = 8192
CAPACITY = 1280
N_DP = 4


def column_profile(key, power):
    head_index = jnp.arange(HEADS, dtype=jnp.float32)
    rising = jnp.exp(math.log(3.0) * power * head_index / max(HEADS - 1, 1))
    jitter = jax.random.uniform(key, (HEADS * HEAD_DIM,), jnp.float32, math.log(0.7), math.log(1.4))
    return jnp.repeat(rising, HEAD_DIM) * jnp.exp(jitter)


def projection(key):
    entry_key = jax.random.fold_in(key, 11)
    scale_key = jax.random.fold_in(key, 12)
    entries = jnp.clip(jax.random.normal(entry_key, (D, D), jnp.float32), -6.0, 6.0)
    profile = column_profile(scale_key, 0.5)
    return (entries * profile[None, :] / math.sqrt(D)).astype(jnp.bfloat16)


def draw_w_query(key, part):
    return projection(jax.random.fold_in(key, 3))


def draw_w_key(key, part):
    return projection(jax.random.fold_in(key, 5))


def steps_of(stream_key, dims, shards, least, high):
    loudness = 1.0
    for dim, blocks in shards:
        steps = jax.random.uniform(jax.random.fold_in(jax.random.fold_in(stream_key, 6), dim), (blocks,), jnp.float32, least / len(shards), high / len(shards))
        loudness = loudness * jnp.repeat(jnp.exp(steps), dims[dim] // blocks).reshape((-1,) + (1,) * (len(dims) - 1 - dim))
    return loudness


def picks_of(stream_key, rows, number_of, top, lift):
    sequence = jax.random.permutation(jax.random.fold_in(stream_key, 1), number_of)
    favour = sequence
    for power in range(3):
        favour = favour * favour // number_of
    favour = favour * lift // number_of
    tickets = jax.random.randint(jax.random.fold_in(stream_key, 2), (rows, number_of), 0, 4096) + favour
    fixed_rows = jax.random.permutation(jax.random.fold_in(stream_key, 3), rows)[jnp.arange(number_of) % rows]
    tickets = jnp.where(jnp.arange(rows)[:, None] == fixed_rows[None, :], 1 << 14, tickets)
    score = tickets * number_of + jnp.arange(number_of)
    return lax.top_k(score.astype(jnp.int32), top)[1].astype(jnp.int32)


def split_up(amount, total, limit, lean):
    loads = [(1 << 20) // math.isqrt(rank ** lean) + 1 for rank in range(2, amount + 1)]
    spare, counts = total - limit - (amount - 1), [1] * (amount - 1)
    while spare > 0:
        candidates = [i for i in range(amount - 1) if counts[i] < limit]
        whole, left = sum([loads[i] for i in candidates]), spare
        for i in candidates:
            addition = min(limit - counts[i], max(1, left * loads[i] // whole), spare)
            counts[i] = counts[i] + addition
            spare = spare - addition
    return np.array([limit] + counts)


def uneven(key, count, total, limit, skew):
    if count == 2:
        one = jax.random.randint(key, (), max(1, total - limit), min(limit, total - 1) + 1)
        return jnp.stack([one, total - one])
    sizes = jnp.asarray(split_up(count, total, limit, skew), jnp.int32)
    couples = (count - 1) // 2
    donor, receiver = sizes[1:1 + 2 * couples:2], sizes[2:2 + 2 * couples:2]
    slack = jnp.minimum(donor - 1, limit - receiver)
    moved = jax.random.randint(jax.random.fold_in(key, 1), (couples,), 0, 1 << 20) % (slack + 1)
    sizes = sizes.at[1:1 + 2 * couples:2].set(donor - moved).at[2:2 + 2 * couples:2].set(receiver + moved)
    return sizes[jax.random.permutation(jax.random.fold_in(key, 2), count)]


def scatter_about(rng, dims, spread, most, split=(), kind=jnp.bfloat16):
    values = spread * jax.random.normal(rng, dims, jnp.float32)
    if split:
        values = values * steps_of(rng, dims, split, -0.22, 0.18)
    return jnp.clip(values, -most, most).astype(kind)


def setup_inputs(seed: int = 0) -> dict:
    splits = jax.random.split(jax.random.key(seed), 17)
    return {
        "block_input": scatter_about(splits[0], (TOKENS, D), 1.0, 6.0, ((0, 32),)),
        "segments": jax.vmap(lambda own: jnp.searchsorted(jnp.cumsum(uneven(own, max(4, SEQ_LEN // 128), SEQ_LEN, SEQ_LEN // 2, 2)), jnp.arange(SEQ_LEN), side="right"))(jax.random.split(splits[1], SEQS)).reshape((SEQS, SEQ_LEN)).astype(jnp.int32),
        "routes": picks_of(splits[2], TOKENS, EXPERTS, TOPK, 4096),
        "w_query": draw_w_query(jax.random.fold_in(splits[16], 71), 0),
        "w_key": draw_w_key(jax.random.fold_in(splits[16], 71), 0),
        "w_value": scatter_about(splits[5], (D, D), D ** -0.5, 0.125, ((1, 8),)),
        "w_output": scatter_about(splits[6], (D, D), (D // 16) ** -0.5, 0.5, ((0, 8),)),
        "attn_gain": jnp.clip(1.0 + 0.1 * jax.random.normal(splits[7], (D,), jnp.float32), 0.5, 1.5),
        "query_gain": jnp.clip(1.0 + 0.1 * jax.random.normal(splits[8], (D,), jnp.float32), 0.5, 1.5),
        "key_gain": jnp.clip(1.0 + 0.1 * jax.random.normal(splits[9], (D,), jnp.float32), 0.5, 1.5),
        "moe_gain": jnp.clip(1.0 + 0.1 * jax.random.normal(splits[10], (D,), jnp.float32), 0.5, 1.5),
        "router": scatter_about(splits[11], (D, EXPERTS), 0.011, 0.06591797),
        "w_gate": scatter_about(splits[12], (EXPERTS, D, EXPERT_FF), D ** -0.5, 0.125, ((2, 8),)),
        "w_up": scatter_about(splits[13], (EXPERTS, D, EXPERT_FF), D ** -0.5, 0.125, ((2, 8),)),
        "w_down": scatter_about(splits[14], (EXPERTS, EXPERT_FF, D), (max(1, EXPERT_FF // 64)) ** -0.5, 1.5, ((1, 8),)),
        "cotangent": scatter_about(splits[15], (TOKENS, D), 1.0, 6.0, ((0, 32),)),
    }


EPS = 1e-05

@jax.custom_vjp
def low(v):
    return lax.optimization_barrier(v.astype(jnp.bfloat16)).astype(jnp.float32)

@jax.custom_vjp
def low_back(v):
    return v

def low_keep(v):
    return (low(v), None)

def low_pass(kept, grad):
    return (grad,)

def back_keep(v):
    return (v, None)

def back_low(kept, grad):
    return (low(grad),)
low.defvjp(low_keep, low_pass)
low_back.defvjp(back_keep, back_low)

def rms_scale(values):
    return lax.rsqrt(lax.optimization_barrier(jnp.mean(values * values, axis=-1, keepdims=True)) + EPS)

def doc_positions(segments):
    row_length = segments.shape[1]
    token_index = jnp.broadcast_to(jnp.arange(row_length, dtype=jnp.int32)[None, :], segments.shape)
    previous = jnp.concatenate([segments[:, :1] - 1, segments[:, :-1]], axis=1)
    doc_start = jnp.where(segments != previous, token_index, jnp.zeros_like(token_index))
    return (token_index - lax.cummax(doc_start, axis=1)).astype(jnp.int32)

def route_slots(routes, capacity, experts):
    pair_count = routes.shape[0] * routes.shape[1]
    chosen = routes.reshape(pair_count)
    onehot = (chosen[:, None] == jnp.arange(experts, dtype=jnp.int32)[None, :]).astype(jnp.int32)
    earlier = (jnp.cumsum(onehot, axis=0) - onehot).astype(jnp.int32)
    position = lax.optimization_barrier(jnp.sum(earlier * onehot, axis=1)).astype(jnp.int32)
    kept_pairs = position < capacity
    slot_total = experts * capacity
    slot_index = jnp.where(kept_pairs, chosen * capacity + position, slot_total).astype(jnp.int32)
    pair_index = jnp.arange(pair_count, dtype=jnp.int32)
    pair_of_slot = jnp.zeros((slot_total,), jnp.int32).at[slot_index].set(pair_index, mode='drop')
    filled = jnp.zeros((slot_total,), jnp.int32).at[slot_index].set(jnp.ones((pair_count,), jnp.int32), mode='drop')
    return (slot_index, kept_pairs, pair_of_slot, filled)

def rope_tables(positions, head_dim):
    half_dim = head_dim // 2
    frequency = jnp.exp(jnp.arange(half_dim, dtype=jnp.float32) * (-2.0 * math.log(10000.0) / head_dim))
    angles = positions.astype(jnp.float32)[:, None] * frequency[None, :]
    return (jnp.cos(angles), jnp.sin(angles))

def rotate(values, cosine, sine_table):
    half_dim = values.shape[-1] // 2
    leading, trailing = (values[..., :half_dim], values[..., half_dim:])
    cos_heads = cosine[:, None, :]
    sin_heads = sine_table[:, None, :]
    return jnp.concatenate([leading * cos_heads - trailing * sin_heads, trailing * cos_heads + leading * sin_heads], axis=-1)

def shard_forward(params, inputs):
    w_query, w_key, w_value, w_output, attn_gain, query_gain, key_gain, moe_gain, router, w_gate, w_up, w_down = params
    hidden_in, segments, routes = inputs
    token_count = hidden_in.shape[0]
    score_scale = 1.0 / math.sqrt(HEAD_DIM)
    normed = low(hidden_in * rms_scale(hidden_in) * attn_gain)
    query_raw = low_back(jnp.dot(normed, w_query, precision=lax.Precision.HIGHEST))
    key_raw = low_back(jnp.dot(normed, w_key, precision=lax.Precision.HIGHEST))
    values = low(low_back(jnp.dot(normed, w_value, precision=lax.Precision.HIGHEST)))
    query_normed = query_raw * rms_scale(query_raw) * query_gain
    key_normed = key_raw * rms_scale(key_raw) * key_gain
    positions = doc_positions(segments).reshape(token_count)
    cosine, sine_table = rope_tables(positions, HEAD_DIM)
    queries = low(rotate(query_normed.reshape(token_count, HEADS, HEAD_DIM), cosine, sine_table))
    keys_rot = low(rotate(key_normed.reshape(token_count, HEADS, HEAD_DIM), cosine, sine_table))
    value_heads = values.reshape(token_count, HEADS, HEAD_DIM)
    segment_ids = segments.reshape(token_count)
    block_rows = min(512, SEQ_LEN)
    block_count = token_count // block_rows

    def attend(block_id):
        row_start = block_id * block_rows
        seq_start = row_start // SEQ_LEN * SEQ_LEN
        query_block = lax.dynamic_slice_in_dim(queries, row_start, block_rows, 0)
        key_block = lax.dynamic_slice_in_dim(keys_rot, seq_start, SEQ_LEN, 0)
        value_block = lax.dynamic_slice_in_dim(value_heads, seq_start, SEQ_LEN, 0)
        query_seg = lax.dynamic_slice_in_dim(segment_ids, row_start, block_rows, 0)
        key_seg = lax.dynamic_slice_in_dim(segment_ids, seq_start, SEQ_LEN, 0)
        query_pos = row_start - seq_start + jnp.arange(block_rows, dtype=jnp.int32)
        key_pos = jnp.arange(SEQ_LEN, dtype=jnp.int32)
        allowed = (query_seg[:, None] == key_seg[None, :]) & (key_pos[None, :] <= query_pos[:, None])
        scores = low_back(jnp.einsum('qhd,khd->hqk', query_block, key_block, precision=lax.Precision.HIGHEST) * score_scale)
        scores = jnp.where(allowed[None, :, :], scores, -1e+30)
        weights = jax.nn.softmax(scores, axis=-1)
        return jnp.einsum('hqk,khd->qhd', low(weights), value_block, precision=lax.Precision.HIGHEST)
    attended = lax.map(jax.checkpoint(attend), jnp.arange(block_count, dtype=jnp.int32))
    attn_heads = low(low_back(attended.reshape(token_count, D)))
    attn_total = low_back(jnp.dot(attn_heads, w_output, precision=lax.Precision.HIGHEST))
    residual = hidden_in + attn_total
    moe_in = low(residual * rms_scale(residual) * moe_gain)
    logits = low_back(jnp.dot(moe_in, router, precision=lax.Precision.HIGHEST))
    router_probs = jax.nn.softmax(logits, axis=-1)
    gate_values = jnp.take_along_axis(router_probs, routes, axis=1)
    slot_index, kept_pairs, pair_of_slot, filled = route_slots(routes, CAPACITY, EXPERTS)
    live_slots = filled.astype(jnp.float32)
    gate_slot = gate_values.reshape(token_count * TOPK)[pair_of_slot] * live_slots
    token_of_slot = (pair_of_slot // TOPK).astype(jnp.int32)

    def expert_step(moe_sum, pieces):
        rows_of, live_of, gate_of, gate_w, up_w, down_w = pieces
        slot_rows = moe_in[rows_of] * live_of[:, None]
        gate_pre = low_back(jnp.dot(slot_rows, gate_w, precision=lax.Precision.HIGHEST))
        up_pre = low_back(jnp.dot(slot_rows, up_w, precision=lax.Precision.HIGHEST))
        activated = low(jax.nn.silu(gate_pre) * up_pre)
        expert_out = low_back(jnp.dot(activated, down_w, precision=lax.Precision.HIGHEST))
        return (moe_sum.at[rows_of].add(gate_of[:, None] * expert_out), None)
    moe_total, unused_out = lax.scan(jax.checkpoint(expert_step), jnp.zeros((token_count, D), jnp.float32), (token_of_slot.reshape(EXPERTS, CAPACITY), live_slots.reshape(EXPERTS, CAPACITY), gate_slot.reshape(EXPERTS, CAPACITY), w_gate, w_up, w_down))
    return residual + moe_total

def forward(values, segments, routes):
    block_input = values[0]
    params = tuple(values[1:])
    shard_in = block_input.reshape(N_DP, TOK_DP, D)
    shard_seg = segments.reshape(N_DP, SEQ_DP, SEQ_LEN)
    shard_routes = routes.reshape(N_DP, TOK_DP, TOPK)
    remat_shard = jax.checkpoint(shard_forward)

    def step_shard(carry_none, inputs):
        return (carry_none, remat_shard(params, inputs))
    unused_carry, outputs = lax.scan(step_shard, None, (shard_in, shard_seg, shard_routes))
    return outputs.reshape(N_DP * TOK_DP, D)

def reference(block_input, segments, routes, w_query, w_key, w_value, w_output, attn_gain, query_gain, key_gain, moe_gain, router, w_gate, w_up, w_down, cotangent):
    floats = tuple((operand.astype(jnp.float32) for operand in (block_input, w_query, w_key, w_value, w_output, attn_gain, query_gain, key_gain, moe_gain, router, w_gate, w_up, w_down)))

    def wrapped(*inputs):
        return forward(inputs, segments, routes)
    result, pullback = jax.vjp(wrapped, *floats)
    gradients = pullback(cotangent.astype(jnp.float32))
    return (result.astype(jnp.bfloat16), gradients[0], gradients[1], gradients[2], gradients[3], gradients[4], gradients[5], gradients[6], gradients[7], gradients[8], gradients[9], gradients[10], gradients[11], gradients[12])
```

```python
import functools
import math

import jax
import jax.numpy as jnp
from jax import lax
from jax.experimental import pallas as pl
from jax.experimental.pallas import tpu as pltpu
from jax.sharding import PartitionSpec as P

HEAD_DIM = 128
EPS = 1e-05
NEG = -1e30
MIB = 1 << 20
BF = jnp.bfloat16
F32 = jnp.float32


def rms_scale(values):
    return lax.rsqrt(jnp.mean(values * values, axis=-1, keepdims=True) + EPS)


def dot_nn(a, b):
    return lax.dot_general(a, b, (((1,), (0,)), ((), ())), preferred_element_type=F32)


def dot_nt(a, b):
    return lax.dot_general(a, b, (((1,), (1,)), ((), ())), preferred_element_type=F32)


def dot_tn(a, b):
    return lax.dot_general(a, b, (((0,), (0,)), ((), ())), preferred_element_type=F32)


def attn_fwd_body(lo_ref, q_ref, k_ref, v_ref, sq_ref, sk_ref, o_ref, lse_ref, *, block, heads):
    qb = pl.program_id(0)
    scale = 1.0 / math.sqrt(HEAD_DIM)
    seg_q = sq_ref[...]
    row = qb * block + lax.broadcasted_iota(jnp.int32, (block, block), 0)
    col0 = lax.broadcasted_iota(jnp.int32, (block, block), 1)
    qs = [q_ref[:, h * HEAD_DIM : (h + 1) * HEAD_DIM] for h in range(heads)]

    def step(kb, carry):
        rows = pl.ds(pl.multiple_of(kb * block, block), block)
        allowed = (seg_q == sk_ref[kb]) & (kb * block + col0 <= row)
        out = []
        for h in range(heads):
            m, l, acc = carry[h]
            cols = slice(h * HEAD_DIM, (h + 1) * HEAD_DIM)
            s = jnp.where(allowed, dot_nt(qs[h], k_ref[rows, cols]) * scale, NEG)
            m_new = jnp.maximum(m, jnp.max(s, axis=1, keepdims=True))
            p = jnp.exp(s - m_new)
            alpha = jnp.exp(m - m_new)
            l = alpha * l + jnp.sum(p, axis=1, keepdims=True)
            acc = alpha * acc + dot_nn(p.astype(BF), v_ref[rows, cols])
            out.append((m_new, l, acc))
        return tuple(out)

    init = tuple(
        (
            jnp.full((block, 1), NEG, F32),
            jnp.zeros((block, 1), F32),
            jnp.zeros((block, HEAD_DIM), F32),
        )
        for _ in range(heads)
    )
    final = lax.fori_loop(lo_ref[qb], qb + 1, step, init)
    for h in range(heads):
        m, l, acc = final[h]
        o_ref[:, h * HEAD_DIM : (h + 1) * HEAD_DIM] = acc / l
        lse_ref[:, h : h + 1] = m + jnp.log(l)


def attn_fwd(lo, q, k, v, seg_col, seg_rows, block):
    tokens, cols = q.shape
    heads = cols // HEAD_DIM
    nb = tokens // block
    full = lambda shape: pl.BlockSpec(shape, lambda i, lo: (0,) * len(shape))
    return pl.pallas_call(
        functools.partial(attn_fwd_body, block=block, heads=heads),
        out_shape=(
            jax.ShapeDtypeStruct((tokens, cols), F32),
            jax.ShapeDtypeStruct((tokens, heads), F32),
        ),
        grid_spec=pltpu.PrefetchScalarGridSpec(
            num_scalar_prefetch=1,
            grid=(nb,),
            in_specs=[
                pl.BlockSpec((block, cols), lambda i, lo: (i, 0)),
                full((tokens, cols)),
                full((tokens, cols)),
                pl.BlockSpec((block, 1), lambda i, lo: (i, 0)),
                full((nb, 1, block)),
            ],
            out_specs=[
                pl.BlockSpec((block, cols), lambda i, lo: (i, 0)),
                pl.BlockSpec((block, heads), lambda i, lo: (i, 0)),
            ],
        ),
        compiler_params=pltpu.CompilerParams(vmem_limit_bytes=32 * MIB),
        cost_estimate=pl.CostEstimate(
            flops=8 * 10**9, bytes_accessed=8 * MIB, transcendentals=8 * 10**6
        ),
        name="attn_fwd",
    )(lo, q, k, v, seg_col, seg_rows)


def attn_bwd_body(
    lo_ref, q_ref, k_ref, v_ref, do_ref, o_ref, lse_ref, sq_ref, sk_ref, dq_ref, dk_ref, dv_ref, *, block, heads
):
    qb = pl.program_id(0)
    scale = 1.0 / math.sqrt(HEAD_DIM)

    @pl.when(qb == 0)
    def _():
        dk_ref[...] = jnp.zeros_like(dk_ref)
        dv_ref[...] = jnp.zeros_like(dv_ref)

    seg_q = sq_ref[...]
    row = qb * block + lax.broadcasted_iota(jnp.int32, (block, block), 0)
    col0 = lax.broadcasted_iota(jnp.int32, (block, block), 1)
    hc = [slice(h * HEAD_DIM, (h + 1) * HEAD_DIM) for h in range(heads)]
    qs = [q_ref[:, c] for c in hc]
    dos = [do_ref[:, c] for c in hc]
    lse = [lse_ref[:, h : h + 1] for h in range(heads)]
    dsum = [
        jnp.sum(dos[h].astype(F32) * o_ref[:, hc[h]], axis=1, keepdims=True) for h in range(heads)
    ]

    def step(kb, carry):
        rows = pl.ds(pl.multiple_of(kb * block, block), block)
        allowed = (seg_q == sk_ref[kb]) & (kb * block + col0 <= row)
        out = []
        for h in range(heads):
            k_blk = k_ref[rows, hc[h]]
            s = jnp.where(allowed, dot_nt(qs[h], k_blk) * scale, NEG)
            p = jnp.exp(s - lse[h])
            dp = dot_nt(dos[h], v_ref[rows, hc[h]])
            ds = (p * (dp - dsum[h])).astype(BF)
            dv_ref[rows, hc[h]] += dot_tn(p.astype(BF), dos[h])
            dk_ref[rows, hc[h]] += dot_tn(ds, qs[h]) * scale
            out.append(carry[h] + dot_nn(ds, k_blk))
        return tuple(out)

    init = tuple(jnp.zeros((block, HEAD_DIM), F32) for _ in range(heads))
    final = lax.fori_loop(lo_ref[qb], qb + 1, step, init)
    for h in range(heads):
        dq_ref[:, hc[h]] = final[h] * scale


def attn_bwd(lo, q, k, v, do, o, lse, seg_col, seg_rows, block):
    tokens, cols = q.shape
    heads = cols // HEAD_DIM
    nb = tokens // block
    full = lambda shape: pl.BlockSpec(shape, lambda i, lo: (0,) * len(shape))
    rowed = lambda c: pl.BlockSpec((block, c), lambda i, lo: (i, 0))
    return pl.pallas_call(
        functools.partial(attn_bwd_body, block=block, heads=heads),
        out_shape=tuple(jax.ShapeDtypeStruct((tokens, cols), F32) for _ in range(3)),
        grid_spec=pltpu.PrefetchScalarGridSpec(
            num_scalar_prefetch=1,
            grid=(nb,),
            in_specs=[
                rowed(cols),
                full((tokens, cols)),
                full((tokens, cols)),
                rowed(cols),
                rowed(cols),
                rowed(heads),
                rowed(1),
                full((nb, 1, block)),
            ],
            out_specs=[rowed(cols), full((tokens, cols)), full((tokens, cols))],
        ),
        compiler_params=pltpu.CompilerParams(vmem_limit_bytes=40 * MIB),
        cost_estimate=pl.CostEstimate(
            flops=20 * 10**9, bytes_accessed=16 * MIB, transcendentals=8 * 10**6
        ),
        name="attn_bwd",
    )(lo, q, k, v, do, o, lse, seg_col, seg_rows)


def expert_body(
    x_hbm, xt_hbm, g_hbm, gates_ref, wg_ref, wu_ref, wd_ref, _dgu_in, _ga_in,
    dgu_ref, ga_ref, dots_ref, grads_ref,
    x_v, xt_v, g_v, wcat, sem_x, sem_t, sem_g, *, first, rows_blk, parts
):
    p = pl.program_id(0)
    tokens, width = x_v.shape
    nblk = tokens // rows_blk
    hid = wg_ref.shape[2]
    experts = gates_ref.shape[1]
    ds = width // parts

    def x_copy(i):
        r = pl.ds(i * rows_blk, rows_blk)
        return pltpu.make_async_copy(x_hbm.at[r], x_v.at[r], sem_x.at[i])

    def g_copy(i):
        r = pl.ds(i * rows_blk, rows_blk)
        return pltpu.make_async_copy(g_hbm.at[r], g_v.at[r], sem_g.at[i])

    t_copy = pltpu.make_async_copy(xt_hbm, xt_v, sem_t)

    @pl.when(p == 0)
    def _():
        for i in range(nblk):
            x_copy(i).start()
            g_copy(i).start()
        t_copy.start()
        dots_ref[...] = jnp.zeros_like(dots_ref)

    wcat[:, 0:hid] = wg_ref[0]
    wcat[:, hid : 2 * hid] = wg_ref[1]
    wcat[:, 2 * hid : 3 * hid] = wu_ref[0]
    wcat[:, 3 * hid : 4 * hid] = wu_ref[1]
    lane = lax.broadcasted_iota(jnp.int32, (rows_blk, experts), 1)
    e0 = 2 * (first + p)

    def block(i, _):
        r = pl.ds(pl.multiple_of(i * rows_blk, rows_blk), rows_blk)

        @pl.when(p == 0)
        def _():
            pltpu.make_async_copy(x_hbm.at[r], x_v.at[r], sem_x.at[i]).wait()
            pltpu.make_async_copy(g_hbm.at[r], g_v.at[r], sem_g.at[i]).wait()

        gu = dot_nn(x_v[r, :], wcat[...])
        q = dot_nt(g_v[r, :], wd_ref[...])
        gate_rows = gates_ref[r, :]
        dots = dots_ref[r, :]
        for j in range(2):
            pre = gu[:, j * hid : (j + 1) * hid]
            up = gu[:, (2 + j) * hid : (3 + j) * hid]
            back = q[:, j * hid : (j + 1) * hid]
            here = lane == e0 + j
            gate = jnp.sum(jnp.where(here, gate_rows, 0.0), axis=1, keepdims=True)
            sig = jax.nn.sigmoid(pre)
            silu = pre * sig
            act = silu * up
            dot = jnp.sum(act * back, axis=1, keepdims=True)
            dots = dots + jnp.where(here, dot, 0.0)
            scaled = gate * back
            d_up = scaled * silu
            d_gate = scaled * up * (sig + silu * (1.0 - sig))
            dgu_ref[0, r, j * hid : (j + 1) * hid] = d_gate.astype(BF)
            dgu_ref[0, r, (2 + j) * hid : (3 + j) * hid] = d_up.astype(BF)
            ga_ref[0, r, j * hid : (j + 1) * hid] = (gate * act).astype(BF)
        dots_ref[r, :] = dots
        return 0

    lax.fori_loop(0, nblk, block, 0)

    @pl.when(p == 0)
    def _():
        t_copy.wait()

    for s in range(parts):
        gd = dot_tn(ga_ref[0], g_v[:, s * ds : (s + 1) * ds]).astype(BF)
        gw = dot_nn(xt_v[s * ds : (s + 1) * ds, :], dgu_ref[0]).astype(BF)
        for j in range(2):
            grads_ref[s, 3 * j] = gw[:, j * hid : (j + 1) * hid]
            grads_ref[s, 3 * j + 1] = gw[:, (2 + j) * hid : (3 + j) * hid]
            for c in range(ds // hid):
                grads_ref[s, 3 * j + 2, c * hid : (c + 1) * hid, :] = gd[
                    j * hid : (j + 1) * hid, c * hid : (c + 1) * hid
                ]


def expert_chunk(x, xt, g, gates, wg, wu, wd, dgu, ga, *, first, pairs, parts):
    tokens, width = x.shape
    experts, _, hid = wg.shape
    rows_blk = 512
    nblk = tokens // rows_blk
    ds = width // parts
    any_spec = pl.BlockSpec(memory_space=pl.ANY)
    return pl.pallas_call(
        functools.partial(expert_body, first=first, rows_blk=rows_blk, parts=parts),
        out_shape=(
            jax.ShapeDtypeStruct(dgu.shape, BF),
            jax.ShapeDtypeStruct(ga.shape, BF),
            jax.ShapeDtypeStruct((tokens, experts), F32),
            jax.ShapeDtypeStruct((parts, pairs * 6, ds, hid), BF),
        ),
        grid=(pairs,),
        in_specs=[
            any_spec,
            any_spec,
            any_spec,
            pl.BlockSpec((tokens, experts), lambda p: (0, 0)),
            pl.BlockSpec((2, width, hid), lambda p: (first + p, 0, 0)),
            pl.BlockSpec((2, width, hid), lambda p: (first + p, 0, 0)),
            pl.BlockSpec((2 * hid, width), lambda p: (first + p, 0)),
            any_spec,
            any_spec,
        ],
        out_specs=[
            pl.BlockSpec((1, tokens, 4 * hid), lambda p: (first + p, 0, 0)),
            pl.BlockSpec((1, tokens, 2 * hid), lambda p: (first + p, 0, 0)),
            pl.BlockSpec((tokens, experts), lambda p: (0, 0)),
            pl.BlockSpec((parts, 6, ds, hid), lambda p: (0, p, 0, 0)),
        ],
        scratch_shapes=[
            pltpu.VMEM((tokens, width), BF),
            pltpu.VMEM((width, tokens), BF),
            pltpu.VMEM((tokens, width), BF),
            pltpu.VMEM((width, 4 * hid), BF),
            pltpu.SemaphoreType.DMA((nblk,)),
            pltpu.SemaphoreType.DMA,
            pltpu.SemaphoreType.DMA((nblk,)),
        ],
        input_output_aliases={7: 0, 8: 1},
        compiler_params=pltpu.CompilerParams(vmem_limit_bytes=60 * MIB),
        cost_estimate=pl.CostEstimate(
            flops=pairs * 12 * tokens * width * hid * 2,
            bytes_accessed=40 * MIB,
            transcendentals=pairs * tokens * 2 * hid,
        ),
        name="expert_chunk",
    )(x, xt, g, gates, wg, wu, wd, dgu, ga)


def expert_back_body(dgu_ref, wg_ref, wu_ref, out_ref, wcat, acc):
    p = pl.program_id(1)
    hid = wg_ref.shape[2]
    wcat[:, 0:hid] = wg_ref[0]
    wcat[:, hid : 2 * hid] = wg_ref[1]
    wcat[:, 2 * hid : 3 * hid] = wu_ref[0]
    wcat[:, 3 * hid : 4 * hid] = wu_ref[1]
    rows = 256
    cols = 1024
    for i in range(acc.shape[0] // rows):
        for j in range(acc.shape[1] // cols):
            r = slice(i * rows, (i + 1) * rows)
            c = slice(j * cols, (j + 1) * cols)
            part = dot_nt(dgu_ref[0, r, :], wcat[c, :])

            @pl.when(p == 0)
            def _():
                acc[r, c] = part

            @pl.when(p > 0)
            def _():
                acc[r, c] += part

    @pl.when(p == pl.num_programs(1) - 1)
    def _():
        out_ref[...] = acc[...].astype(BF)


def expert_back(dgu, wg, wu):
    pairs, tokens, _ = dgu.shape
    _, width, hid = wg.shape
    rows = 1024
    return pl.pallas_call(
        expert_back_body,
        out_shape=jax.ShapeDtypeStruct((tokens, width), BF),
        grid=(tokens // rows, pairs),
        in_specs=[
            pl.BlockSpec((1, rows, 4 * hid), lambda i, p: (p, i, 0)),
            pl.BlockSpec((2, width, hid), lambda i, p: (p, 0, 0)),
            pl.BlockSpec((2, width, hid), lambda i, p: (p, 0, 0)),
        ],
        out_specs=pl.BlockSpec((rows, width), lambda i, p: (i, 0)),
        scratch_shapes=[pltpu.VMEM((width, 4 * hid), BF), pltpu.VMEM((rows, width), F32)],
        compiler_params=pltpu.CompilerParams(vmem_limit_bytes=48 * MIB),
        cost_estimate=pl.CostEstimate(
            flops=2 * pairs * tokens * width * 4 * hid,
            bytes_accessed=64 * MIB,
            transcendentals=0,
        ),
        name="expert_back",
    )(dgu, wg, wu)


def swap(value, axis, size, bit):
    return lax.ppermute(value, axis, [(i, i ^ bit) for i in range(size)])


def sum_all(value, axis, size):
    bit = 1
    while bit < size:
        value = value + swap(value, axis, size, bit)
        bit *= 2
    return value


def bits_of(size):
    return [1 << b for b in range(size.bit_length() - 1)]


def scatter_sum(value, size):
    me = lax.axis_index("tensor")
    rows, cols = value.shape
    own = rows // size
    nbits = size.bit_length() - 1
    x = value.reshape((2,) * nbits + (own, cols))

    def halve(y, live, bit):
        axis = live.index(bit)
        mine = (me // bit) % 2
        send = lax.dynamic_index_in_dim(y, 1 - mine, axis, keepdims=False)
        keep = lax.dynamic_index_in_dim(y, mine, axis, keepdims=False)
        got = swap(send, "tensor", size, bit)
        return (keep.astype(F32) + got.astype(F32)).astype(BF), [b for b in live if b != bit]

    live = bits_of(size)[::-1]
    x, live = halve(x, live, 1)
    rest = bits_of(size)[1:]
    halves = []
    for order, part in ((rest, slice(0, cols // 2)), (rest[::-1], slice(cols // 2, cols))):
        y, ly = x[..., part], list(live)
        for bit in order:
            y, ly = halve(y, ly, bit)
        halves.append(y)
    return jnp.concatenate(halves, axis=-1)


def gather_rows(value, size):
    me = lax.axis_index("tensor")
    own, cols = value.shape
    rest = bits_of(size)[1:]
    halves = []

    def join(y, bit):
        got = swap(y, "tensor", size, bit)
        low = (me // bit) % 2 == 0
        return jnp.stack([jnp.where(low, y, got), jnp.where(low, got, y)], axis=0)

    for order, part in ((rest, slice(0, cols // 2)), (rest[::-1], slice(cols // 2, cols))):
        y = value[:, part]
        for bit in order:
            y = join(y, bit)
        lead = list(order[::-1])
        perm = [lead.index(b) for b in rest[::-1]]
        n = len(lead)
        y = y.transpose(tuple(perm) + (n, n + 1))
        halves.append(y)
    y = jnp.concatenate(halves, axis=-1)
    y = join(y, 1)
    n = len(rest)
    y = y.transpose(tuple(range(1, n + 1)) + (0, n + 1, n + 2))
    return y.reshape(own * size, cols)


def half_swap(values):
    pieces = []
    half = HEAD_DIM // 2
    for h in range(values.shape[1] // HEAD_DIM):
        base = h * HEAD_DIM
        pieces += [values[:, base + half : base + HEAD_DIM], values[:, base : base + half]]
    return jnp.concatenate(pieces, axis=1)


def per_device(
    block_input, segments, routes, w_query, w_key, w_value, w_output, attn_gain, query_gain, key_gain,
    moe_gain, router, w_gate, w_up, w_down, cotangent, *, n_dp, n_tensor
):
    own_rows, model_width = block_input.shape
    local_cols = w_query.shape[1]
    local_heads = local_cols // HEAD_DIM
    token_count = segments.shape[0] * segments.shape[1]
    experts = router.shape[1]
    top_count = routes.shape[1]
    hid = w_gate.shape[2]
    capacity = 5 * token_count * top_count // (4 * experts)
    me = lax.axis_index("tensor")
    rank_start = me * own_rows
    col_start = me * local_cols
    block = 256

    full_input = lax.all_gather(block_input, "tensor", axis=0, tiled=True)

    seg = segments.reshape(token_count)
    values16 = jnp.arange(16, dtype=jnp.int32)
    below = jnp.sum((seg[None, :] < values16[:, None]).astype(jnp.int32), axis=1)
    doc_start = jnp.sum(
        jnp.where(seg[:, None] == values16[None, :], below[None, :], 0), axis=1
    )
    positions = jnp.arange(token_count, dtype=jnp.int32) - doc_start
    half = HEAD_DIM // 2
    frequency = jnp.exp(
        jnp.arange(half, dtype=F32) * (-2.0 * math.log(10000.0) / HEAD_DIM)
    )
    angles = positions.astype(F32)[:, None] * frequency[None, :]
    cosine, sine = jnp.cos(angles), jnp.sin(angles)
    cos_all = jnp.concatenate([cosine] * (2 * local_heads), axis=1)
    sin_all = jnp.concatenate([-sine, sine] * local_heads, axis=1)
    cos_all, sin_all = lax.optimization_barrier((cos_all, sin_all))
    lo_block = doc_start[::block] // block
    seg_col = seg[:, None]
    seg_rows = seg.reshape(token_count // block, 1, block)

    expert_ids = jnp.arange(experts, dtype=jnp.int32)
    routed = jnp.sum(
        (routes[:, :, None] == expert_ids[None, None, :]).astype(F32), axis=1
    )
    tri = (
        jnp.arange(block, dtype=jnp.int32)[:, None] > jnp.arange(block, dtype=jnp.int32)[None, :]
    ).astype(BF)
    nb = token_count // block
    routed_b = routed.reshape(nb, block, experts)
    within = jnp.einsum("ij,bje->bie", tri, routed_b.astype(BF), preferred_element_type=F32)
    sums = jnp.sum(routed_b, axis=1)
    before = jnp.sum(
        jnp.where(
            (jnp.arange(nb)[:, None] > jnp.arange(nb)[None, :])[:, :, None], sums[None, :, :], 0.0
        ),
        axis=1,
    )
    place = within + before[:, None, :]
    mask = (routed_b * (place < capacity).astype(F32)).reshape(token_count, experts)

    full_input, w_output_in = lax.optimization_barrier((full_input, w_output))
    full_wo = lax.all_gather(w_output_in, "tensor", axis=0, tiled=True)
    full_wo, cot_in = lax.optimization_barrier((full_wo, cotangent))
    full_cot = lax.all_gather(cot_in, "tensor", axis=0, tiled=True)

    input_wide = full_input.astype(F32)
    scale_one = rms_scale(input_wide)
    normed = (input_wide * scale_one * attn_gain).astype(BF)
    w_qkv = jnp.concatenate([w_query, w_key, w_value], axis=1)
    qkv = dot_nn(normed, w_qkv)
    query_raw = qkv[:, :local_cols]
    key_raw = qkv[:, local_cols : 2 * local_cols]
    value_low = qkv[:, 2 * local_cols :].astype(BF)
    squares = jnp.stack(
        [jnp.sum(query_raw * query_raw, axis=1), jnp.sum(key_raw * key_raw, axis=1)]
    )
    squares = sum_all(squares, "tensor", n_tensor)
    scales = lax.rsqrt(squares / model_width + EPS)
    query_rs = scales[0][:, None]
    key_rs = scales[1][:, None]
    query_unit = query_raw * query_rs
    key_unit = key_raw * key_rs
    q_n = query_unit * query_gain
    k_n = key_unit * key_gain
    queries = (q_n * cos_all + half_swap(q_n) * sin_all).astype(BF)
    keys_rot = (k_n * cos_all + half_swap(k_n) * sin_all).astype(BF)
    attended, lse = attn_fwd(lo_block, queries, keys_rot, value_low, seg_col, seg_rows, block)
    attn_low = attended.astype(BF)

    own_attn = lax.all_to_all(
        attn_low.reshape(n_tensor, own_rows, local_cols), "tensor", 0, 0
    )
    own_attn = own_attn.transpose(1, 0, 2).reshape(own_rows, model_width)
    input_own = block_input.astype(F32)
    residual = input_own + dot_nn(own_attn, full_wo)
    scale_two = rms_scale(residual)
    own_moe_in = (residual * scale_two * moe_gain).astype(BF)
    moe_in = lax.all_gather(own_moe_in, "tensor", axis=0, tiled=True)

    router_probs = jax.nn.softmax(dot_nn(moe_in, router), axis=-1)
    gates = router_probs * mask
    moe_in_t = moe_in.T
    pairs_total = experts // 2
    chunk_pairs = 2
    wd_flat = w_down.reshape(experts * hid, model_width)
    dgu = jnp.zeros((pairs_total, token_count, 4 * hid), BF)
    ga = jnp.zeros((pairs_total, token_count, 2 * hid), BF)
    dots = None
    reduced = []
    for c in range(pairs_total // chunk_pairs):
        dgu, ga, dot_c, grads = expert_chunk(
            moe_in, moe_in_t, full_cot, gates, w_gate, w_up, wd_flat, dgu, ga,
            first=c * chunk_pairs, pairs=chunk_pairs, parts=n_dp,
        )
        dots = dot_c if dots is None else dots + dot_c
        reduced.append(lax.psum_scatter(grads, "dp", scatter_dimension=0, tiled=False))
    back_part = expert_back(dgu, w_gate, w_up)
    moe_back = scatter_sum(back_part, n_tensor).astype(F32)

    out_part = sum(
        dot_nn(ga[p], wd_flat[p * 2 * hid : (p + 1) * 2 * hid]) for p in range(pairs_total)
    )
    moe_out = scatter_sum(out_part.astype(BF), n_tensor).astype(F32)
    block_output = (residual + moe_out).astype(BF)

    own_dots = jnp.sum(
        lax.all_to_all(dots.reshape(n_tensor, own_rows, experts), "tensor", 0, 0), axis=0
    )
    own_mask = lax.dynamic_slice_in_dim(mask, rank_start, own_rows, 0)
    own_probs = lax.dynamic_slice_in_dim(router_probs, rank_start, own_rows, 0)
    prob_grads = own_dots * own_mask
    own_logit = (
        own_probs * (prob_grads - jnp.sum(own_probs * prob_grads, axis=1, keepdims=True))
    ).astype(BF)
    router_grad = dot_tn(own_logit, own_moe_in)
    moe_grad = moe_back + dot_nt(own_logit, router)

    unit_two = residual * scale_two
    moe_gain_grad = jnp.sum(moe_grad * unit_two, axis=0)
    scaled_two = moe_grad * moe_gain
    residual_grad = cotangent.astype(F32) + scale_two * (
        scaled_two - unit_two * jnp.mean(scaled_two * unit_two, axis=1, keepdims=True)
    )
    residual_low = gather_rows(residual_grad.astype(BF), n_tensor)
    output_grad = dot_tn(attn_low, residual_low)
    heads_grad = dot_nt(residual_low, w_output).astype(BF)

    dq_rot, dk_rot, dv = attn_bwd(
        lo_block, queries, keys_rot, value_low, heads_grad, attended, lse, seg_col, seg_rows, block
    )
    query_norm_grad = dq_rot * cos_all - half_swap(dq_rot) * sin_all
    key_norm_grad = dk_rot * cos_all - half_swap(dk_rot) * sin_all
    query_gain_grad = jnp.sum(query_norm_grad * query_unit, axis=0)
    key_gain_grad = jnp.sum(key_norm_grad * key_unit, axis=0)
    query_scaled = query_norm_grad * query_gain
    key_scaled = key_norm_grad * key_gain
    inner = jnp.stack(
        [jnp.sum(query_scaled * query_unit, axis=1), jnp.sum(key_scaled * key_unit, axis=1)]
    )
    inner = sum_all(inner, "tensor", n_tensor) / model_width
    query_grad_low = (query_rs * (query_scaled - query_unit * inner[0][:, None])).astype(BF)
    key_grad_low = (key_rs * (key_scaled - key_unit * inner[1][:, None])).astype(BF)
    qkv_grad = jnp.concatenate([query_grad_low, key_grad_low, dv.astype(BF)], axis=1)
    qkv_w_grad = dot_tn(normed, qkv_grad).astype(BF)
    normed_part = dot_nt(qkv_grad, w_qkv).astype(BF)
    normed_grad = scatter_sum(normed_part, n_tensor).astype(F32)
    scale_own = rms_scale(input_own)
    unit_one = input_own * scale_own
    attn_gain_grad = jnp.sum(normed_grad * unit_one, axis=0)
    scaled_one = normed_grad * attn_gain
    grad_input = residual_grad + scale_own * (
        scaled_one - unit_one * jnp.mean(scaled_one * unit_one, axis=1, keepdims=True)
    )

    wo_red = lax.psum_scatter(
        output_grad.astype(BF), "dp", scatter_dimension=1, tiled=True
    ).astype(F32)
    qkv_red = lax.psum_scatter(qkv_w_grad, "dp", scatter_dimension=0, tiled=True).astype(F32)
    early = jnp.concatenate([router_grad, moe_gain_grad[None, :]], axis=0)
    early = sum_all(sum_all(early, "tensor", n_tensor), "dp", n_dp)
    gains = jnp.stack(
        [
            attn_gain_grad,
            lax.dynamic_update_slice_in_dim(
                jnp.zeros((model_width,), F32), query_gain_grad, col_start, 0
            ),
            lax.dynamic_update_slice_in_dim(
                jnp.zeros((model_width,), F32), key_gain_grad, col_start, 0
            ),
        ]
    )
    gains = sum_all(sum_all(gains, "tensor", n_tensor), "dp", n_dp)

    ds = model_width // n_dp
    gate_out, up_out, down_out = [], [], []
    for r in reduced:
        r = r.reshape(2 * chunk_pairs, 3, ds, hid)
        gate_out.append(r[:, 0])
        up_out.append(r[:, 1])
        down = r[:, 2].reshape(2 * chunk_pairs, ds // hid, hid, hid)
        down_out.append(down.transpose(0, 2, 1, 3).reshape(2 * chunk_pairs, hid, ds))
    grad_gate = jnp.concatenate(gate_out, axis=0).astype(F32)
    grad_up = jnp.concatenate(up_out, axis=0).astype(F32)
    grad_down = jnp.concatenate(down_out, axis=0).astype(F32)
    return (
        block_output,
        grad_input,
        qkv_red[:, :local_cols],
        qkv_red[:, local_cols : 2 * local_cols],
        qkv_red[:, 2 * local_cols :],
        wo_red,
        gains[0],
        gains[1],
        gains[2],
        early[experts],
        early[:experts].T,
        grad_gate,
        grad_up,
        grad_down,
    )


def solution(mesh):
    rows = P(("dp", "tensor"), None)
    cols = P(None, "tensor")
    wide = P(None, None, "tensor")
    placed = (
        rows, P("dp", None), P("dp", None), cols, cols, cols, P("tensor", None), P(), P("tensor"), P("tensor"),
        P(), P(), wide, wide, P(None, "tensor", None), rows,
    )
    outs = (
        rows, rows, P("dp", "tensor"), P("dp", "tensor"), P("dp", "tensor"), P("tensor", "dp"), P(), P(), P(), P(),
        P(), P(None, "dp", "tensor"), P(None, "dp", "tensor"), P(None, "tensor", "dp"),
    )
    return jax.shard_map(
        functools.partial(
            per_device, n_dp=mesh.shape["dp"], n_tensor=mesh.shape["tensor"]
        ),
        mesh=mesh,
        in_specs=placed,
        out_specs=outs,
        check_vma=False,
    )
```

```python
import functools
import math

import jax
import jax.numpy as jnp
from jax import lax
from jax.experimental import pallas as pl
from jax.experimental.pallas import tpu as pltpu
from jax.sharding import PartitionSpec as P

HEAD_DIM = 128
EPS = 1e-05
NEG = -1e30
MIB = 1 << 20
BF = jnp.bfloat16
F32 = jnp.float32


def rms_scale(values):
    return lax.rsqrt(jnp.mean(values * values, axis=-1, keepdims=True) + EPS)


def dot_nn(a, b):
    return lax.dot_general(a, b, (((1,), (0,)), ((), ())), preferred_element_type=F32)


def dot_nt(a, b):
    return lax.dot_general(a, b, (((1,), (1,)), ((), ())), preferred_element_type=F32)


def dot_tn(a, b):
    return lax.dot_general(a, b, (((0,), (0,)), ((), ())), preferred_element_type=F32)


def partner(me, bit):
    return me + bit * (1 - 2 * ((me // bit) % 2))


def remote(src, dst, send_sem, recv_sem, target):
    return pltpu.make_async_remote_copy(
        src_ref=src,
        dst_ref=dst,
        send_sem=send_sem,
        recv_sem=recv_sem,
        device_id={"tensor": target},
        device_id_type=pl.DeviceIdType.MESH,
    )


def greet(targets):
    barrier = pltpu.get_barrier_semaphore()
    for t in targets:
        pl.semaphore_signal(
            barrier, inc=1, device_id={"tensor": t}, device_id_type=pl.DeviceIdType.MESH
        )
    pl.semaphore_wait(barrier, len(targets))


def attn_fwd_body(
    q_ref, k_ref, v_ref, sq_ref, sk_ref, o_ref, low_ref, lse_ref, own_ref, buf, send_sem, recv_sem, here_sem,
    *, block, heads, reach, size
):
    qb = pl.program_id(0)
    me = lax.axis_index("tensor")
    scale = 1.0 / math.sqrt(HEAD_DIM)
    cols_all = heads * HEAD_DIM

    @pl.when(qb == 0)
    def _():
        greet([lax.rem(me + t, size) for t in range(1, size)])

    seg_q = sq_ref[...]
    row = qb * block + lax.broadcasted_iota(jnp.int32, (block, block), 0)
    col0 = lax.broadcasted_iota(jnp.int32, (block, block), 1)
    qs = [q_ref[:, h * HEAD_DIM : (h + 1) * HEAD_DIM] for h in range(heads)]

    def step(kb, carry):
        rows = pl.ds(pl.multiple_of(kb * block, block), block)
        allowed = (seg_q == sk_ref[kb]) & (kb * block + col0 <= row)
        out = []
        for h in range(heads):
            m, l, acc = carry[h]
            cols = slice(h * HEAD_DIM, (h + 1) * HEAD_DIM)
            s = jnp.where(allowed, dot_nt(qs[h], k_ref[rows, cols]) * scale, NEG)
            m_new = jnp.maximum(m, jnp.max(s, axis=1, keepdims=True))
            p = jnp.exp(s - m_new)
            alpha = jnp.exp(m - m_new)
            l = alpha * l + jnp.sum(p, axis=1, keepdims=True)
            acc = alpha * acc + dot_nn(p.astype(BF), v_ref[rows, cols])
            out.append((m_new, l, acc))
        return tuple(out)

    init = tuple(
        (
            jnp.full((block, 1), NEG, F32),
            jnp.zeros((block, 1), F32),
            jnp.zeros((block, HEAD_DIM), F32),
        )
        for _ in range(heads)
    )
    final = lax.fori_loop(jnp.maximum(qb - reach, 0), qb + 1, step, init)
    for h in range(heads):
        m, l, acc = final[h]
        cols = slice(h * HEAD_DIM, (h + 1) * HEAD_DIM)
        out = acc / l
        o_ref[:, cols] = out
        low_ref[:, cols] = out.astype(BF)
        buf[qb, :, cols] = out.astype(BF)
        lse_ref[:, h : h + 1] = m + jnp.log(l)

    own = own_ref.shape[0]
    per = block // own

    def rows_of(dev):
        return buf.at[dev // per, pl.ds(pl.multiple_of((dev % per) * own, own), own)]

    def land(src):
        return own_ref.at[:, pl.ds(pl.multiple_of(src * cols_all, HEAD_DIM), cols_all)]

    def send(t):
        return remote(rows_of(t), land(me), send_sem.at[t], recv_sem.at[me], t)

    for j in range(per):
        dest = qb * per + j

        @pl.when(dest != me)
        def _():
            send(dest).start()

        @pl.when(dest == me)
        def _():
            pltpu.make_async_copy(rows_of(me), land(me), here_sem).start()

    @pl.when(qb == pl.num_programs(0) - 1)
    def _():
        pltpu.make_async_copy(rows_of(me), land(me), here_sem).wait()
        for t in range(1, size):
            other = lax.rem(me + t, size)
            send(other).wait_send()
            remote(
                rows_of(other), land(other), send_sem.at[other], recv_sem.at[other], other
            ).wait_recv()


def attn_fwd(q, k, v, seg_col, seg_rows, block, reach, size, cid):
    tokens, cols = q.shape
    heads = cols // HEAD_DIM
    nb = tokens // block
    full = lambda shape: pl.BlockSpec(shape, lambda i: (0,) * len(shape))
    rowed = lambda c: pl.BlockSpec((block, c), lambda i: (i, 0))
    return pl.pallas_call(
        functools.partial(attn_fwd_body, block=block, heads=heads, reach=reach, size=size),
        out_shape=(
            jax.ShapeDtypeStruct((tokens, cols), F32),
            jax.ShapeDtypeStruct((tokens, cols), BF),
            jax.ShapeDtypeStruct((tokens, heads), F32),
            jax.ShapeDtypeStruct((tokens // size, cols * size), BF),
        ),
        grid=(nb,),
        in_specs=[
            rowed(cols),
            full((tokens, cols)),
            full((tokens, cols)),
            rowed(1),
            full((nb, 1, block)),
        ],
        out_specs=[rowed(cols), rowed(cols), rowed(heads), pl.BlockSpec(memory_space=pl.ANY)],
        scratch_shapes=[
            pltpu.VMEM((nb, block, cols), BF),
            pltpu.SemaphoreType.DMA((size,)),
            pltpu.SemaphoreType.DMA((size,)),
            pltpu.SemaphoreType.DMA,
        ],
        compiler_params=pltpu.CompilerParams(
            vmem_limit_bytes=32 * MIB, collective_id=cid, has_side_effects=True
        ),
        cost_estimate=pl.CostEstimate(
            flops=10**8, bytes_accessed=4 * MIB, transcendentals=10**5
        ),
        name="attn_fwd",
    )(q, k, v, seg_col, seg_rows)


def attn_bwd_body(
    lo_ref, q_ref, k_ref, v_ref, do_ref, o_ref, lse_ref, sq_ref, sk_ref, dq_ref, dk_ref, dv_ref, *, block, heads
):
    qb = pl.program_id(0)
    scale = 1.0 / math.sqrt(HEAD_DIM)

    @pl.when(qb == 0)
    def _():
        dk_ref[...] = jnp.zeros_like(dk_ref)
        dv_ref[...] = jnp.zeros_like(dv_ref)

    seg_q = sq_ref[...]
    row = qb * block + lax.broadcasted_iota(jnp.int32, (block, block), 0)
    col0 = lax.broadcasted_iota(jnp.int32, (block, block), 1)
    hc = [slice(h * HEAD_DIM, (h + 1) * HEAD_DIM) for h in range(heads)]
    qs = [q_ref[:, c] for c in hc]
    dos = [do_ref[:, c] for c in hc]
    lse = [lse_ref[:, h : h + 1] for h in range(heads)]
    dsum = [
        jnp.sum(dos[h].astype(F32) * o_ref[:, hc[h]], axis=1, keepdims=True) for h in range(heads)
    ]

    def step(kb, carry):
        rows = pl.ds(pl.multiple_of(kb * block, block), block)
        allowed = (seg_q == sk_ref[kb]) & (kb * block + col0 <= row)
        out = []
        for h in range(heads):
            k_blk = k_ref[rows, hc[h]]
            s = jnp.where(allowed, dot_nt(qs[h], k_blk) * scale, NEG)
            p = jnp.exp(s - lse[h])
            dp = dot_nt(dos[h], v_ref[rows, hc[h]])
            ds = (p * (dp - dsum[h])).astype(BF)
            dv_ref[rows, hc[h]] += dot_tn(p.astype(BF), dos[h])
            dk_ref[rows, hc[h]] += dot_tn(ds, qs[h]) * scale
            out.append(carry[h] + dot_nn(ds, k_blk))
        return tuple(out)

    init = tuple(jnp.zeros((block, HEAD_DIM), F32) for _ in range(heads))
    final = lax.fori_loop(lo_ref[qb], qb + 1, step, init)
    for h in range(heads):
        dq_ref[:, hc[h]] = final[h] * scale


def attn_bwd(lo, q, k, v, do, o, lse, seg_col, seg_rows, block):
    tokens, cols = q.shape
    heads = cols // HEAD_DIM
    nb = tokens // block
    full = lambda shape: pl.BlockSpec(shape, lambda i, lo: (0,) * len(shape))
    rowed = lambda c: pl.BlockSpec((block, c), lambda i, lo: (i, 0))
    return pl.pallas_call(
        functools.partial(attn_bwd_body, block=block, heads=heads),
        out_shape=tuple(jax.ShapeDtypeStruct((tokens, cols), F32) for _ in range(3)),
        grid_spec=pltpu.PrefetchScalarGridSpec(
            num_scalar_prefetch=1,
            grid=(nb,),
            in_specs=[
                rowed(cols),
                full((tokens, cols)),
                full((tokens, cols)),
                rowed(cols),
                rowed(cols),
                rowed(heads),
                rowed(1),
                full((nb, 1, block)),
            ],
            out_specs=[rowed(cols), full((tokens, cols)), full((tokens, cols))],
        ),
        compiler_params=pltpu.CompilerParams(vmem_limit_bytes=40 * MIB),
        cost_estimate=pl.CostEstimate(
            flops=10**8, bytes_accessed=4 * MIB, transcendentals=10**5
        ),
        name="attn_bwd",
    )(lo, q, k, v, do, o, lse, seg_col, seg_rows)


def expert_body(*refs, first, rows_blk, parts):
    lead = first == 0
    if lead:
        x_hbm, g_hbm, gates_ref, wg_ref, wu_ref, wd_ref = refs[:6]
        dgu_ref, ga_ref, wcat, dots_ref, grads_ref, xt_hbm = refs[6:12]
        x_v, xt_v, g_v, sem_x, sem_t, sem_g = refs[12:]
    else:
        x_hbm, g_hbm, gates_ref, wg_ref, wu_ref, wd_ref, xt_hbm = refs[:7]
        dgu_ref, ga_ref, wcat, dots_ref, grads_ref = refs[10:15]
        x_v, xt_v, g_v, sem_x, sem_t, sem_g = refs[15:]
    p = pl.program_id(0)
    tokens, width = x_v.shape
    nblk = tokens // rows_blk
    hid = wg_ref.shape[2]
    experts = gates_ref.shape[1]
    ds = width // parts

    if lead:
        t_copy = pltpu.make_async_copy(xt_v, xt_hbm, sem_t)
    else:
        t_copy = pltpu.make_async_copy(xt_hbm, xt_v, sem_t)

    def copies(i):
        r = pl.ds(i * rows_blk, rows_blk)
        return (
            pltpu.make_async_copy(x_hbm.at[r], x_v.at[r], sem_x.at[i]),
            pltpu.make_async_copy(g_hbm.at[r], g_v.at[r], sem_g.at[i]),
        )

    @pl.when(p == 0)
    def _():
        for i in range(nblk):
            for c in copies(i):
                c.start()
        if not lead:
            t_copy.start()
        dots_ref[...] = jnp.zeros_like(dots_ref)

    wcat[:, 0:hid] = wg_ref[0]
    wcat[:, hid : 2 * hid] = wg_ref[1]
    wcat[:, 2 * hid : 3 * hid] = wu_ref[0]
    wcat[:, 3 * hid : 4 * hid] = wu_ref[1]
    lane = lax.broadcasted_iota(jnp.int32, (rows_blk, experts), 1)
    e0 = 2 * (first + p)

    def block(i, _):
        start = pl.multiple_of(i * rows_blk, rows_blk)
        r = pl.ds(start, rows_blk)

        @pl.when(p == 0)
        def _():
            for c in copies(i):
                c.wait()

        if lead:
            xt_v[:, r] = x_v[r, :].T
        gu = dot_nn(x_v[r, :], wcat[...])
        q = dot_nt(g_v[r, :], wd_ref[...])
        gate_rows = gates_ref[r, :]
        dots = dots_ref[r, :]
        for j in range(2):
            pre = gu[:, j * hid : (j + 1) * hid]
            up = gu[:, (2 + j) * hid : (3 + j) * hid]
            back = q[:, j * hid : (j + 1) * hid]
            here = lane == e0 + j
            gate = jnp.sum(jnp.where(here, gate_rows, 0.0), axis=1, keepdims=True)
            sig = jax.nn.sigmoid(pre)
            silu = pre * sig
            act = silu * up
            dot = jnp.sum(act * back, axis=1, keepdims=True)
            dots = dots + jnp.where(here, dot, 0.0)
            scaled = gate * back
            d_up = scaled * silu
            d_gate = scaled * up * (sig + silu * (1.0 - sig))
            dgu_ref[r, j * hid : (j + 1) * hid] = d_gate.astype(BF)
            dgu_ref[r, (2 + j) * hid : (3 + j) * hid] = d_up.astype(BF)
            ga_ref[r, j * hid : (j + 1) * hid] = (gate * act).astype(BF)
        dots_ref[r, :] = dots
        return 0

    lax.fori_loop(0, nblk, block, 0)

    @pl.when(p == 0)
    def _():
        if lead:
            t_copy.start()
        else:
            t_copy.wait()

    for s in range(parts):
        gd = dot_tn(ga_ref[...], g_v[:, s * ds : (s + 1) * ds]).astype(BF)
        gw = dot_nn(xt_v[s * ds : (s + 1) * ds, :], dgu_ref[...]).astype(BF)
        for j in range(2):
            grads_ref[s, 3 * j] = gw[:, j * hid : (j + 1) * hid]
            grads_ref[s, 3 * j + 1] = gw[:, (2 + j) * hid : (3 + j) * hid]
            for c in range(ds // hid):
                grads_ref[s, 3 * j + 2, c * hid : (c + 1) * hid, :] = gd[
                    j * hid : (j + 1) * hid, c * hid : (c + 1) * hid
                ]

    if lead:

        @pl.when(p == 0)
        def _():
            t_copy.wait()


def expert_chunk(x, g, gates, wg, wu, wd, carried, *, first, pairs, parts):
    tokens, width = x.shape
    experts, _, hid = wg.shape
    total = experts // 2
    rows_blk = 512
    nblk = tokens // rows_blk
    ds = width // parts
    lead = first == 0
    assert not lead or pairs == 1
    any_spec = pl.BlockSpec(memory_space=pl.ANY)
    colblk = lambda rows, c: pl.BlockSpec((rows, c), lambda p: (0, first + p))
    in_specs = [
        any_spec,
        any_spec,
        pl.BlockSpec((tokens, experts), lambda p: (0, 0)),
        pl.BlockSpec((2, width, hid), lambda p: (first + p, 0, 0)),
        pl.BlockSpec((2, width, hid), lambda p: (first + p, 0, 0)),
        pl.BlockSpec((2 * hid, width), lambda p: (first + p, 0)),
    ]
    out_shape = [
        jax.ShapeDtypeStruct((tokens, total * 4 * hid), BF),
        jax.ShapeDtypeStruct((tokens, total * 2 * hid), BF),
        jax.ShapeDtypeStruct((width, total * 4 * hid), BF),
        jax.ShapeDtypeStruct((tokens, experts), F32),
        jax.ShapeDtypeStruct((parts, pairs * 6, ds, hid), BF),
    ]
    out_specs = [
        colblk(tokens, 4 * hid),
        colblk(tokens, 2 * hid),
        colblk(width, 4 * hid),
        pl.BlockSpec((tokens, experts), lambda p: (0, 0)),
        pl.BlockSpec((parts, 6, ds, hid), lambda p: (0, p, 0, 0)),
    ]
    args = [x, g, gates, wg, wu, wd]
    alias = {}
    if lead:
        out_shape.append(jax.ShapeDtypeStruct((width, tokens), BF))
        out_specs.append(any_spec)
    else:
        xt, dgu, ga, wcat = carried
        args += [xt, dgu, ga, wcat]
        in_specs += [any_spec] * 4
        alias = {7: 0, 8: 1, 9: 2}
    return pl.pallas_call(
        functools.partial(expert_body, first=first, rows_blk=rows_blk, parts=parts),
        out_shape=tuple(out_shape),
        grid=(pairs,),
        in_specs=in_specs,
        out_specs=out_specs,
        scratch_shapes=[
            pltpu.VMEM((tokens, width), BF),
            pltpu.VMEM((width, tokens), BF),
            pltpu.VMEM((tokens, width), BF),
            pltpu.SemaphoreType.DMA((nblk,)),
            pltpu.SemaphoreType.DMA,
            pltpu.SemaphoreType.DMA((nblk,)),
        ],
        input_output_aliases=alias,
        compiler_params=pltpu.CompilerParams(vmem_limit_bytes=61 * MIB),
        cost_estimate=pl.CostEstimate(
            flops=10**9, bytes_accessed=4 * MIB, transcendentals=10**5
        ),
        name="expert_chunk",
    )(*args)


def matmul_scatter_body(
    l_hbm, r_hbm, out_ref, l_v, r_v, part, got1, got2, got3, sem_l, sem_r, send_sem, recv_sem,
    *, size, slices, nt
):
    me = lax.axis_index("tensor")
    tokens = l_v.shape[0]
    own = tokens // size
    sn = out_ref.shape[1] // slices
    mine = [(me // b) % 2 for b in (1, 2, 4)]
    group = 2

    def l_copy(i):
        r = pl.ds(i * own * group, own * group)
        return pltpu.make_async_copy(l_hbm.at[r], l_v.at[r], sem_l.at[i])

    def r_copy(s):
        c = pl.ds(s * sn, sn)
        if nt:
            return pltpu.make_async_copy(r_hbm.at[c], r_v.at[c], sem_r.at[s])
        return pltpu.make_async_copy(r_hbm.at[:, c], r_v.at[:, c], sem_r.at[s])

    r_copy(0).start()
    for i in range(size // group):
        l_copy(i).start()
    for s in range(1, slices):
        r_copy(s).start()
    greet([partner(me, b) for b in (1, 2, 4)])

    def hop(s, stage):
        a, b = (1, 2) if s % 2 == 0 else (2, 1)
        if stage == 0:
            src, dst, bit = part.at[s, 1 - mine[0]], got1.at[s], 1
        elif stage == 1:
            src, dst, bit = part.at[s, mine[0], pl.ds(2 * (1 - mine[a]), 2)], got2.at[s], 1 << a
        else:
            src, dst, bit = part.at[s, mine[0], 2 * mine[a] + 1 - mine[b]], got3.at[s], 1 << b
        return remote(src, dst, send_sem.at[stage, s], recv_sem.at[stage, s], partner(me, bit))

    def compute(s):
        r_copy(s).wait()

        def rows(i, _):
            if s == 0:
                l_copy(i).wait()
            r = pl.ds(pl.multiple_of(i * own * group, own * group), own * group)
            if nt:
                res = dot_nt(l_v[r, :], r_v[s * sn : (s + 1) * sn, :])
            else:
                res = dot_nn(l_v[r, :], r_v[:, s * sn : (s + 1) * sn])
            res = res.astype(BF)
            x, y = i % 2, i // 2
            pos = 2 * x + y if s % 2 == 0 else 2 * y + x
            for c in range(2):
                part[s, c, pos] = res[c * own : (c + 1) * own]
            return 0

        lax.fori_loop(0, size // group, rows, 0)
        hop(s, 0).start()

    def first(s):
        hop(s, 0).wait_recv()
        part[s, mine[0]] = (part[s, mine[0]].astype(F32) + got1[s].astype(F32)).astype(BF)
        hop(s, 1).start()

    def second(s):
        a = 1 if s % 2 == 0 else 2
        hop(s, 1).wait_recv()
        ix = pl.ds(2 * mine[a], 2)
        part[s, mine[0], ix] = (part[s, mine[0], ix].astype(F32) + got2[s].astype(F32)).astype(BF)
        hop(s, 2).start()

    def third(s):
        a, b = (1, 2) if s % 2 == 0 else (2, 1)
        hop(s, 2).wait_recv()
        out_ref[:, s * sn : (s + 1) * sn] = part[s, mine[0], 2 * mine[a] + mine[b]].astype(
            F32
        ) + got3[s].astype(F32)

    for t in range(slices + 5):
        if t < slices:
            compute(t)
        if 0 <= t - 1 < slices:
            first(t - 1)
        if 0 <= t - 3 < slices:
            second(t - 3)
        if 0 <= t - 5 < slices:
            third(t - 5)
    for s in range(slices):
        for stage in range(3):
            hop(s, stage).wait_send()


def matmul_scatter(left, right, size, cid, nt, name):
    tokens, depth = left.shape
    width = right.shape[0] if nt else right.shape[1]
    own = tokens // size
    if size != 8:
        part = (dot_nt if nt else dot_nn)(left, right).astype(BF)
        return lax.psum_scatter(part, "tensor", scatter_dimension=0, tiled=True).astype(F32)
    slices = 8
    sn = width // slices
    any_spec = pl.BlockSpec(memory_space=pl.ANY)
    return pl.pallas_call(
        functools.partial(matmul_scatter_body, size=size, slices=slices, nt=nt),
        out_shape=jax.ShapeDtypeStruct((own, width), F32),
        in_specs=[any_spec, any_spec],
        out_specs=pl.BlockSpec(memory_space=pltpu.VMEM),
        scratch_shapes=[
            pltpu.VMEM(left.shape, BF),
            pltpu.VMEM(right.shape, BF),
            pltpu.VMEM((slices, 2, size // 2, own, sn), BF),
            pltpu.VMEM((slices, size // 2, own, sn), BF),
            pltpu.VMEM((slices, size // 4, own, sn), BF),
            pltpu.VMEM((slices, own, sn), BF),
            pltpu.SemaphoreType.DMA((size // 2,)),
            pltpu.SemaphoreType.DMA((slices,)),
            pltpu.SemaphoreType.DMA((3, slices)),
            pltpu.SemaphoreType.DMA((3, slices)),
        ],
        compiler_params=pltpu.CompilerParams(
            vmem_limit_bytes=60 * MIB, collective_id=cid, has_side_effects=True
        ),
        cost_estimate=pl.CostEstimate(
            flops=10**9, bytes_accessed=4 * MIB, transcendentals=0
        ),
        name=name,
    )(left, right)


def gather_body(x_ref, out_ref, send_sem, recv_sem, here_sem):
    me = lax.axis_index("tensor")
    own = x_ref.shape[0]
    half = own // 2
    pc, px, py = (partner(me, b) for b in (1, 2, 4))
    diag = partner(px, 4)
    greet([pc, px, py])

    def piece(dev, a, n):
        return out_ref.at[pl.ds(pl.multiple_of(dev * own + a, half), n)]

    here = pltpu.make_async_copy(x_ref, piece(me, 0, own), here_sem)
    here.start()
    plan = [
        (me, 0, half, px),
        (me, half, half, py),
        (me, half, half, px),
        (me, 0, half, py),
        (me, 0, own, pc),
        (px, 0, half, py),
        (py, half, half, px),
        (px, 0, half, pc),
        (py, half, half, pc),
        (px, half, half, pc),
        (py, 0, half, pc),
        (diag, 0, half, pc),
        (diag, half, half, pc),
    ]

    def copy(k):
        dev, a, n, target = plan[k]
        src = x_ref.at[pl.ds(a, n)] if k < 5 else piece(dev, a, n)
        return remote(src, piece(dev, a, n), send_sem.at[k], recv_sem.at[k], target)

    def arrived(k):
        dev, a, n, target = plan[k]
        bit_dev = {0: px, 1: py, 2: px, 3: py, 4: pc, 5: diag, 6: diag}
        if k in bit_dev:
            src = bit_dev[k]
        else:
            src = partner(dev, 1)
        return remote(piece(src, a, n), piece(src, a, n), send_sem.at[k], recv_sem.at[k], target)

    for k in range(5):
        copy(k).start()
    arrived(0).wait_recv()
    copy(5).start()
    copy(7).start()
    arrived(1).wait_recv()
    copy(6).start()
    copy(8).start()
    arrived(2).wait_recv()
    copy(9).start()
    arrived(3).wait_recv()
    copy(10).start()
    arrived(5).wait_recv()
    copy(11).start()
    arrived(6).wait_recv()
    copy(12).start()
    for k in (4, 7, 8, 9, 10, 11, 12):
        arrived(k).wait_recv()
    for k in range(13):
        copy(k).wait_send()
    here.wait()


def gather_all(value, size, cid, name):
    own, cols = value.shape
    if size != 8:
        return lax.all_gather(value, "tensor", axis=0, tiled=True)
    any_spec = pl.BlockSpec(memory_space=pl.ANY)
    return pl.pallas_call(
        gather_body,
        out_shape=jax.ShapeDtypeStruct((own * size, cols), value.dtype),
        in_specs=[any_spec],
        out_specs=any_spec,
        scratch_shapes=[
            pltpu.SemaphoreType.DMA((13,)),
            pltpu.SemaphoreType.DMA((13,)),
            pltpu.SemaphoreType.DMA,
        ],
        compiler_params=pltpu.CompilerParams(collective_id=cid, has_side_effects=True),
        cost_estimate=pl.CostEstimate(flops=0, bytes_accessed=4 * MIB, transcendentals=0),
        name=name,
    )(value)


def swap(value, axis, size, bit):
    return lax.ppermute(value, axis, [(i, i ^ bit) for i in range(size)])


def sum_all(value, axis, size):
    bit = 1
    while bit < size:
        value = value + swap(value, axis, size, bit)
        bit *= 2
    return value


def bits_of(size):
    return [1 << b for b in range(size.bit_length() - 1)]


def half_swap(values):
    pieces = []
    half = HEAD_DIM // 2
    for h in range(values.shape[1] // HEAD_DIM):
        base = h * HEAD_DIM
        pieces += [values[:, base + half : base + HEAD_DIM], values[:, base : base + half]]
    return jnp.concatenate(pieces, axis=1)


def per_device(
    block_input, segments, routes, w_query, w_key, w_value, w_output, attn_gain, query_gain, key_gain,
    moe_gain, router, w_gate, w_up, w_down, cotangent, *, n_dp, n_tensor
):
    own_rows, model_width = block_input.shape
    local_cols = w_query.shape[1]
    local_heads = local_cols // HEAD_DIM
    token_count = segments.shape[0] * segments.shape[1]
    experts = router.shape[1]
    top_count = routes.shape[1]
    hid = w_gate.shape[2]
    capacity = 5 * token_count * top_count // (4 * experts)
    me = lax.axis_index("tensor")
    rank_start = me * own_rows
    col_start = me * local_cols
    block = 256

    full_input = lax.all_gather(block_input, "tensor", axis=0, tiled=True)

    seg = segments.reshape(token_count)
    values16 = jnp.arange(16, dtype=jnp.int32)
    below = jnp.sum((seg[None, :] < values16[:, None]).astype(jnp.int32), axis=1)
    doc_start = jnp.sum(
        jnp.where(seg[:, None] == values16[None, :], below[None, :], 0), axis=1
    )
    positions = jnp.arange(token_count, dtype=jnp.int32) - doc_start
    half = HEAD_DIM // 2
    frequency = jnp.exp(
        jnp.arange(half, dtype=F32) * (-2.0 * math.log(10000.0) / HEAD_DIM)
    )
    angles = positions.astype(F32)[:, None] * frequency[None, :]
    cosine, sine = jnp.cos(angles), jnp.sin(angles)
    cos_all = jnp.concatenate([cosine] * (2 * local_heads), axis=1)
    sin_all = jnp.concatenate([-sine, sine] * local_heads, axis=1)
    cos_all, sin_all = lax.optimization_barrier((cos_all, sin_all))
    lo_block = doc_start[::block] // block
    seg_col = seg[:, None]
    seg_rows = seg.reshape(token_count // block, 1, block)

    expert_ids = jnp.arange(experts, dtype=jnp.int32)
    routed = jnp.sum(
        (routes[:, :, None] == expert_ids[None, None, :]).astype(F32), axis=1
    )
    tri = (
        jnp.arange(block, dtype=jnp.int32)[:, None] > jnp.arange(block, dtype=jnp.int32)[None, :]
    ).astype(BF)
    nb = token_count // block
    routed_b = routed.reshape(nb, block, experts)
    within = jnp.einsum("ij,bje->bie", tri, routed_b.astype(BF), preferred_element_type=F32)
    sums = jnp.sum(routed_b, axis=1)
    before = jnp.sum(
        jnp.where(
            (jnp.arange(nb)[:, None] > jnp.arange(nb)[None, :])[:, :, None], sums[None, :, :], 0.0
        ),
        axis=1,
    )
    place = within + before[:, None, :]
    mask = (routed_b * (place < capacity).astype(F32)).reshape(token_count, experts)

    w_qkv = jnp.concatenate([w_query, w_key, w_value], axis=1)
    full_input, cos_all, sin_all, mask, w_qkv, lo_block, seg_col, seg_rows = lax.optimization_barrier(
        (full_input, cos_all, sin_all, mask, w_qkv, lo_block, seg_col, seg_rows)
    )
    full_input, w_output_in = lax.optimization_barrier((full_input, w_output))
    full_wo = lax.all_gather(w_output_in, "tensor", axis=0, tiled=True)

    input_wide = full_input.astype(F32)
    scale_one = rms_scale(input_wide)
    normed = (input_wide * scale_one * attn_gain).astype(BF)
    qkv = dot_nn(normed, w_qkv)
    query_raw = qkv[:, :local_cols]
    key_raw = qkv[:, local_cols : 2 * local_cols]
    value_low = qkv[:, 2 * local_cols :].astype(BF)
    squares = jnp.stack(
        [jnp.sum(query_raw * query_raw, axis=1), jnp.sum(key_raw * key_raw, axis=1)]
    )
    squares = sum_all(squares, "tensor", n_tensor)
    scales = lax.rsqrt(squares / model_width + EPS)
    query_rs = scales[0][:, None]
    key_rs = scales[1][:, None]
    query_unit = query_raw * query_rs
    key_unit = key_raw * key_rs
    q_n = query_unit * query_gain
    k_n = key_unit * key_gain
    queries = (q_n * cos_all + half_swap(q_n) * sin_all).astype(BF)
    keys_rot = (k_n * cos_all + half_swap(k_n) * sin_all).astype(BF)
    reach = min(1024 // block, token_count // block)
    attended, attn_low, lse, own_attn = attn_fwd(
        queries, keys_rot, value_low, seg_col, seg_rows, block, reach, n_tensor, 0
    )

    own_attn, cot_in = lax.optimization_barrier((own_attn, cotangent))
    full_cot = lax.all_gather(cot_in, "tensor", axis=0, tiled=True)

    input_own = block_input.astype(F32)
    residual = input_own + dot_nn(own_attn, full_wo)
    scale_two = rms_scale(residual)
    own_moe_in = (residual * scale_two * moe_gain).astype(BF)
    moe_in = gather_all(own_moe_in, n_tensor, 1, "gather_moe")

    router_probs = jax.nn.softmax(dot_nn(moe_in, router), axis=-1)
    gates = router_probs * mask
    wd_flat = w_down.reshape(experts * hid, model_width)
    pairs_total = experts // 2
    chunks = (1, 4, 3)
    dots = None
    reduced = []
    carried = None
    first = 0
    for count in chunks:
        res = expert_chunk(
            moe_in, full_cot, gates, w_gate, w_up, wd_flat, carried,
            first=first, pairs=count, parts=n_dp,
        )
        dgu, ga, wcat, dot_c, grads = res[:5]
        xt = res[5] if first == 0 else carried[0]
        if len(reduced) == 1:
            reduced[0], dgu = lax.optimization_barrier((reduced[0], dgu))
        carried = (xt, dgu, ga, wcat)
        dots = dot_c if dots is None else dots + dot_c
        if first + count < pairs_total:
            reduced.append(lax.psum_scatter(grads, "dp", scatter_dimension=0, tiled=False))
        first += count
    moe_back = matmul_scatter(dgu, wcat, n_tensor, 2, True, "moe_back")

    own_dots = jnp.sum(
        lax.all_to_all(dots.reshape(n_tensor, own_rows, experts), "tensor", 0, 0), axis=0
    )
    own_mask = lax.dynamic_slice_in_dim(mask, rank_start, own_rows, 0)
    own_probs = lax.dynamic_slice_in_dim(router_probs, rank_start, own_rows, 0)
    prob_grads = own_dots * own_mask
    own_logit = (
        own_probs * (prob_grads - jnp.sum(own_probs * prob_grads, axis=1, keepdims=True))
    ).astype(BF)
    router_grad = dot_tn(own_logit, own_moe_in)
    moe_grad = moe_back + dot_nt(own_logit, router)

    unit_two = residual * scale_two
    moe_gain_grad = jnp.sum(moe_grad * unit_two, axis=0)
    scaled_two = moe_grad * moe_gain
    residual_grad = cotangent.astype(F32) + scale_two * (
        scaled_two - unit_two * jnp.mean(scaled_two * unit_two, axis=1, keepdims=True)
    )
    residual_low = gather_all(residual_grad.astype(BF), n_tensor, 3, "gather_residual")
    output_grad = dot_tn(residual_low, attn_low).astype(BF)
    heads_grad = dot_nt(residual_low, w_output).astype(BF)

    dq_rot, dk_rot, dv = attn_bwd(
        lo_block, queries, keys_rot, value_low, heads_grad, attended, lse, seg_col, seg_rows, block
    )
    reduced[1], grads, dq_rot = lax.optimization_barrier((reduced[1], grads, dq_rot))
    reduced.append(lax.psum_scatter(grads, "dp", scatter_dimension=0, tiled=False))
    query_norm_grad = dq_rot * cos_all - half_swap(dq_rot) * sin_all
    key_norm_grad = dk_rot * cos_all - half_swap(dk_rot) * sin_all
    query_gain_grad = jnp.sum(query_norm_grad * query_unit, axis=0)
    key_gain_grad = jnp.sum(key_norm_grad * key_unit, axis=0)
    query_scaled = query_norm_grad * query_gain
    key_scaled = key_norm_grad * key_gain
    inner = jnp.stack(
        [jnp.sum(query_scaled * query_unit, axis=1), jnp.sum(key_scaled * key_unit, axis=1)]
    )
    inner = sum_all(inner, "tensor", n_tensor) / model_width
    query_grad_low = (query_rs * (query_scaled - query_unit * inner[0][:, None])).astype(BF)
    key_grad_low = (key_rs * (key_scaled - key_unit * inner[1][:, None])).astype(BF)
    qkv_grad = jnp.concatenate([query_grad_low, key_grad_low, dv.astype(BF)], axis=1)
    qkv_w_grad = dot_tn(normed, qkv_grad).astype(BF)
    normed_grad = matmul_scatter(qkv_grad, w_qkv, n_tensor, 4, True, "normed_back")
    moe_out = matmul_scatter(ga, wd_flat, n_tensor, 5, False, "moe_out")
    block_output = (residual + moe_out).astype(BF)
    scale_own = rms_scale(input_own)
    unit_one = input_own * scale_own
    attn_gain_grad = jnp.sum(normed_grad * unit_one, axis=0)
    scaled_one = normed_grad * attn_gain
    grad_input = residual_grad + scale_own * (
        scaled_one - unit_one * jnp.mean(scaled_one * unit_one, axis=1, keepdims=True)
    )

    proj_grad = jnp.concatenate([qkv_w_grad, output_grad], axis=1)
    reduced[2], proj_grad, block_output, grad_input = lax.optimization_barrier(
        (reduced[2], proj_grad, block_output, grad_input)
    )
    qkv_red = lax.psum_scatter(proj_grad, "dp", scatter_dimension=0, tiled=True).astype(F32)
    wo_red = qkv_red[:, 3 * local_cols :].T
    early = jnp.concatenate([router_grad, moe_gain_grad[None, :]], axis=0)
    early = sum_all(sum_all(early, "tensor", n_tensor), "dp", n_dp)
    gains = jnp.stack(
        [
            attn_gain_grad,
            lax.dynamic_update_slice_in_dim(
                jnp.zeros((model_width,), F32), query_gain_grad, col_start, 0
            ),
            lax.dynamic_update_slice_in_dim(
                jnp.zeros((model_width,), F32), key_gain_grad, col_start, 0
            ),
        ]
    )
    gains = sum_all(sum_all(gains, "tensor", n_tensor), "dp", n_dp)

    ds = model_width // n_dp
    gate_out, up_out, down_out = [], [], []
    for r, count in zip(reduced, chunks):
        r = r.reshape(2 * count, 3, ds, hid)
        gate_out.append(r[:, 0])
        up_out.append(r[:, 1])
        down = r[:, 2].reshape(2 * count, ds // hid, hid, hid)
        down_out.append(down.transpose(0, 2, 1, 3).reshape(2 * count, hid, ds))
    grad_gate = jnp.concatenate(gate_out, axis=0).astype(F32)
    grad_up = jnp.concatenate(up_out, axis=0).astype(F32)
    grad_down = jnp.concatenate(down_out, axis=0).astype(F32)
    return (
        block_output,
        grad_input,
        qkv_red[:, :local_cols],
        qkv_red[:, local_cols : 2 * local_cols],
        qkv_red[:, 2 * local_cols : 3 * local_cols],
        wo_red,
        gains[0],
        gains[1],
        gains[2],
        early[experts],
        early[:experts].T,
        grad_gate,
        grad_up,
        grad_down,
    )


def solution(mesh):
    rows = P(("dp", "tensor"), None)
    cols = P(None, "tensor")
    wide = P(None, None, "tensor")
    placed = (
        rows, P("dp", None), P("dp", None), cols, cols, cols, P("tensor", None), P(), P("tensor"), P("tensor"),
        P(), P(), wide, wide, P(None, "tensor", None), rows,
    )
    outs = (
        rows, rows, P("dp", "tensor"), P("dp", "tensor"), P("dp", "tensor"), P("tensor", "dp"), P(), P(), P(), P(),
        P(), P(None, "dp", "tensor"), P(None, "dp", "tensor"), P(None, "tensor", "dp"),
    )
    return jax.shard_map(
        functools.partial(
            per_device, n_dp=mesh.shape["dp"], n_tensor=mesh.shape["tensor"]
        ),
        mesh=mesh,
        in_specs=placed,
        out_specs=outs,
        check_vma=False,
    )
```

```python
import functools
import math

import jax
import jax.numpy as jnp
from jax import lax
from jax.experimental import pallas as pl
from jax.experimental.pallas import tpu as pltpu
from jax.sharding import PartitionSpec as P

HEAD_DIM = 128
EPS = 1e-05
NEG = -1e30
MIB = 1 << 20
BF = jnp.bfloat16
F32 = jnp.float32


def rms_scale(values):
    return lax.rsqrt(jnp.mean(values * values, axis=-1, keepdims=True) + EPS)


def dot_nn(a, b):
    return lax.dot_general(a, b, (((1,), (0,)), ((), ())), preferred_element_type=F32)


def dot_nt(a, b):
    return lax.dot_general(a, b, (((1,), (1,)), ((), ())), preferred_element_type=F32)


def dot_tn(a, b):
    return lax.dot_general(a, b, (((0,), (0,)), ((), ())), preferred_element_type=F32)


def partner(me, bit):
    return me + bit * (1 - 2 * ((me // bit) % 2))


def remote(src, dst, send_sem, recv_sem, target):
    return pltpu.make_async_remote_copy(
        src_ref=src,
        dst_ref=dst,
        send_sem=send_sem,
        recv_sem=recv_sem,
        device_id={"tensor": target},
        device_id_type=pl.DeviceIdType.MESH,
    )


def greet(targets):
    barrier = pltpu.get_barrier_semaphore()
    for t in targets:
        pl.semaphore_signal(
            barrier, inc=1, device_id={"tensor": t}, device_id_type=pl.DeviceIdType.MESH
        )
    pl.semaphore_wait(barrier, len(targets))


def attn_fwd_body(
    q_ref, k_ref, v_ref, sq_ref, sk_ref, o_ref, low_ref, lse_ref, own_ref, buf, send_sem, recv_sem, here_sem,
    *, block, heads, reach, size
):
    qb = pl.program_id(0)
    me = lax.axis_index("tensor")
    scale = 1.0 / math.sqrt(HEAD_DIM)
    cols_all = heads * HEAD_DIM

    @pl.when(qb == 0)
    def _():
        greet([lax.rem(me + t, size) for t in range(1, size)])

    seg_q = sq_ref[...]
    row = qb * block + lax.broadcasted_iota(jnp.int32, (block, block), 0)
    col0 = lax.broadcasted_iota(jnp.int32, (block, block), 1)
    qs = [q_ref[:, h * HEAD_DIM : (h + 1) * HEAD_DIM] for h in range(heads)]

    def step(kb, carry):
        rows = pl.ds(pl.multiple_of(kb * block, block), block)
        allowed = (seg_q == sk_ref[kb]) & (kb * block + col0 <= row)
        out = []
        for h in range(heads):
            m, l, acc = carry[h]
            cols = slice(h * HEAD_DIM, (h + 1) * HEAD_DIM)
            s = jnp.where(allowed, dot_nt(qs[h], k_ref[rows, cols]) * scale, NEG)
            m_new = jnp.maximum(m, jnp.max(s, axis=1, keepdims=True))
            p = jnp.exp(s - m_new)
            alpha = jnp.exp(m - m_new)
            l = alpha * l + jnp.sum(p, axis=1, keepdims=True)
            acc = alpha * acc + dot_nn(p.astype(BF), v_ref[rows, cols])
            out.append((m_new, l, acc))
        return tuple(out)

    init = tuple(
        (
            jnp.full((block, 1), NEG, F32),
            jnp.zeros((block, 1), F32),
            jnp.zeros((block, HEAD_DIM), F32),
        )
        for _ in range(heads)
    )
    final = lax.fori_loop(jnp.maximum(qb - reach, 0), qb + 1, step, init)
    for h in range(heads):
        m, l, acc = final[h]
        cols = slice(h * HEAD_DIM, (h + 1) * HEAD_DIM)
        out = acc / l
        o_ref[:, cols] = out
        low_ref[:, cols] = out.astype(BF)
        buf[qb, :, cols] = out.astype(BF)
        lse_ref[:, h : h + 1] = m + jnp.log(l)

    own = own_ref.shape[0]
    per = block // own

    def rows_of(dev):
        return buf.at[dev // per, pl.ds(pl.multiple_of((dev % per) * own, own), own)]

    def land(src):
        return own_ref.at[:, pl.ds(pl.multiple_of(src * cols_all, HEAD_DIM), cols_all)]

    def send(t):
        return remote(rows_of(t), land(me), send_sem.at[t], recv_sem.at[me], t)

    for j in range(per):
        dest = qb * per + j

        @pl.when(dest != me)
        def _():
            send(dest).start()

        @pl.when(dest == me)
        def _():
            pltpu.make_async_copy(rows_of(me), land(me), here_sem).start()

    @pl.when(qb == pl.num_programs(0) - 1)
    def _():
        pltpu.make_async_copy(rows_of(me), land(me), here_sem).wait()
        for t in range(1, size):
            other = lax.rem(me + t, size)
            send(other).wait_send()
            remote(
                rows_of(other), land(other), send_sem.at[other], recv_sem.at[other], other
            ).wait_recv()


def attn_fwd(q, k, v, seg_col, seg_rows, block, reach, size, cid):
    tokens, cols = q.shape
    heads = cols // HEAD_DIM
    nb = tokens // block
    full = lambda shape: pl.BlockSpec(shape, lambda i: (0,) * len(shape))
    rowed = lambda c: pl.BlockSpec((block, c), lambda i: (i, 0))
    return pl.pallas_call(
        functools.partial(attn_fwd_body, block=block, heads=heads, reach=reach, size=size),
        out_shape=(
            jax.ShapeDtypeStruct((tokens, cols), F32),
            jax.ShapeDtypeStruct((tokens, cols), BF),
            jax.ShapeDtypeStruct((tokens, heads), F32),
            jax.ShapeDtypeStruct((tokens // size, cols * size), BF),
        ),
        grid=(nb,),
        in_specs=[
            rowed(cols),
            full((tokens, cols)),
            full((tokens, cols)),
            rowed(1),
            full((nb, 1, block)),
        ],
        out_specs=[rowed(cols), rowed(cols), rowed(heads), pl.BlockSpec(memory_space=pl.ANY)],
        scratch_shapes=[
            pltpu.VMEM((nb, block, cols), BF),
            pltpu.SemaphoreType.DMA((size,)),
            pltpu.SemaphoreType.DMA((size,)),
            pltpu.SemaphoreType.DMA,
        ],
        compiler_params=pltpu.CompilerParams(
            vmem_limit_bytes=32 * MIB, collective_id=cid, has_side_effects=True
        ),
        cost_estimate=pl.CostEstimate(
            flops=10**8, bytes_accessed=4 * MIB, transcendentals=10**5
        ),
        name="attn_fwd",
    )(q, k, v, seg_col, seg_rows)


def attn_bwd_body(
    lo_ref, q_ref, k_ref, v_ref, do_ref, o_ref, lse_ref, sq_ref, sk_ref, dq_ref, dk_ref, dv_ref, *, block, heads
):
    qb = pl.program_id(0)
    scale = 1.0 / math.sqrt(HEAD_DIM)

    @pl.when(qb == 0)
    def _():
        dk_ref[...] = jnp.zeros_like(dk_ref)
        dv_ref[...] = jnp.zeros_like(dv_ref)

    seg_q = sq_ref[...]
    row = qb * block + lax.broadcasted_iota(jnp.int32, (block, block), 0)
    col0 = lax.broadcasted_iota(jnp.int32, (block, block), 1)
    hc = [slice(h * HEAD_DIM, (h + 1) * HEAD_DIM) for h in range(heads)]
    qs = [q_ref[:, c] for c in hc]
    dos = [do_ref[:, c] for c in hc]
    lse = [lse_ref[:, h : h + 1] for h in range(heads)]
    dsum = [
        jnp.sum(dos[h].astype(F32) * o_ref[:, hc[h]], axis=1, keepdims=True) for h in range(heads)
    ]

    def step(kb, carry):
        rows = pl.ds(pl.multiple_of(kb * block, block), block)
        allowed = (seg_q == sk_ref[kb]) & (kb * block + col0 <= row)
        out = []
        for h in range(heads):
            k_blk = k_ref[rows, hc[h]]
            s = jnp.where(allowed, dot_nt(qs[h], k_blk) * scale, NEG)
            p = jnp.exp(s - lse[h])
            dp = dot_nt(dos[h], v_ref[rows, hc[h]])
            ds = (p * (dp - dsum[h])).astype(BF)
            dv_ref[rows, hc[h]] += dot_tn(p.astype(BF), dos[h])
            dk_ref[rows, hc[h]] += dot_tn(ds, qs[h]) * scale
            out.append(carry[h] + dot_nn(ds, k_blk))
        return tuple(out)

    init = tuple(jnp.zeros((block, HEAD_DIM), F32) for _ in range(heads))
    final = lax.fori_loop(lo_ref[qb], qb + 1, step, init)
    for h in range(heads):
        dq_ref[:, hc[h]] = final[h] * scale


def attn_bwd(lo, q, k, v, do, o, lse, seg_col, seg_rows, block):
    tokens, cols = q.shape
    heads = cols // HEAD_DIM
    nb = tokens // block
    full = lambda shape: pl.BlockSpec(shape, lambda i, lo: (0,) * len(shape))
    rowed = lambda c: pl.BlockSpec((block, c), lambda i, lo: (i, 0))
    return pl.pallas_call(
        functools.partial(attn_bwd_body, block=block, heads=heads),
        out_shape=tuple(jax.ShapeDtypeStruct((tokens, cols), F32) for _ in range(3)),
        grid_spec=pltpu.PrefetchScalarGridSpec(
            num_scalar_prefetch=1,
            grid=(nb,),
            in_specs=[
                rowed(cols),
                full((tokens, cols)),
                full((tokens, cols)),
                rowed(cols),
                rowed(cols),
                rowed(heads),
                rowed(1),
                full((nb, 1, block)),
            ],
            out_specs=[rowed(cols), full((tokens, cols)), full((tokens, cols))],
        ),
        compiler_params=pltpu.CompilerParams(vmem_limit_bytes=40 * MIB),
        cost_estimate=pl.CostEstimate(
            flops=10**8, bytes_accessed=4 * MIB, transcendentals=10**5
        ),
        name="attn_bwd",
    )(lo, q, k, v, do, o, lse, seg_col, seg_rows)


def expert_body(*refs, first, rows_blk, parts):
    lead = first == 0
    if lead:
        x_hbm, g_hbm, mask_ref, wg_ref, wu_ref, wd_ref, router_ref = refs[:7]
        dgu_ref, ga_ref, wcat, dots_ref, grads_ref, xt_hbm, gates_ref, probs_ref = refs[7:15]
        x_v, xt_v, g_v, sem_x, sem_t, sem_g = refs[15:]
    else:
        x_hbm, g_hbm, gates_ref, wg_ref, wu_ref, wd_ref, xt_hbm = refs[:7]
        dgu_ref, ga_ref, wcat, dots_ref, grads_ref = refs[10:15]
        x_v, xt_v, g_v, sem_x, sem_t, sem_g = refs[15:]
    p = pl.program_id(0)
    tokens, width = x_v.shape
    nblk = tokens // rows_blk
    hid = wg_ref.shape[2]
    experts = gates_ref.shape[1]
    ds = width // parts

    if lead:
        t_copy = pltpu.make_async_copy(xt_v, xt_hbm, sem_t)
    else:
        t_copy = pltpu.make_async_copy(xt_hbm, xt_v, sem_t)

    def copies(i):
        r = pl.ds(i * rows_blk, rows_blk)
        return (
            pltpu.make_async_copy(x_hbm.at[r], x_v.at[r], sem_x.at[i]),
            pltpu.make_async_copy(g_hbm.at[r], g_v.at[r], sem_g.at[i]),
        )

    @pl.when(p == 0)
    def _():
        for i in range(nblk):
            for c in copies(i):
                c.start()
        if not lead:
            t_copy.start()
        dots_ref[...] = jnp.zeros_like(dots_ref)

    wcat[:, 0:hid] = wg_ref[0]
    wcat[:, hid : 2 * hid] = wg_ref[1]
    wcat[:, 2 * hid : 3 * hid] = wu_ref[0]
    wcat[:, 3 * hid : 4 * hid] = wu_ref[1]
    lane = lax.broadcasted_iota(jnp.int32, (rows_blk, experts), 1)
    e0 = 2 * (first + p)

    def block(i, _):
        start = pl.multiple_of(i * rows_blk, rows_blk)
        r = pl.ds(start, rows_blk)

        @pl.when(p == 0)
        def _():
            for c in copies(i):
                c.wait()

        if lead:
            xt_v[:, r] = x_v[r, :].T
            logits = dot_nn(x_v[r, :], router_ref[...])
            grown = jnp.exp(logits - jnp.max(logits, axis=1, keepdims=True))
            probs = grown / jnp.sum(grown, axis=1, keepdims=True)
            probs_ref[r, :] = probs
            gates_ref[r, :] = probs * mask_ref[r, :]
        gu = dot_nn(x_v[r, :], wcat[...])
        q = dot_nt(g_v[r, :], wd_ref[...])
        gate_rows = gates_ref[r, :]
        dots = dots_ref[r, :]
        for j in range(2):
            pre = gu[:, j * hid : (j + 1) * hid]
            up = gu[:, (2 + j) * hid : (3 + j) * hid]
            back = q[:, j * hid : (j + 1) * hid]
            here = lane == e0 + j
            gate = jnp.sum(jnp.where(here, gate_rows, 0.0), axis=1, keepdims=True)
            sig = jax.nn.sigmoid(pre)
            silu = pre * sig
            act = silu * up
            dot = jnp.sum(act * back, axis=1, keepdims=True)
            dots = dots + jnp.where(here, dot, 0.0)
            scaled = gate * back
            d_up = scaled * silu
            d_gate = scaled * up * (sig + silu * (1.0 - sig))
            dgu_ref[r, j * hid : (j + 1) * hid] = d_gate.astype(BF)
            dgu_ref[r, (2 + j) * hid : (3 + j) * hid] = d_up.astype(BF)
            ga_ref[r, j * hid : (j + 1) * hid] = (gate * act).astype(BF)
        dots_ref[r, :] = dots
        return 0

    lax.fori_loop(0, nblk, block, 0)

    @pl.when(p == 0)
    def _():
        if lead:
            t_copy.start()
        else:
            t_copy.wait()

    for s in range(parts):
        gd = dot_tn(ga_ref[...], g_v[:, s * ds : (s + 1) * ds]).astype(BF)
        gw = dot_nn(xt_v[s * ds : (s + 1) * ds, :], dgu_ref[...]).astype(BF)
        for j in range(2):
            grads_ref[s, 3 * j] = gw[:, j * hid : (j + 1) * hid]
            grads_ref[s, 3 * j + 1] = gw[:, (2 + j) * hid : (3 + j) * hid]
            for c in range(ds // hid):
                grads_ref[s, 3 * j + 2, c * hid : (c + 1) * hid, :] = gd[
                    j * hid : (j + 1) * hid, c * hid : (c + 1) * hid
                ]

    if lead:

        @pl.when(p == 0)
        def _():
            t_copy.wait()


def expert_chunk(x, g, gates, wg, wu, wd, router, carried, *, first, pairs, parts):
    tokens, width = x.shape
    experts, _, hid = wg.shape
    total = experts // 2
    rows_blk = 512
    nblk = tokens // rows_blk
    ds = width // parts
    lead = first == 0
    assert not lead or pairs == 1
    any_spec = pl.BlockSpec(memory_space=pl.ANY)
    colblk = lambda rows, c: pl.BlockSpec((rows, c), lambda p: (0, first + p))
    in_specs = [
        any_spec,
        any_spec,
        pl.BlockSpec((tokens, experts), lambda p: (0, 0)),
        pl.BlockSpec((2, width, hid), lambda p: (first + p, 0, 0)),
        pl.BlockSpec((2, width, hid), lambda p: (first + p, 0, 0)),
        pl.BlockSpec((2 * hid, width), lambda p: (first + p, 0)),
    ]
    out_shape = [
        jax.ShapeDtypeStruct((tokens, total * 4 * hid), BF),
        jax.ShapeDtypeStruct((tokens, total * 2 * hid), BF),
        jax.ShapeDtypeStruct((width, total * 4 * hid), BF),
        jax.ShapeDtypeStruct((tokens, experts), F32),
        jax.ShapeDtypeStruct((parts, pairs * 6, ds, hid), BF),
    ]
    out_specs = [
        colblk(tokens, 4 * hid),
        colblk(tokens, 2 * hid),
        colblk(width, 4 * hid),
        pl.BlockSpec((tokens, experts), lambda p: (0, 0)),
        pl.BlockSpec((parts, 6, ds, hid), lambda p: (0, p, 0, 0)),
    ]
    args = [x, g, gates, wg, wu, wd]
    alias = {}
    if lead:
        args.append(router)
        in_specs.append(pl.BlockSpec(router.shape, lambda p: (0, 0)))
        narrow = jax.ShapeDtypeStruct((tokens, experts), F32)
        out_shape += [jax.ShapeDtypeStruct((width, tokens), BF), narrow, narrow]
        out_specs += [any_spec] + [pl.BlockSpec((tokens, experts), lambda p: (0, 0))] * 2
    else:
        xt, dgu, ga, wcat = carried
        args += [xt, dgu, ga, wcat]
        in_specs += [any_spec] * 4
        alias = {7: 0, 8: 1, 9: 2}
    return pl.pallas_call(
        functools.partial(expert_body, first=first, rows_blk=rows_blk, parts=parts),
        out_shape=tuple(out_shape),
        grid=(pairs,),
        in_specs=in_specs,
        out_specs=out_specs,
        scratch_shapes=[
            pltpu.VMEM((tokens, width), BF),
            pltpu.VMEM((width, tokens), BF),
            pltpu.VMEM((tokens, width), BF),
            pltpu.SemaphoreType.DMA((nblk,)),
            pltpu.SemaphoreType.DMA,
            pltpu.SemaphoreType.DMA((nblk,)),
        ],
        input_output_aliases=alias,
        compiler_params=pltpu.CompilerParams(vmem_limit_bytes=61 * MIB),
        cost_estimate=pl.CostEstimate(
            flops=10**9, bytes_accessed=4 * MIB, transcendentals=10**5
        ),
        name="expert_chunk",
    )(*args)


GATHER_COPIES = 13


def gather_plan(x_hbm, land, me, own, send_sem, recv_sem):
    half = own // 2
    pc, px, py = (partner(me, b) for b in (1, 2, 4))
    diag = partner(px, 4)

    def piece(dev, a, n):
        return land.at[pl.ds(pl.multiple_of(dev * own + a, half), n)]

    plan = [
        (me, 0, half, px),
        (me, half, half, py),
        (me, half, half, px),
        (me, 0, half, py),
        (me, 0, own, pc),
        (px, 0, half, py),
        (py, half, half, px),
        (px, 0, half, pc),
        (py, half, half, pc),
        (px, half, half, pc),
        (py, 0, half, pc),
        (diag, 0, half, pc),
        (diag, half, half, pc),
    ]
    origin = {0: px, 1: py, 2: px, 3: py, 4: pc, 5: diag, 6: diag}

    def copy(k):
        dev, a, n, target = plan[k]
        src = x_hbm.at[pl.ds(a, n)] if k < 5 else piece(dev, a, n)
        return remote(src, piece(dev, a, n), send_sem.at[k], recv_sem.at[k], target)

    def arrived(k):
        dev, a, n, target = plan[k]
        src = origin[k] if k in origin else partner(dev, 1)
        return remote(piece(src, a, n), piece(src, a, n), send_sem.at[k], recv_sem.at[k], target)

    return copy, arrived, pc, px, py, diag


def project_body(
    x_hbm, wq_hbm, wk_hbm, wv_hbm, gain_ref, qg_ref, kg_ref, pos_ref,
    normed_hbm, q_ref, k_ref, v_ref, qu_ref, ku_ref, rs_ref, cos_ref, sin_ref,
    x_v, n_v, w_v, sums, sums_all, send_sem, recv_sem, ss_send, ss_recv, w_sem, x_sem, n_sem, *, size
):
    me = lax.axis_index("tensor")
    own = x_hbm.shape[0]
    width = x_hbm.shape[1]
    cols = q_ref.shape[1]
    heads = cols // HEAD_DIM
    half_dim = HEAD_DIM // 2
    weights = [
        pltpu.make_async_copy(w, w_v.at[:, pl.ds(i * cols, cols)], w_sem.at[i])
        for i, w in enumerate((wq_hbm, wk_hbm, wv_hbm))
    ]
    mine = pl.ds(pl.multiple_of(me * own, own), own)
    here = pltpu.make_async_copy(x_hbm, x_v.at[mine], x_sem)
    here.start()
    for w in weights:
        w.start()
    greet([lax.rem(me + t, size) for t in range(1, size)])
    copy, arrived, pc, px, py, diag = gather_plan(x_hbm, x_v, me, own, send_sem, recv_sem)
    for k in range(5):
        copy(k).start()

    lane = lax.broadcasted_iota(jnp.int32, (own, HEAD_DIM), 1)
    power = (lane % half_dim).astype(F32) * (-2.0 * math.log(10000.0) / HEAD_DIM)
    frequency = jnp.exp(power)

    def table(i, _):
        r = pl.ds(pl.multiple_of(i * own, own), own)
        angle = pos_ref[r, :] * frequency
        cos_ref[r, :] = jnp.cos(angle)
        sine = jnp.sin(angle)
        sin_ref[r, :] = jnp.where(lane < half_dim, -sine, sine)
        return 0

    lax.fori_loop(0, size, table, 0)

    def stored(dev):
        r = pl.ds(pl.multiple_of(dev * own, own), own)
        return pltpu.make_async_copy(n_v.at[r], normed_hbm.at[r], n_sem.at[dev])

    def process(dev):
        r = pl.ds(pl.multiple_of(dev * own, own), own)
        wide = x_v[r, :].astype(F32)
        scale = lax.rsqrt(jnp.mean(wide * wide, axis=1, keepdims=True) + EPS)
        normed = (wide * scale * gain_ref[...]).astype(BF)
        n_v[r, :] = normed
        stored(dev).start()
        res = dot_nn(normed, w_v[...])
        q = res[:, :cols]
        k = res[:, cols : 2 * cols]
        qu_ref[r, :] = q
        ku_ref[r, :] = k
        v_ref[r, :] = res[:, 2 * cols :].astype(BF)
        pair = jnp.where(
            lane == 0,
            jnp.sum(q * q, axis=1, keepdims=True),
            jnp.sum(k * k, axis=1, keepdims=True),
        )
        sums[dev] = pair.T[0:2, :]

    here.wait()
    for w in weights:
        w.wait()
    process(me)
    arrived(4).wait_recv()
    process(pc)
    arrived(0).wait_recv()
    copy(5).start()
    copy(7).start()
    arrived(1).wait_recv()
    copy(6).start()
    copy(8).start()
    arrived(2).wait_recv()
    copy(9).start()
    arrived(3).wait_recv()
    copy(10).start()
    process(px)
    process(py)
    arrived(7).wait_recv()
    arrived(9).wait_recv()
    process(partner(px, 1))
    arrived(8).wait_recv()
    arrived(10).wait_recv()
    process(partner(py, 1))
    arrived(5).wait_recv()
    copy(11).start()
    arrived(6).wait_recv()
    copy(12).start()
    process(diag)
    arrived(11).wait_recv()
    arrived(12).wait_recv()
    process(partner(diag, 1))

    def exchange(t, src):
        other = lax.rem(me + t, size)
        slot = me if src is None else other
        return remote(sums, sums_all.at[slot], ss_send.at[other], ss_recv.at[slot], other)

    for t in range(1, size):
        exchange(t, None).start()
    sums_all[me] = sums[...]
    for t in range(1, size):
        exchange(t, 1).wait_recv()
    total = sums_all[0]
    for d in range(1, size):
        total = total + sums_all[d]
    rows_iota = lax.broadcasted_iota(jnp.int32, (HEAD_DIM, own), 0)
    for d in range(size):
        r = slice(d * own, (d + 1) * own)
        tot = total[d]
        both = jnp.where(rows_iota == 0, tot[0:1, :], tot[1:2, :])
        rs = lax.rsqrt(both / width + EPS).T
        rs_ref[r, :] = rs[:, 0:2]
        cos, sin = cos_ref[r, :], sin_ref[r, :]
        for j, (unit_ref, gain, dst) in enumerate(((qu_ref, qg_ref, q_ref), (ku_ref, kg_ref, k_ref))):
            unit = unit_ref[r, :] * rs[:, j : j + 1]
            unit_ref[r, :] = unit
            wide = unit * gain[...]
            for h in range(heads):
                c = slice(h * HEAD_DIM, (h + 1) * HEAD_DIM)
                w = wide[:, c]
                dst[r, c] = (w * cos + pltpu.roll(w, half_dim, 1) * sin).astype(BF)
    for t in range(1, size):
        exchange(t, None).wait_send()
    for k in range(GATHER_COPIES):
        copy(k).wait_send()
    for d in range(size):
        stored(d).wait()


def project(x, wq, wk, wv, gain, qg, kg, pos, size, cid):
    own, width = x.shape
    cols = wq.shape[1]
    tokens = own * size
    any_spec = pl.BlockSpec(memory_space=pl.ANY)
    vm = pl.BlockSpec(memory_space=pltpu.VMEM)
    return pl.pallas_call(
        functools.partial(project_body, size=size),
        out_shape=(
            jax.ShapeDtypeStruct((tokens, width), BF),
            jax.ShapeDtypeStruct((tokens, cols), BF),
            jax.ShapeDtypeStruct((tokens, cols), BF),
            jax.ShapeDtypeStruct((tokens, cols), BF),
            jax.ShapeDtypeStruct((tokens, cols), F32),
            jax.ShapeDtypeStruct((tokens, cols), F32),
            jax.ShapeDtypeStruct((tokens, 2), F32),
            jax.ShapeDtypeStruct((tokens, HEAD_DIM), F32),
            jax.ShapeDtypeStruct((tokens, HEAD_DIM), F32),
        ),
        in_specs=[any_spec] * 4 + [vm] * 4,
        out_specs=[any_spec] + [vm] * 8,
        scratch_shapes=[
            pltpu.VMEM((tokens, width), BF),
            pltpu.VMEM((tokens, width), BF),
            pltpu.VMEM((width, 3 * cols), BF),
            pltpu.VMEM((size, 2, own), F32),
            pltpu.VMEM((size, size, 2, own), F32),
            pltpu.SemaphoreType.DMA((GATHER_COPIES,)),
            pltpu.SemaphoreType.DMA((GATHER_COPIES,)),
            pltpu.SemaphoreType.DMA((size,)),
            pltpu.SemaphoreType.DMA((size,)),
            pltpu.SemaphoreType.DMA((3,)),
            pltpu.SemaphoreType.DMA,
            pltpu.SemaphoreType.DMA((size,)),
        ],
        compiler_params=pltpu.CompilerParams(
            vmem_limit_bytes=56 * MIB, collective_id=cid, has_side_effects=True
        ),
        cost_estimate=pl.CostEstimate(flops=10**8, bytes_accessed=4 * MIB, transcendentals=0),
        name="project",
    )(x, wq, wk, wv, gain[None, :], qg[None, :], kg[None, :], pos)


def matmul_scatter_body(
    l_hbm, r_hbm, out_ref, l_v, r_v, part, got1, got2, got3, sem_l, sem_r, send_sem, recv_sem,
    *, size, slices, nt
):
    me = lax.axis_index("tensor")
    tokens = l_v.shape[0]
    own = tokens // size
    sn = out_ref.shape[1] // slices
    mine = [(me // b) % 2 for b in (1, 2, 4)]
    group = 2

    def l_copy(i):
        r = pl.ds(i * own * group, own * group)
        return pltpu.make_async_copy(l_hbm.at[r], l_v.at[r], sem_l.at[i])

    def r_copy(s):
        c = pl.ds(s * sn, sn)
        if nt:
            return pltpu.make_async_copy(r_hbm.at[c], r_v.at[c], sem_r.at[s])
        return pltpu.make_async_copy(r_hbm.at[:, c], r_v.at[:, c], sem_r.at[s])

    r_copy(0).start()
    for i in range(size // group):
        l_copy(i).start()
    for s in range(1, slices):
        r_copy(s).start()
    greet([partner(me, b) for b in (1, 2, 4)])

    def hop(s, stage):
        a, b = (1, 2) if s % 2 == 0 else (2, 1)
        if stage == 0:
            src, dst, bit = part.at[s, 1 - mine[0]], got1.at[s], 1
        elif stage == 1:
            src, dst, bit = part.at[s, mine[0], pl.ds(2 * (1 - mine[a]), 2)], got2.at[s], 1 << a
        else:
            src, dst, bit = part.at[s, mine[0], 2 * mine[a] + 1 - mine[b]], got3.at[s], 1 << b
        return remote(src, dst, send_sem.at[stage, s], recv_sem.at[stage, s], partner(me, bit))

    def compute(s):
        r_copy(s).wait()

        def rows(i, _):
            if s == 0:
                l_copy(i).wait()
            r = pl.ds(pl.multiple_of(i * own * group, own * group), own * group)
            if nt:
                res = dot_nt(l_v[r, :], r_v[s * sn : (s + 1) * sn, :])
            else:
                res = dot_nn(l_v[r, :], r_v[:, s * sn : (s + 1) * sn])
            res = res.astype(BF)
            x, y = i % 2, i // 2
            pos = 2 * x + y if s % 2 == 0 else 2 * y + x
            for c in range(2):
                part[s, c, pos] = res[c * own : (c + 1) * own]
            return 0

        lax.fori_loop(0, size // group, rows, 0)
        hop(s, 0).start()

    def first(s):
        hop(s, 0).wait_recv()
        part[s, mine[0]] = (part[s, mine[0]].astype(F32) + got1[s].astype(F32)).astype(BF)
        hop(s, 1).start()

    def second(s):
        a = 1 if s % 2 == 0 else 2
        hop(s, 1).wait_recv()
        ix = pl.ds(2 * mine[a], 2)
        part[s, mine[0], ix] = (part[s, mine[0], ix].astype(F32) + got2[s].astype(F32)).astype(BF)
        hop(s, 2).start()

    def third(s):
        a, b = (1, 2) if s % 2 == 0 else (2, 1)
        hop(s, 2).wait_recv()
        out_ref[:, s * sn : (s + 1) * sn] = part[s, mine[0], 2 * mine[a] + mine[b]].astype(
            F32
        ) + got3[s].astype(F32)

    for t in range(slices + 5):
        if t < slices:
            compute(t)
        if 0 <= t - 1 < slices:
            first(t - 1)
        if 0 <= t - 3 < slices:
            second(t - 3)
        if 0 <= t - 5 < slices:
            third(t - 5)
    for s in range(slices):
        for stage in range(3):
            hop(s, stage).wait_send()


def matmul_scatter(left, right, size, cid, nt, name):
    tokens, depth = left.shape
    width = right.shape[0] if nt else right.shape[1]
    own = tokens // size
    if size != 8:
        part = (dot_nt if nt else dot_nn)(left, right).astype(BF)
        return lax.psum_scatter(part, "tensor", scatter_dimension=0, tiled=True).astype(F32)
    slices = 8
    sn = width // slices
    any_spec = pl.BlockSpec(memory_space=pl.ANY)
    return pl.pallas_call(
        functools.partial(matmul_scatter_body, size=size, slices=slices, nt=nt),
        out_shape=jax.ShapeDtypeStruct((own, width), F32),
        in_specs=[any_spec, any_spec],
        out_specs=pl.BlockSpec(memory_space=pltpu.VMEM),
        scratch_shapes=[
            pltpu.VMEM(left.shape, BF),
            pltpu.VMEM(right.shape, BF),
            pltpu.VMEM((slices, 2, size // 2, own, sn), BF),
            pltpu.VMEM((slices, size // 2, own, sn), BF),
            pltpu.VMEM((slices, size // 4, own, sn), BF),
            pltpu.VMEM((slices, own, sn), BF),
            pltpu.SemaphoreType.DMA((size // 2,)),
            pltpu.SemaphoreType.DMA((slices,)),
            pltpu.SemaphoreType.DMA((3, slices)),
            pltpu.SemaphoreType.DMA((3, slices)),
        ],
        compiler_params=pltpu.CompilerParams(
            vmem_limit_bytes=60 * MIB, collective_id=cid, has_side_effects=True
        ),
        cost_estimate=pl.CostEstimate(
            flops=10**9, bytes_accessed=4 * MIB, transcendentals=0
        ),
        name=name,
    )(left, right)


def gather_body(x_ref, out_ref, send_sem, recv_sem, here_sem):
    me = lax.axis_index("tensor")
    own = x_ref.shape[0]
    greet([partner(me, b) for b in (1, 2, 4)])
    mine = pl.ds(pl.multiple_of(me * own, own), own)
    here = pltpu.make_async_copy(x_ref, out_ref.at[mine], here_sem)
    here.start()
    copy, arrived = gather_plan(x_ref, out_ref, me, own, send_sem, recv_sem)[:2]
    for k in range(5):
        copy(k).start()
    for k, following in ((0, (5, 7)), (1, (6, 8)), (2, (9,)), (3, (10,)), (5, (11,)), (6, (12,))):
        arrived(k).wait_recv()
        for f in following:
            copy(f).start()
    for k in (4, 7, 8, 9, 10, 11, 12):
        arrived(k).wait_recv()
    for k in range(GATHER_COPIES):
        copy(k).wait_send()
    here.wait()


def gather_all(value, size, cid, name):
    own, cols = value.shape
    if size != 8:
        return lax.all_gather(value, "tensor", axis=0, tiled=True)
    any_spec = pl.BlockSpec(memory_space=pl.ANY)
    return pl.pallas_call(
        gather_body,
        out_shape=jax.ShapeDtypeStruct((own * size, cols), value.dtype),
        in_specs=[any_spec],
        out_specs=any_spec,
        scratch_shapes=[
            pltpu.SemaphoreType.DMA((GATHER_COPIES,)),
            pltpu.SemaphoreType.DMA((GATHER_COPIES,)),
            pltpu.SemaphoreType.DMA,
        ],
        compiler_params=pltpu.CompilerParams(collective_id=cid, has_side_effects=True),
        cost_estimate=pl.CostEstimate(flops=0, bytes_accessed=4 * MIB, transcendentals=0),
        name=name,
    )(value)


def swap(value, axis, size, bit):
    return lax.ppermute(value, axis, [(i, i ^ bit) for i in range(size)])


def sum_all(value, axis, size):
    bit = 1
    while bit < size:
        value = value + swap(value, axis, size, bit)
        bit *= 2
    return value


def bits_of(size):
    return [1 << b for b in range(size.bit_length() - 1)]


def half_swap(values):
    pieces = []
    half = HEAD_DIM // 2
    for h in range(values.shape[1] // HEAD_DIM):
        base = h * HEAD_DIM
        pieces += [values[:, base + half : base + HEAD_DIM], values[:, base : base + half]]
    return jnp.concatenate(pieces, axis=1)


def per_device(
    block_input, segments, routes, w_query, w_key, w_value, w_output, attn_gain, query_gain, key_gain,
    moe_gain, router, w_gate, w_up, w_down, cotangent, *, n_dp, n_tensor
):
    own_rows, model_width = block_input.shape
    local_cols = w_query.shape[1]
    local_heads = local_cols // HEAD_DIM
    token_count = segments.shape[0] * segments.shape[1]
    experts = router.shape[1]
    top_count = routes.shape[1]
    hid = w_gate.shape[2]
    capacity = 5 * token_count * top_count // (4 * experts)
    me = lax.axis_index("tensor")
    rank_start = me * own_rows
    col_start = me * local_cols
    block = 256

    seg = segments.reshape(token_count)
    values16 = jnp.arange(16, dtype=jnp.int32)
    below = jnp.sum((seg[None, :] < values16[:, None]).astype(jnp.int32), axis=1)
    doc_start = jnp.sum(
        jnp.where(seg[:, None] == values16[None, :], below[None, :], 0), axis=1
    )
    positions = jnp.arange(token_count, dtype=jnp.int32) - doc_start
    lo_block = doc_start[::block] // block
    seg_col = seg[:, None]
    seg_rows = seg.reshape(token_count // block, 1, block)

    expert_ids = jnp.arange(experts, dtype=jnp.int32)
    routed = jnp.sum(
        (routes[:, :, None] == expert_ids[None, None, :]).astype(F32), axis=1
    )
    tri = (
        jnp.arange(block, dtype=jnp.int32)[:, None] > jnp.arange(block, dtype=jnp.int32)[None, :]
    ).astype(BF)
    nb = token_count // block
    routed_b = routed.reshape(nb, block, experts)
    within = jnp.einsum("ij,bje->bie", tri, routed_b.astype(BF), preferred_element_type=F32)
    sums = jnp.sum(routed_b, axis=1)
    before = jnp.sum(
        jnp.where(
            (jnp.arange(nb)[:, None] > jnp.arange(nb)[None, :])[:, :, None], sums[None, :, :], 0.0
        ),
        axis=1,
    )
    place = within + before[:, None, :]
    mask = (routed_b * (place < capacity).astype(F32)).reshape(token_count, experts)

    w_qkv = jnp.concatenate([w_query, w_key, w_value], axis=1)
    full_wo = lax.all_gather(w_output, "tensor", axis=0, tiled=True)
    pos_col = positions.astype(F32)[:, None]
    if n_tensor == 8:
        normed, queries, keys_rot, value_low, query_unit, key_unit, scales, cos_one, sin_one = project(
            block_input, w_query, w_key, w_value, attn_gain, query_gain, key_gain, pos_col, n_tensor, 6
        )
        query_rs, key_rs = scales[:, 0:1], scales[:, 1:2]
        cos_all = jnp.concatenate([cos_one] * local_heads, axis=1)
        sin_all = jnp.concatenate([sin_one] * local_heads, axis=1)
    else:
        half = HEAD_DIM // 2
        frequency = jnp.exp(
            jnp.arange(half, dtype=F32) * (-2.0 * math.log(10000.0) / HEAD_DIM)
        )
        angles = pos_col * frequency[None, :]
        cosine, sine = jnp.cos(angles), jnp.sin(angles)
        cos_all = jnp.concatenate([cosine] * (2 * local_heads), axis=1)
        sin_all = jnp.concatenate([-sine, sine] * local_heads, axis=1)
        input_wide = lax.all_gather(block_input, "tensor", axis=0, tiled=True).astype(F32)
        normed = (input_wide * rms_scale(input_wide) * attn_gain).astype(BF)
        qkv = dot_nn(normed, w_qkv)
        query_raw = qkv[:, :local_cols]
        key_raw = qkv[:, local_cols : 2 * local_cols]
        value_low = qkv[:, 2 * local_cols :].astype(BF)
        squares = jnp.stack(
            [jnp.sum(query_raw * query_raw, axis=1), jnp.sum(key_raw * key_raw, axis=1)]
        )
        squares = sum_all(squares, "tensor", n_tensor)
        scales = lax.rsqrt(squares / model_width + EPS)
        query_rs, key_rs = scales[0][:, None], scales[1][:, None]
        query_unit = query_raw * query_rs
        key_unit = key_raw * key_rs
        q_n = query_unit * query_gain
        k_n = key_unit * key_gain
        queries = (q_n * cos_all + half_swap(q_n) * sin_all).astype(BF)
        keys_rot = (k_n * cos_all + half_swap(k_n) * sin_all).astype(BF)
    queries, cot_in = lax.optimization_barrier((queries, cotangent))
    full_cot = lax.all_gather(cot_in, "tensor", axis=0, tiled=True)
    reach = min(1024 // block, token_count // block)
    attended, attn_low, lse, own_attn = attn_fwd(
        queries, keys_rot, value_low, seg_col, seg_rows, block, reach, n_tensor, 0
    )


    input_own = block_input.astype(F32)
    residual = input_own + dot_nn(own_attn, full_wo)
    scale_two = rms_scale(residual)
    own_moe_in = (residual * scale_two * moe_gain).astype(BF)
    moe_in = gather_all(own_moe_in, n_tensor, 1, "gather_moe")

    wd_flat = w_down.reshape(experts * hid, model_width)
    pairs_total = experts // 2
    chunks = (1, 3, 4)
    dots = None
    reduced = []
    carried = None
    first = 0
    for count in chunks:
        res = expert_chunk(
            moe_in, full_cot, mask if first == 0 else gates, w_gate, w_up, wd_flat, router, carried,
            first=first, pairs=count, parts=n_dp,
        )
        dgu, ga, wcat, dot_c, grads = res[:5]
        if first == 0:
            xt, gates, router_probs = res[5:]
        if len(reduced) == 2:
            reduced[0], dgu = lax.optimization_barrier((reduced[0], dgu))
        carried = (xt, dgu, ga, wcat)
        dots = dot_c if dots is None else dots + dot_c
        reduced.append(lax.psum_scatter(grads, "dp", scatter_dimension=0, tiled=False))
        first += count
    moe_back = matmul_scatter(dgu, wcat, n_tensor, 2, True, "moe_back")

    own_dots = jnp.sum(
        lax.all_to_all(dots.reshape(n_tensor, own_rows, experts), "tensor", 0, 0), axis=0
    )
    own_mask = lax.dynamic_slice_in_dim(mask, rank_start, own_rows, 0)
    own_probs = lax.dynamic_slice_in_dim(router_probs, rank_start, own_rows, 0)
    prob_grads = own_dots * own_mask
    own_logit = (
        own_probs * (prob_grads - jnp.sum(own_probs * prob_grads, axis=1, keepdims=True))
    ).astype(BF)
    router_grad = dot_tn(own_logit, own_moe_in)
    moe_grad = moe_back + dot_nt(own_logit, router)

    unit_two = residual * scale_two
    moe_gain_grad = jnp.sum(moe_grad * unit_two, axis=0)
    scaled_two = moe_grad * moe_gain
    residual_grad = cotangent.astype(F32) + scale_two * (
        scaled_two - unit_two * jnp.mean(scaled_two * unit_two, axis=1, keepdims=True)
    )
    residual_low = gather_all(residual_grad.astype(BF), n_tensor, 3, "gather_residual")
    output_grad = dot_tn(residual_low, attn_low).astype(BF)
    heads_grad = dot_nt(residual_low, w_output).astype(BF)

    dq_rot, dk_rot, dv = attn_bwd(
        lo_block, queries, keys_rot, value_low, heads_grad, attended, lse, seg_col, seg_rows, block
    )
    reduced[1], dq_rot = lax.optimization_barrier((reduced[1], dq_rot))
    query_norm_grad = dq_rot * cos_all - half_swap(dq_rot) * sin_all
    key_norm_grad = dk_rot * cos_all - half_swap(dk_rot) * sin_all
    query_gain_grad = jnp.sum(query_norm_grad * query_unit, axis=0)
    key_gain_grad = jnp.sum(key_norm_grad * key_unit, axis=0)
    query_scaled = query_norm_grad * query_gain
    key_scaled = key_norm_grad * key_gain
    inner = jnp.stack(
        [jnp.sum(query_scaled * query_unit, axis=1), jnp.sum(key_scaled * key_unit, axis=1)]
    )
    inner = sum_all(inner, "tensor", n_tensor) / model_width
    query_grad_low = (query_rs * (query_scaled - query_unit * inner[0][:, None])).astype(BF)
    key_grad_low = (key_rs * (key_scaled - key_unit * inner[1][:, None])).astype(BF)
    qkv_grad = jnp.concatenate([query_grad_low, key_grad_low, dv.astype(BF)], axis=1)
    qkv_w_grad = dot_tn(normed, qkv_grad).astype(BF)
    normed_grad = matmul_scatter(qkv_grad, w_qkv, n_tensor, 4, True, "normed_back")
    moe_out = matmul_scatter(ga, wd_flat, n_tensor, 5, False, "moe_out")
    block_output = (residual + moe_out).astype(BF)
    scale_own = rms_scale(input_own)
    unit_one = input_own * scale_own
    attn_gain_grad = jnp.sum(normed_grad * unit_one, axis=0)
    scaled_one = normed_grad * attn_gain
    grad_input = residual_grad + scale_own * (
        scaled_one - unit_one * jnp.mean(scaled_one * unit_one, axis=1, keepdims=True)
    )

    proj_grad = jnp.concatenate([qkv_w_grad, output_grad], axis=1)
    reduced[2], proj_grad, block_output, grad_input = lax.optimization_barrier(
        (reduced[2], proj_grad, block_output, grad_input)
    )
    qkv_red = lax.psum_scatter(proj_grad, "dp", scatter_dimension=0, tiled=True).astype(F32)
    wo_red = qkv_red[:, 3 * local_cols :].T
    early = jnp.concatenate([router_grad, moe_gain_grad[None, :]], axis=0)
    early = sum_all(sum_all(early, "tensor", n_tensor), "dp", n_dp)
    gains = jnp.stack(
        [
            attn_gain_grad,
            lax.dynamic_update_slice_in_dim(
                jnp.zeros((model_width,), F32), query_gain_grad, col_start, 0
            ),
            lax.dynamic_update_slice_in_dim(
                jnp.zeros((model_width,), F32), key_gain_grad, col_start, 0
            ),
        ]
    )
    gains = sum_all(sum_all(gains, "tensor", n_tensor), "dp", n_dp)

    ds = model_width // n_dp
    gate_out, up_out, down_out = [], [], []
    for r, count in zip(reduced, chunks):
        r = r.reshape(2 * count, 3, ds, hid)
        gate_out.append(r[:, 0])
        up_out.append(r[:, 1])
        down = r[:, 2].reshape(2 * count, ds // hid, hid, hid)
        down_out.append(down.transpose(0, 2, 1, 3).reshape(2 * count, hid, ds))
    grad_gate = jnp.concatenate(gate_out, axis=0).astype(F32)
    grad_up = jnp.concatenate(up_out, axis=0).astype(F32)
    grad_down = jnp.concatenate(down_out, axis=0).astype(F32)
    return (
        block_output,
        grad_input,
        qkv_red[:, :local_cols],
        qkv_red[:, local_cols : 2 * local_cols],
        qkv_red[:, 2 * local_cols : 3 * local_cols],
        wo_red,
        gains[0],
        gains[1],
        gains[2],
        early[experts],
        early[:experts].T,
        grad_gate,
        grad_up,
        grad_down,
    )


def solution(mesh):
    rows = P(("dp", "tensor"), None)
    cols = P(None, "tensor")
    wide = P(None, None, "tensor")
    placed = (
        rows, P("dp", None), P("dp", None), cols, cols, cols, P("tensor", None), P(), P("tensor"), P("tensor"),
        P(), P(), wide, wide, P(None, "tensor", None), rows,
    )
    outs = (
        rows, rows, P("dp", "tensor"), P("dp", "tensor"), P("dp", "tensor"), P("tensor", "dp"), P(), P(), P(), P(),
        P(), P(None, "dp", "tensor"), P(None, "dp", "tensor"), P(None, "tensor", "dp"),
    )
    return jax.shard_map(
        functools.partial(
            per_device, n_dp=mesh.shape["dp"], n_tensor=mesh.shape["tensor"]
        ),
        mesh=mesh,
        in_specs=placed,
        out_specs=outs,
        check_vma=False,
    )
```

```python
import functools
import math

import jax
import jax.numpy as jnp
from jax import lax
from jax.experimental import pallas as pl
from jax.experimental.pallas import tpu as pltpu
from jax.sharding import PartitionSpec as P

HEAD_DIM = 128
EPS = 1e-05
NEG = -1e30
MIB = 1 << 20
BF = jnp.bfloat16
F32 = jnp.float32


def rms_scale(values):
    return lax.rsqrt(jnp.mean(values * values, axis=-1, keepdims=True) + EPS)


def dot_nn(a, b):
    return lax.dot_general(a, b, (((1,), (0,)), ((), ())), preferred_element_type=F32)


def dot_nt(a, b):
    return lax.dot_general(a, b, (((1,), (1,)), ((), ())), preferred_element_type=F32)


def dot_tn(a, b):
    return lax.dot_general(a, b, (((0,), (0,)), ((), ())), preferred_element_type=F32)


def partner(me, bit):
    return me + bit * (1 - 2 * ((me // bit) % 2))


def remote(src, dst, send_sem, recv_sem, target):
    return pltpu.make_async_remote_copy(
        src_ref=src,
        dst_ref=dst,
        send_sem=send_sem,
        recv_sem=recv_sem,
        device_id={"tensor": target},
        device_id_type=pl.DeviceIdType.MESH,
    )


def greet(targets):
    barrier = pltpu.get_barrier_semaphore()
    for t in targets:
        pl.semaphore_signal(
            barrier, inc=1, device_id={"tensor": t}, device_id_type=pl.DeviceIdType.MESH
        )
    pl.semaphore_wait(barrier, len(targets))


def attn_fwd_body(
    q_ref, k_ref, v_ref, sq_ref, sk_ref, o_ref, low_ref, lse_ref, own_ref, buf, send_sem, recv_sem, here_sem,
    *, block, heads, reach, size
):
    qb = pl.program_id(0)
    me = lax.axis_index("tensor")
    scale = 1.0 / math.sqrt(HEAD_DIM)
    cols_all = heads * HEAD_DIM

    @pl.when(qb == 0)
    def _():
        greet([lax.rem(me + t, size) for t in range(1, size)])

    seg_q = sq_ref[...]
    row = qb * block + lax.broadcasted_iota(jnp.int32, (block, block), 0)
    col0 = lax.broadcasted_iota(jnp.int32, (block, block), 1)
    qs = [q_ref[:, h * HEAD_DIM : (h + 1) * HEAD_DIM] for h in range(heads)]

    def step(kb, carry):
        rows = pl.ds(pl.multiple_of(kb * block, block), block)
        allowed = (seg_q == sk_ref[kb]) & (kb * block + col0 <= row)
        out = []
        for h in range(heads):
            m, l, acc = carry[h]
            cols = slice(h * HEAD_DIM, (h + 1) * HEAD_DIM)
            s = jnp.where(allowed, dot_nt(qs[h], k_ref[rows, cols]) * scale, NEG)
            m_new = jnp.maximum(m, jnp.max(s, axis=1, keepdims=True))
            p = jnp.exp(s - m_new)
            alpha = jnp.exp(m - m_new)
            l = alpha * l + jnp.sum(p, axis=1, keepdims=True)
            acc = alpha * acc + dot_nn(p.astype(BF), v_ref[rows, cols])
            out.append((m_new, l, acc))
        return tuple(out)

    init = tuple(
        (
            jnp.full((block, 1), NEG, F32),
            jnp.zeros((block, 1), F32),
            jnp.zeros((block, HEAD_DIM), F32),
        )
        for _ in range(heads)
    )
    final = lax.fori_loop(jnp.maximum(qb - reach, 0), qb + 1, step, init)
    for h in range(heads):
        m, l, acc = final[h]
        cols = slice(h * HEAD_DIM, (h + 1) * HEAD_DIM)
        out = acc / l
        o_ref[:, cols] = out
        low_ref[:, cols] = out.astype(BF)
        buf[qb, :, cols] = out.astype(BF)
        lse_ref[:, h : h + 1] = m + jnp.log(l)

    own = own_ref.shape[0]
    per = block // own

    def rows_of(dev):
        return buf.at[dev // per, pl.ds(pl.multiple_of((dev % per) * own, own), own)]

    def land(src):
        return own_ref.at[:, pl.ds(pl.multiple_of(src * cols_all, HEAD_DIM), cols_all)]

    def send(t):
        return remote(rows_of(t), land(me), send_sem.at[t], recv_sem.at[me], t)

    for j in range(per):
        dest = qb * per + j

        @pl.when(dest != me)
        def _():
            send(dest).start()

        @pl.when(dest == me)
        def _():
            pltpu.make_async_copy(rows_of(me), land(me), here_sem).start()

    @pl.when(qb == pl.num_programs(0) - 1)
    def _():
        pltpu.make_async_copy(rows_of(me), land(me), here_sem).wait()
        for t in range(1, size):
            other = lax.rem(me + t, size)
            send(other).wait_send()
            remote(
                rows_of(other), land(other), send_sem.at[other], recv_sem.at[other], other
            ).wait_recv()


def attn_fwd(q, k, v, seg_col, seg_rows, block, reach, size, cid):
    tokens, cols = q.shape
    heads = cols // HEAD_DIM
    nb = tokens // block
    full = lambda shape: pl.BlockSpec(shape, lambda i: (0,) * len(shape))
    rowed = lambda c: pl.BlockSpec((block, c), lambda i: (i, 0))
    return pl.pallas_call(
        functools.partial(attn_fwd_body, block=block, heads=heads, reach=reach, size=size),
        out_shape=(
            jax.ShapeDtypeStruct((tokens, cols), F32),
            jax.ShapeDtypeStruct((tokens, cols), BF),
            jax.ShapeDtypeStruct((tokens, heads), F32),
            jax.ShapeDtypeStruct((tokens // size, cols * size), BF),
        ),
        grid=(nb,),
        in_specs=[
            rowed(cols),
            full((tokens, cols)),
            full((tokens, cols)),
            rowed(1),
            full((nb, 1, block)),
        ],
        out_specs=[rowed(cols), rowed(cols), rowed(heads), pl.BlockSpec(memory_space=pl.ANY)],
        scratch_shapes=[
            pltpu.VMEM((nb, block, cols), BF),
            pltpu.SemaphoreType.DMA((size,)),
            pltpu.SemaphoreType.DMA((size,)),
            pltpu.SemaphoreType.DMA,
        ],
        compiler_params=pltpu.CompilerParams(
            vmem_limit_bytes=32 * MIB, collective_id=cid, has_side_effects=True
        ),
        cost_estimate=pl.CostEstimate(
            flops=10**8, bytes_accessed=4 * MIB, transcendentals=10**5
        ),
        name="attn_fwd",
    )(q, k, v, seg_col, seg_rows)


def attn_bwd_body(
    lo_ref, q_ref, k_ref, v_ref, do_ref, o_ref, lse_ref, sq_ref, sk_ref, dq_ref, dk_ref, dv_ref, *, block, heads
):
    qb = pl.program_id(0)
    scale = 1.0 / math.sqrt(HEAD_DIM)

    @pl.when(qb == 0)
    def _():
        dk_ref[...] = jnp.zeros_like(dk_ref)
        dv_ref[...] = jnp.zeros_like(dv_ref)

    seg_q = sq_ref[...]
    row = qb * block + lax.broadcasted_iota(jnp.int32, (block, block), 0)
    col0 = lax.broadcasted_iota(jnp.int32, (block, block), 1)
    hc = [slice(h * HEAD_DIM, (h + 1) * HEAD_DIM) for h in range(heads)]
    qs = [q_ref[:, c] for c in hc]
    dos = [do_ref[:, c] for c in hc]
    lse = [lse_ref[:, h : h + 1] for h in range(heads)]
    dsum = [
        jnp.sum(dos[h].astype(F32) * o_ref[:, hc[h]], axis=1, keepdims=True) for h in range(heads)
    ]

    def step(kb, carry):
        rows = pl.ds(pl.multiple_of(kb * block, block), block)
        allowed = (seg_q == sk_ref[kb]) & (kb * block + col0 <= row)
        out = []
        for h in range(heads):
            k_blk = k_ref[rows, hc[h]]
            s = jnp.where(allowed, dot_nt(qs[h], k_blk) * scale, NEG)
            p = jnp.exp(s - lse[h])
            dp = dot_nt(dos[h], v_ref[rows, hc[h]])
            ds = (p * (dp - dsum[h])).astype(BF)
            dv_ref[rows, hc[h]] += dot_tn(p.astype(BF), dos[h])
            dk_ref[rows, hc[h]] += dot_tn(ds, qs[h]) * scale
            out.append(carry[h] + dot_nn(ds, k_blk))
        return tuple(out)

    init = tuple(jnp.zeros((block, HEAD_DIM), F32) for _ in range(heads))
    final = lax.fori_loop(lo_ref[qb], qb + 1, step, init)
    for h in range(heads):
        dq_ref[:, hc[h]] = final[h] * scale


def attn_bwd(lo, q, k, v, do, o, lse, seg_col, seg_rows, block):
    tokens, cols = q.shape
    heads = cols // HEAD_DIM
    nb = tokens // block
    full = lambda shape: pl.BlockSpec(shape, lambda i, lo: (0,) * len(shape))
    rowed = lambda c: pl.BlockSpec((block, c), lambda i, lo: (i, 0))
    return pl.pallas_call(
        functools.partial(attn_bwd_body, block=block, heads=heads),
        out_shape=tuple(jax.ShapeDtypeStruct((tokens, cols), F32) for _ in range(3)),
        grid_spec=pltpu.PrefetchScalarGridSpec(
            num_scalar_prefetch=1,
            grid=(nb,),
            in_specs=[
                rowed(cols),
                full((tokens, cols)),
                full((tokens, cols)),
                rowed(cols),
                rowed(cols),
                rowed(heads),
                rowed(1),
                full((nb, 1, block)),
            ],
            out_specs=[rowed(cols), full((tokens, cols)), full((tokens, cols))],
        ),
        compiler_params=pltpu.CompilerParams(vmem_limit_bytes=40 * MIB),
        cost_estimate=pl.CostEstimate(
            flops=10**8, bytes_accessed=4 * MIB, transcendentals=10**5
        ),
        name="attn_bwd",
    )(lo, q, k, v, do, o, lse, seg_col, seg_rows)


def expert_body(*refs, first, rows_blk, parts):
    lead = first == 0
    if lead:
        x_hbm, g_hbm, mask_ref, wg_ref, wu_ref, wd_ref, router_ref = refs[:7]
        dgu_ref, ga_ref, wcat, dots_ref, grads_ref, xt_hbm, gates_ref, probs_ref = refs[7:15]
        x_v, xt_v, g_v, sem_x, sem_t, sem_g = refs[15:]
    else:
        x_hbm, g_hbm, gates_ref, wg_ref, wu_ref, wd_ref, xt_hbm = refs[:7]
        dgu_ref, ga_ref, wcat, dots_ref, grads_ref = refs[10:15]
        x_v, xt_v, g_v, sem_x, sem_t, sem_g = refs[15:]
    p = pl.program_id(0)
    tokens, width = x_v.shape
    nblk = tokens // rows_blk
    hid = wg_ref.shape[2]
    experts = gates_ref.shape[1]
    ds = width // parts

    if lead:
        t_copy = pltpu.make_async_copy(xt_v, xt_hbm, sem_t)
    else:
        t_copy = pltpu.make_async_copy(xt_hbm, xt_v, sem_t)

    def copies(i):
        r = pl.ds(i * rows_blk, rows_blk)
        return (
            pltpu.make_async_copy(x_hbm.at[r], x_v.at[r], sem_x.at[i]),
            pltpu.make_async_copy(g_hbm.at[r], g_v.at[r], sem_g.at[i]),
        )

    @pl.when(p == 0)
    def _():
        for i in range(nblk):
            for c in copies(i):
                c.start()
        if not lead:
            t_copy.start()
        dots_ref[...] = jnp.zeros_like(dots_ref)

    wcat[:, 0:hid] = wg_ref[0]
    wcat[:, hid : 2 * hid] = wg_ref[1]
    wcat[:, 2 * hid : 3 * hid] = wu_ref[0]
    wcat[:, 3 * hid : 4 * hid] = wu_ref[1]
    lane = lax.broadcasted_iota(jnp.int32, (rows_blk, experts), 1)
    e0 = 2 * (first + p)

    def block(i, _):
        start = pl.multiple_of(i * rows_blk, rows_blk)
        r = pl.ds(start, rows_blk)

        @pl.when(p == 0)
        def _():
            for c in copies(i):
                c.wait()

        if lead:
            xt_v[:, r] = x_v[r, :].T
            logits = dot_nn(x_v[r, :], router_ref[...])
            grown = jnp.exp(logits - jnp.max(logits, axis=1, keepdims=True))
            probs = grown / jnp.sum(grown, axis=1, keepdims=True)
            probs_ref[r, :] = probs
            gates_ref[r, :] = probs * mask_ref[r, :]
        gu = dot_nn(x_v[r, :], wcat[...])
        q = dot_nt(g_v[r, :], wd_ref[...])
        gate_rows = gates_ref[r, :]
        dots = dots_ref[r, :]
        for j in range(2):
            pre = gu[:, j * hid : (j + 1) * hid]
            up = gu[:, (2 + j) * hid : (3 + j) * hid]
            back = q[:, j * hid : (j + 1) * hid]
            here = lane == e0 + j
            gate = jnp.sum(jnp.where(here, gate_rows, 0.0), axis=1, keepdims=True)
            sig = jax.nn.sigmoid(pre)
            silu = pre * sig
            act = silu * up
            dot = jnp.sum(act * back, axis=1, keepdims=True)
            dots = dots + jnp.where(here, dot, 0.0)
            scaled = gate * back
            d_up = scaled * silu
            d_gate = scaled * up * (sig + silu * (1.0 - sig))
            dgu_ref[r, j * hid : (j + 1) * hid] = d_gate.astype(BF)
            dgu_ref[r, (2 + j) * hid : (3 + j) * hid] = d_up.astype(BF)
            ga_ref[r, j * hid : (j + 1) * hid] = (gate * act).astype(BF)
        dots_ref[r, :] = dots
        return 0

    lax.fori_loop(0, nblk, block, 0)

    @pl.when(p == 0)
    def _():
        if lead:
            t_copy.start()
        else:
            t_copy.wait()

    for s in range(parts):
        gd = dot_tn(ga_ref[...], g_v[:, s * ds : (s + 1) * ds]).astype(BF)
        gw = dot_nn(xt_v[s * ds : (s + 1) * ds, :], dgu_ref[...]).astype(BF)
        for j in range(2):
            grads_ref[s, 3 * j] = gw[:, j * hid : (j + 1) * hid]
            grads_ref[s, 3 * j + 1] = gw[:, (2 + j) * hid : (3 + j) * hid]
            for c in range(ds // hid):
                grads_ref[s, 3 * j + 2, c * hid : (c + 1) * hid, :] = gd[
                    j * hid : (j + 1) * hid, c * hid : (c + 1) * hid
                ]

    if lead:

        @pl.when(p == 0)
        def _():
            t_copy.wait()


def expert_chunk(x, g, gates, wg, wu, wd, router, carried, *, first, pairs, parts):
    tokens, width = x.shape
    experts, _, hid = wg.shape
    total = experts // 2
    rows_blk = 512
    nblk = tokens // rows_blk
    ds = width // parts
    lead = first == 0
    assert not lead or pairs == 1
    any_spec = pl.BlockSpec(memory_space=pl.ANY)
    colblk = lambda rows, c: pl.BlockSpec((rows, c), lambda p: (0, first + p))
    in_specs = [
        any_spec,
        any_spec,
        pl.BlockSpec((tokens, experts), lambda p: (0, 0)),
        pl.BlockSpec((2, width, hid), lambda p: (first + p, 0, 0)),
        pl.BlockSpec((2, width, hid), lambda p: (first + p, 0, 0)),
        pl.BlockSpec((2 * hid, width), lambda p: (first + p, 0)),
    ]
    out_shape = [
        jax.ShapeDtypeStruct((tokens, total * 4 * hid), BF),
        jax.ShapeDtypeStruct((tokens, total * 2 * hid), BF),
        jax.ShapeDtypeStruct((width, total * 4 * hid), BF),
        jax.ShapeDtypeStruct((tokens, experts), F32),
        jax.ShapeDtypeStruct((parts, pairs * 6, ds, hid), BF),
    ]
    out_specs = [
        colblk(tokens, 4 * hid),
        colblk(tokens, 2 * hid),
        colblk(width, 4 * hid),
        pl.BlockSpec((tokens, experts), lambda p: (0, 0)),
        pl.BlockSpec((parts, 6, ds, hid), lambda p: (0, p, 0, 0)),
    ]
    args = [x, g, gates, wg, wu, wd]
    alias = {}
    if lead:
        args.append(router)
        in_specs.append(pl.BlockSpec(router.shape, lambda p: (0, 0)))
        narrow = jax.ShapeDtypeStruct((tokens, experts), F32)
        out_shape += [jax.ShapeDtypeStruct((width, tokens), BF), narrow, narrow]
        out_specs += [any_spec] + [pl.BlockSpec((tokens, experts), lambda p: (0, 0))] * 2
    else:
        xt, dgu, ga, wcat = carried
        args += [xt, dgu, ga, wcat]
        in_specs += [any_spec] * 4
        alias = {7: 0, 8: 1, 9: 2}
    return pl.pallas_call(
        functools.partial(expert_body, first=first, rows_blk=rows_blk, parts=parts),
        out_shape=tuple(out_shape),
        grid=(pairs,),
        in_specs=in_specs,
        out_specs=out_specs,
        scratch_shapes=[
            pltpu.VMEM((tokens, width), BF),
            pltpu.VMEM((width, tokens), BF),
            pltpu.VMEM((tokens, width), BF),
            pltpu.SemaphoreType.DMA((nblk,)),
            pltpu.SemaphoreType.DMA,
            pltpu.SemaphoreType.DMA((nblk,)),
        ],
        input_output_aliases=alias,
        compiler_params=pltpu.CompilerParams(vmem_limit_bytes=61 * MIB),
        cost_estimate=pl.CostEstimate(
            flops=10**9, bytes_accessed=4 * MIB, transcendentals=10**5
        ),
        name="expert_chunk",
    )(*args)


GATHER_COPIES = 13


def gather_plan(x_hbm, land, me, own, send_sem, recv_sem):
    half = own // 2
    pc, px, py = (partner(me, b) for b in (1, 2, 4))
    diag = partner(px, 4)

    def piece(dev, a, n):
        return land.at[pl.ds(pl.multiple_of(dev * own + a, half), n)]

    plan = [
        (me, 0, half, px),
        (me, half, half, py),
        (me, half, half, px),
        (me, 0, half, py),
        (me, 0, own, pc),
        (px, 0, half, py),
        (py, half, half, px),
        (px, 0, half, pc),
        (py, half, half, pc),
        (px, half, half, pc),
        (py, 0, half, pc),
        (diag, 0, half, pc),
        (diag, half, half, pc),
    ]
    origin = {0: px, 1: py, 2: px, 3: py, 4: pc, 5: diag, 6: diag}

    def copy(k):
        dev, a, n, target = plan[k]
        src = x_hbm.at[pl.ds(a, n)] if k < 5 else piece(dev, a, n)
        return remote(src, piece(dev, a, n), send_sem.at[k], recv_sem.at[k], target)

    def arrived(k):
        dev, a, n, target = plan[k]
        src = origin[k] if k in origin else partner(dev, 1)
        return remote(piece(src, a, n), piece(src, a, n), send_sem.at[k], recv_sem.at[k], target)

    return copy, arrived, pc, px, py, diag


def front_body(
    x_hbm, wo_hbm, g_hbm, wq_hbm, wk_hbm, wv_hbm, gain_ref, qg_ref, kg_ref, mg_ref, pos_ref, sq_ref, sk_ref,
    normed_hbm, *rest, size, block, reach
):
    outs, rest = rest[:13], rest[13:]
    g_all, rest = rest[0], rest[1:]
    local, rest = rest[:13], rest[13:]
    (
        q_ref, k_ref, v_ref, qu_ref, ku_ref, rs_ref, cos_ref, sin_ref, o_ref, low_ref, lse_ref, res_ref, moe_ref,
    ) = local
    (
        x_v, n_v, w_v, wo_all, own_ref, sums, sums_all,
        send_sem, recv_sem, wo_send, wo_recv, g_send, g_recv, ss_send, ss_recv, a_send, a_recv,
        w_sem, x_sem, wo_sem, g_sem, a_sem, n_sem, o_sem,
    ) = rest

    def written(i):
        return pltpu.make_async_copy(local[i], outs[i], o_sem.at[i])

    me = lax.axis_index("tensor")
    own = x_hbm.shape[0]
    width = x_hbm.shape[1]
    cols = q_ref.shape[1]
    heads = cols // HEAD_DIM
    half_dim = HEAD_DIM // 2
    weights = [
        pltpu.make_async_copy(w, w_v.at[:, pl.ds(i * cols, cols)], w_sem.at[i])
        for i, w in enumerate((wq_hbm, wk_hbm, wv_hbm))
    ]
    mine = pl.ds(pl.multiple_of(me * own, own), own)
    here = pltpu.make_async_copy(x_hbm, x_v.at[mine], x_sem)
    here.start()
    for w in weights:
        w.start()
    greet([lax.rem(me + t, size) for t in range(1, size)])
    copy, arrived, pc, px, py, diag = gather_plan(x_hbm, x_v, me, own, send_sem, recv_sem)
    wo_copy, wo_arrived = gather_plan(wo_hbm, wo_all, me, own, wo_send, wo_recv)[:2]
    for k in range(5):
        copy(k).start()
    g_copy, g_arrived = gather_plan(g_hbm, g_all, me, own, g_send, g_recv)[:2]
    wo_here = pltpu.make_async_copy(wo_hbm, wo_all.at[mine], wo_sem)
    wo_here.start()
    g_here = pltpu.make_async_copy(g_hbm, g_all.at[mine], g_sem)
    g_here.start()

    lane = lax.broadcasted_iota(jnp.int32, (own, HEAD_DIM), 1)
    power = (lane % half_dim).astype(F32) * (-2.0 * math.log(10000.0) / HEAD_DIM)
    frequency = jnp.exp(power)

    def table(i, _):
        r = pl.ds(pl.multiple_of(i * own, own), own)
        angle = pos_ref[r, :] * frequency
        cos_ref[r, :] = jnp.cos(angle)
        sine = jnp.sin(angle)
        sin_ref[r, :] = jnp.where(lane < half_dim, -sine, sine)
        return 0

    lax.fori_loop(0, size, table, 0)
    for i in (6, 7):
        written(i).start()

    def stored(dev):
        r = pl.ds(pl.multiple_of(dev * own, own), own)
        return pltpu.make_async_copy(n_v.at[r], normed_hbm.at[r], n_sem.at[dev])

    def process(dev):
        r = pl.ds(pl.multiple_of(dev * own, own), own)
        wide = x_v[r, :].astype(F32)
        scale = lax.rsqrt(jnp.mean(wide * wide, axis=1, keepdims=True) + EPS)
        normed = (wide * scale * gain_ref[...]).astype(BF)
        n_v[r, :] = normed
        stored(dev).start()
        res = dot_nn(normed, w_v[...])
        q = res[:, :cols]
        k = res[:, cols : 2 * cols]
        qu_ref[r, :] = q
        ku_ref[r, :] = k
        v_ref[r, :] = res[:, 2 * cols :].astype(BF)
        pair = jnp.where(
            lane == 0,
            jnp.sum(q * q, axis=1, keepdims=True),
            jnp.sum(k * k, axis=1, keepdims=True),
        )
        sums[dev] = pair.T[0:2, :]

    here.wait()
    for w in weights:
        w.wait()
    process(me)
    arrived(4).wait_recv()
    process(pc)
    arrived(0).wait_recv()
    copy(5).start()
    copy(7).start()
    arrived(1).wait_recv()
    copy(6).start()
    copy(8).start()
    arrived(2).wait_recv()
    copy(9).start()
    arrived(3).wait_recv()
    copy(10).start()
    for k in range(5):
        wo_copy(k).start()
    process(px)
    process(py)
    arrived(7).wait_recv()
    arrived(9).wait_recv()
    process(partner(px, 1))
    arrived(8).wait_recv()
    arrived(10).wait_recv()
    process(partner(py, 1))
    arrived(5).wait_recv()
    copy(11).start()
    arrived(6).wait_recv()
    copy(12).start()
    process(diag)
    arrived(11).wait_recv()
    arrived(12).wait_recv()
    process(partner(diag, 1))
    hand_on(wo_arrived, wo_copy, ((0, (5, 7)), (1, (6, 8))))

    def exchange(t, src):
        other = lax.rem(me + t, size)
        slot = me if src is None else other
        return remote(sums, sums_all.at[slot], ss_send.at[other], ss_recv.at[slot], other)

    for t in range(1, size):
        exchange(t, None).start()
    sums_all[me] = sums[...]
    hand_on(wo_arrived, wo_copy, ((2, (9,)), (3, (10,))))
    for k in range(5):
        g_copy(k).start()
    for t in range(1, size):
        exchange(t, 1).wait_recv()
    total = sums_all[0]
    for d in range(1, size):
        total = total + sums_all[d]
    rows_iota = lax.broadcasted_iota(jnp.int32, (HEAD_DIM, own), 0)
    for d in range(size):
        r = slice(d * own, (d + 1) * own)
        tot = total[d]
        both = jnp.where(rows_iota == 0, tot[0:1, :], tot[1:2, :])
        rs = lax.rsqrt(both / width + EPS).T
        rs_ref[r, :] = rs[:, 0:2]
        cos, sin = cos_ref[r, :], sin_ref[r, :]
        for j, (unit_ref, gain, dst) in enumerate(((qu_ref, qg_ref, q_ref), (ku_ref, kg_ref, k_ref))):
            unit = unit_ref[r, :] * rs[:, j : j + 1]
            unit_ref[r, :] = unit
            wide = unit * gain[...]
            for h in range(heads):
                c = slice(h * HEAD_DIM, (h + 1) * HEAD_DIM)
                w = wide[:, c]
                dst[r, c] = (w * cos + pltpu.roll(w, half_dim, 1) * sin).astype(BF)

    for i in range(6):
        written(i).start()
    score_scale = 1.0 / math.sqrt(HEAD_DIM)
    row0 = lax.broadcasted_iota(jnp.int32, (block, block), 0)
    col0 = lax.broadcasted_iota(jnp.int32, (block, block), 1)
    hc = [slice(h * HEAD_DIM, (h + 1) * HEAD_DIM) for h in range(heads)]

    def land(src):
        return own_ref.at[:, pl.ds(pl.multiple_of(src * cols, HEAD_DIM), cols)]

    def rows_of(dev):
        return low_ref.at[pl.ds(pl.multiple_of(dev * own, own), own)]

    def send(t):
        return remote(rows_of(t), land(me), a_send.at[t], a_recv.at[me], t)

    def query_block(qb, _):
        rq = pl.ds(pl.multiple_of(qb * block, block), block)
        seg_q = sq_ref[rq, :]
        qs = [q_ref[rq, c] for c in hc]

        def step(kb, carry):
            rows = pl.ds(pl.multiple_of(kb * block, block), block)
            allowed = (seg_q == sk_ref[kb]) & (kb * block + col0 <= qb * block + row0)
            out = []
            for h in range(heads):
                m, l, acc = carry[h]
                s = jnp.where(allowed, dot_nt(qs[h], k_ref[rows, hc[h]]) * score_scale, NEG)
                m_new = jnp.maximum(m, jnp.max(s, axis=1, keepdims=True))
                p = jnp.exp(s - m_new)
                alpha = jnp.exp(m - m_new)
                l = alpha * l + jnp.sum(p, axis=1, keepdims=True)
                acc = alpha * acc + dot_nn(p.astype(BF), v_ref[rows, hc[h]])
                out.append((m_new, l, acc))
            return tuple(out)

        init = tuple(
            (
                jnp.full((block, 1), NEG, F32),
                jnp.zeros((block, 1), F32),
                jnp.zeros((block, HEAD_DIM), F32),
            )
            for _ in range(heads)
        )
        final = lax.fori_loop(jnp.maximum(qb - reach, 0), qb + 1, step, init)
        for h in range(heads):
            m, l, acc = final[h]
            out = acc / l
            o_ref[rq, hc[h]] = out
            low_ref[rq, hc[h]] = out.astype(BF)
            lse_ref[rq, h : h + 1] = m + jnp.log(l)

        @pl.when(qb != me)
        def _():
            send(qb).start()

        @pl.when(qb == me)
        def _():
            pltpu.make_async_copy(rows_of(me), land(me), a_sem).start()

        @pl.when(qb == 3)
        def _():
            hand_on(wo_arrived, wo_copy, ((5, (11,)), (6, (12,))))

        @pl.when(qb == 5)
        def _():
            hand_on(g_arrived, g_copy, ((0, (5, 7)), (1, (6, 8))))

        return 0

    lax.fori_loop(0, size, query_block, 0)
    for i in (8, 9, 10):
        written(i).start()
    pltpu.make_async_copy(rows_of(me), land(me), a_sem).wait()
    for t in range(1, size):
        other = lax.rem(me + t, size)
        remote(rows_of(other), land(other), a_send.at[other], a_recv.at[other], other).wait_recv()
    for k in (4, 7, 8, 9, 10, 11, 12):
        wo_arrived(k).wait_recv()
    wo_here.wait()
    sl = width // 4
    total = jnp.zeros((own, 1), F32)
    for i in range(4):
        c = slice(i * sl, (i + 1) * sl)
        part = x_v[mine, c].astype(F32) + dot_nn(own_ref[...], wo_all[:, c])
        res_ref[:, c] = part
        total = total + jnp.sum(part * part, axis=1, keepdims=True)
    scale = lax.rsqrt(total / width + EPS)
    for i in range(4):
        c = slice(i * sl, (i + 1) * sl)
        moe_ref[:, c] = (res_ref[:, c] * scale * mg_ref[:, c]).astype(BF)
    for i in (11, 12):
        written(i).start()
    hand_on(g_arrived, g_copy, ((2, (9,)), (3, (10,)), (5, (11,)), (6, (12,))))
    for t in range(1, size):
        exchange(t, None).wait_send()
        send(lax.rem(me + t, size)).wait_send()
    for d in range(size):
        stored(d).wait()
    for k in (4, 7, 8, 9, 10, 11, 12):
        g_arrived(k).wait_recv()
    for k in range(GATHER_COPIES):
        copy(k).wait_send()
        wo_copy(k).wait_send()
        g_copy(k).wait_send()
    g_here.wait()
    for i in range(13):
        written(i).wait()


def hand_on(arrived, copy, steps):
    for k, following in steps:
        arrived(k).wait_recv()
        for f in following:
            copy(f).start()


def front(x, wo, g, wq, wk, wv, gain, qg, kg, mg, pos, seg_col, seg_rows, size, block, reach, cid):
    own, width = x.shape
    cols = wq.shape[1]
    tokens = own * size
    heads = cols // HEAD_DIM
    any_spec = pl.BlockSpec(memory_space=pl.ANY)
    vm = pl.BlockSpec(memory_space=pltpu.VMEM)
    arr = jax.ShapeDtypeStruct
    dma = pltpu.SemaphoreType.DMA
    kept = (
            arr((tokens, cols), BF),
            arr((tokens, cols), BF),
            arr((tokens, cols), BF),
            arr((tokens, cols), F32),
            arr((tokens, cols), F32),
            arr((tokens, 2), F32),
            arr((tokens, HEAD_DIM), F32),
            arr((tokens, HEAD_DIM), F32),
            arr((tokens, cols), F32),
            arr((tokens, cols), BF),
            arr((tokens, heads), F32),
            arr((own, width), F32),
            arr((own, width), BF),
    )
    return pl.pallas_call(
        functools.partial(front_body, size=size, block=block, reach=reach),
        out_shape=(
            arr((tokens, width), BF),
            *kept,
            arr((tokens, width), BF),
        ),
        in_specs=[any_spec] * 6 + [vm] * 7,
        out_specs=[any_spec] * 15,
        scratch_shapes=[pltpu.VMEM(k.shape, k.dtype) for k in kept]
        + [
            pltpu.VMEM((tokens, width), BF),
            pltpu.VMEM((tokens, width), BF),
            pltpu.VMEM((width, 3 * cols), BF),
            pltpu.VMEM((width, width), BF),
            pltpu.VMEM((own, width), BF),
            pltpu.VMEM((size, 2, own), F32),
            pltpu.VMEM((size, size, 2, own), F32),
        ]
        + [dma((GATHER_COPIES,))] * 6
        + [dma((size,))] * 4
        + [
            dma((3,)),
            dma,
            dma,
            dma,
            dma,
            dma((size,)),
            dma((13,)),
        ],
        compiler_params=pltpu.CompilerParams(
            vmem_limit_bytes=58 * MIB, collective_id=cid, has_side_effects=True
        ),
        cost_estimate=pl.CostEstimate(flops=10**8, bytes_accessed=4 * MIB, transcendentals=0),
        name="front",
    )(x, wo, g, wq, wk, wv, gain[None, :], qg[None, :], kg[None, :], mg[None, :], pos, seg_col, seg_rows)


def middle_body(
    own_hbm, g_hbm, mask_ref, router_ref, wg_ref, wu_ref, wd_ref,
    moe_hbm, dgu_hbm, ga_hbm, wcat_hbm, dots_ref, grads_ref, xt_hbm, gates_ref, probs_ref,
    x_v, xt_v, g_v, wcat, dgu_v, ga_v, send_sem, recv_sem, own_sem, g_sem, m_sem, out_sem, *, size, parts
):
    me = lax.axis_index("tensor")
    tokens, width = x_v.shape
    own = tokens // size
    hid = wg_ref.shape[2]
    experts = gates_ref.shape[1]
    ds = width // parts

    def g_copy(d):
        r = pl.ds(d * own, own)
        return pltpu.make_async_copy(g_hbm.at[r], g_v.at[r], g_sem.at[d])

    mine = pl.ds(pl.multiple_of(me * own, own), own)
    own_copy = pltpu.make_async_copy(own_hbm, x_v.at[mine], own_sem)
    own_copy.start()
    greet([partner(me, b) for b in (1, 2, 4)])
    copy, arrived, pc, px, py, diag = gather_plan(own_hbm, x_v, me, own, send_sem, recv_sem)
    for k in range(5):
        copy(k).start()
    for d in range(size):
        g_copy(d).start()

    wcat[:, 0:hid] = wg_ref[0]
    wcat[:, hid : 2 * hid] = wg_ref[1]
    wcat[:, 2 * hid : 3 * hid] = wu_ref[0]
    wcat[:, 3 * hid : 4 * hid] = wu_ref[1]
    wcat_out = pltpu.make_async_copy(wcat, wcat_hbm.at[:, pl.ds(0, 4 * hid)], out_sem.at[0])
    wcat_out.start()
    own_copy.wait()
    for d in range(size):
        g_copy(d).wait()
    lane = lax.broadcasted_iota(jnp.int32, (own, experts), 1)

    def moe_out(dev):
        r = pl.ds(pl.multiple_of(dev * own, own), own)
        return pltpu.make_async_copy(x_v.at[r], moe_hbm.at[r], m_sem.at[dev])

    def process(dev):
        r = pl.ds(pl.multiple_of(dev * own, own), own)
        moe_out(dev).start()
        xt_v[:, r] = x_v[r, :].T
        logits = dot_nn(x_v[r, :], router_ref[...])
        grown = jnp.exp(logits - jnp.max(logits, axis=1, keepdims=True))
        probs = grown / jnp.sum(grown, axis=1, keepdims=True)
        probs_ref[r, :] = probs
        gate_rows = probs * mask_ref[r, :]
        gates_ref[r, :] = gate_rows
        gu = dot_nn(x_v[r, :], wcat[...])
        q = dot_nt(g_v[r, :], wd_ref[...])
        dots = jnp.zeros((own, experts), F32)
        for j in range(2):
            pre = gu[:, j * hid : (j + 1) * hid]
            up = gu[:, (2 + j) * hid : (3 + j) * hid]
            back = q[:, j * hid : (j + 1) * hid]
            here = lane == j
            gate = jnp.sum(jnp.where(here, gate_rows, 0.0), axis=1, keepdims=True)
            sig = jax.nn.sigmoid(pre)
            silu = pre * sig
            act = silu * up
            dot = jnp.sum(act * back, axis=1, keepdims=True)
            dots = dots + jnp.where(here, dot, 0.0)
            scaled = gate * back
            d_up = scaled * silu
            d_gate = scaled * up * (sig + silu * (1.0 - sig))
            dgu_v[r, j * hid : (j + 1) * hid] = d_gate.astype(BF)
            dgu_v[r, (2 + j) * hid : (3 + j) * hid] = d_up.astype(BF)
            ga_v[r, j * hid : (j + 1) * hid] = (gate * act).astype(BF)
        dots_ref[r, :] = dots

    process(me)
    arrived(4).wait_recv()
    process(pc)
    arrived(0).wait_recv()
    copy(5).start()
    copy(7).start()
    arrived(1).wait_recv()
    copy(6).start()
    copy(8).start()
    arrived(2).wait_recv()
    copy(9).start()
    arrived(3).wait_recv()
    copy(10).start()
    process(px)
    process(py)
    arrived(7).wait_recv()
    arrived(9).wait_recv()
    process(partner(px, 1))
    arrived(8).wait_recv()
    arrived(10).wait_recv()
    process(partner(py, 1))
    arrived(5).wait_recv()
    copy(11).start()
    arrived(6).wait_recv()
    copy(12).start()
    process(diag)
    arrived(11).wait_recv()
    arrived(12).wait_recv()
    process(partner(diag, 1))

    outs = [
        pltpu.make_async_copy(dgu_v, dgu_hbm.at[:, pl.ds(0, 4 * hid)], out_sem.at[1]),
        pltpu.make_async_copy(ga_v, ga_hbm.at[:, pl.ds(0, 2 * hid)], out_sem.at[2]),
        pltpu.make_async_copy(xt_v, xt_hbm, out_sem.at[3]),
    ]
    for o in outs:
        o.start()
    for s in range(parts):
        gd = dot_tn(ga_v[...], g_v[:, s * ds : (s + 1) * ds]).astype(BF)
        gw = dot_nn(xt_v[s * ds : (s + 1) * ds, :], dgu_v[...]).astype(BF)
        for j in range(2):
            grads_ref[s, 3 * j] = gw[:, j * hid : (j + 1) * hid]
            grads_ref[s, 3 * j + 1] = gw[:, (2 + j) * hid : (3 + j) * hid]
            for c in range(ds // hid):
                grads_ref[s, 3 * j + 2, c * hid : (c + 1) * hid, :] = gd[
                    j * hid : (j + 1) * hid, c * hid : (c + 1) * hid
                ]
    wcat_out.wait()
    for o in outs:
        o.wait()
    for d in range(size):
        moe_out(d).wait()
    for k in range(GATHER_COPIES):
        copy(k).wait_send()


def middle(own_rows, g, mask, router, wg, wu, wd, size, parts, cid):
    own, width = own_rows.shape
    tokens = own * size
    experts, _, hid = wg.shape
    total = experts // 2
    ds = width // parts
    any_spec = pl.BlockSpec(memory_space=pl.ANY)
    vm = pl.BlockSpec(memory_space=pltpu.VMEM)
    first = lambda shape: pl.BlockSpec(shape, lambda i: (0,) * len(shape))
    arr = jax.ShapeDtypeStruct
    dma = pltpu.SemaphoreType.DMA
    narrow = arr((tokens, experts), F32)
    return pl.pallas_call(
        functools.partial(middle_body, size=size, parts=parts),
        out_shape=(
            arr((tokens, width), BF),
            arr((tokens, total * 4 * hid), BF),
            arr((tokens, total * 2 * hid), BF),
            arr((width, total * 4 * hid), BF),
            narrow,
            arr((parts, 6, ds, hid), BF),
            arr((width, tokens), BF),
            narrow,
            narrow,
        ),
        grid=(1,),
        in_specs=[
            any_spec,
            any_spec,
            first((tokens, experts)),
            first(router.shape),
            first((2, width, hid)),
            first((2, width, hid)),
            first((2 * hid, width)),
        ],
        out_specs=[
            any_spec,
            any_spec,
            any_spec,
            any_spec,
            first((tokens, experts)),
            first((parts, 6, ds, hid)),
            any_spec,
            first((tokens, experts)),
            first((tokens, experts)),
        ],
        scratch_shapes=[
            pltpu.VMEM((tokens, width), BF),
            pltpu.VMEM((width, tokens), BF),
            pltpu.VMEM((tokens, width), BF),
            pltpu.VMEM((width, 4 * hid), BF),
            pltpu.VMEM((tokens, 4 * hid), BF),
            pltpu.VMEM((tokens, 2 * hid), BF),
            dma((GATHER_COPIES,)),
            dma((GATHER_COPIES,)),
            dma,
            dma((size,)),
            dma((size,)),
            dma((4,)),
        ],
        compiler_params=pltpu.CompilerParams(
            vmem_limit_bytes=62 * MIB, collective_id=cid, has_side_effects=True
        ),
        cost_estimate=pl.CostEstimate(flops=10**9, bytes_accessed=4 * MIB, transcendentals=0),
        name="middle",
    )(own_rows, g, mask, router, wg, wu, wd)


def matmul_scatter_body(
    l_hbm, r_hbm, out_ref, l_v, r_v, part, got1, got2, got3, sem_l, sem_r, send_sem, recv_sem,
    *, size, slices, nt
):
    me = lax.axis_index("tensor")
    tokens = l_v.shape[0]
    own = tokens // size
    sn = out_ref.shape[1] // slices
    mine = [(me // b) % 2 for b in (1, 2, 4)]
    group = 2

    def l_copy(i):
        r = pl.ds(i * own * group, own * group)
        return pltpu.make_async_copy(l_hbm.at[r], l_v.at[r], sem_l.at[i])

    def r_copy(s):
        c = pl.ds(s * sn, sn)
        if nt:
            return pltpu.make_async_copy(r_hbm.at[c], r_v.at[c], sem_r.at[s])
        return pltpu.make_async_copy(r_hbm.at[:, c], r_v.at[:, c], sem_r.at[s])

    r_copy(0).start()
    for i in range(size // group):
        l_copy(i).start()
    for s in range(1, slices):
        r_copy(s).start()
    greet([partner(me, b) for b in (1, 2, 4)])

    def hop(s, stage):
        a, b = (1, 2) if s % 2 == 0 else (2, 1)
        if stage == 0:
            src, dst, bit = part.at[s, 1 - mine[0]], got1.at[s], 1
        elif stage == 1:
            src, dst, bit = part.at[s, mine[0], pl.ds(2 * (1 - mine[a]), 2)], got2.at[s], 1 << a
        else:
            src, dst, bit = part.at[s, mine[0], 2 * mine[a] + 1 - mine[b]], got3.at[s], 1 << b
        return remote(src, dst, send_sem.at[stage, s], recv_sem.at[stage, s], partner(me, bit))

    def compute(s):
        r_copy(s).wait()

        def rows(i, _):
            if s == 0:
                l_copy(i).wait()
            r = pl.ds(pl.multiple_of(i * own * group, own * group), own * group)
            if nt:
                res = dot_nt(l_v[r, :], r_v[s * sn : (s + 1) * sn, :])
            else:
                res = dot_nn(l_v[r, :], r_v[:, s * sn : (s + 1) * sn])
            res = res.astype(BF)
            x, y = i % 2, i // 2
            pos = 2 * x + y if s % 2 == 0 else 2 * y + x
            for c in range(2):
                part[s, c, pos] = res[c * own : (c + 1) * own]
            return 0

        lax.fori_loop(0, size // group, rows, 0)
        hop(s, 0).start()

    def first(s):
        hop(s, 0).wait_recv()
        part[s, mine[0]] = (part[s, mine[0]].astype(F32) + got1[s].astype(F32)).astype(BF)
        hop(s, 1).start()

    def second(s):
        a = 1 if s % 2 == 0 else 2
        hop(s, 1).wait_recv()
        ix = pl.ds(2 * mine[a], 2)
        part[s, mine[0], ix] = (part[s, mine[0], ix].astype(F32) + got2[s].astype(F32)).astype(BF)
        hop(s, 2).start()

    def third(s):
        a, b = (1, 2) if s % 2 == 0 else (2, 1)
        hop(s, 2).wait_recv()
        out_ref[:, s * sn : (s + 1) * sn] = part[s, mine[0], 2 * mine[a] + mine[b]].astype(
            F32
        ) + got3[s].astype(F32)

    for t in range(slices + 5):
        if t < slices:
            compute(t)
        if 0 <= t - 1 < slices:
            first(t - 1)
        if 0 <= t - 3 < slices:
            second(t - 3)
        if 0 <= t - 5 < slices:
            third(t - 5)
    for s in range(slices):
        for stage in range(3):
            hop(s, stage).wait_send()


def matmul_scatter(left, right, size, cid, nt, name):
    tokens, depth = left.shape
    width = right.shape[0] if nt else right.shape[1]
    own = tokens // size
    if size != 8:
        part = (dot_nt if nt else dot_nn)(left, right).astype(BF)
        return lax.psum_scatter(part, "tensor", scatter_dimension=0, tiled=True).astype(F32)
    slices = 8
    sn = width // slices
    any_spec = pl.BlockSpec(memory_space=pl.ANY)
    return pl.pallas_call(
        functools.partial(matmul_scatter_body, size=size, slices=slices, nt=nt),
        out_shape=jax.ShapeDtypeStruct((own, width), F32),
        in_specs=[any_spec, any_spec],
        out_specs=pl.BlockSpec(memory_space=pltpu.VMEM),
        scratch_shapes=[
            pltpu.VMEM(left.shape, BF),
            pltpu.VMEM(right.shape, BF),
            pltpu.VMEM((slices, 2, size // 2, own, sn), BF),
            pltpu.VMEM((slices, size // 2, own, sn), BF),
            pltpu.VMEM((slices, size // 4, own, sn), BF),
            pltpu.VMEM((slices, own, sn), BF),
            pltpu.SemaphoreType.DMA((size // 2,)),
            pltpu.SemaphoreType.DMA((slices,)),
            pltpu.SemaphoreType.DMA((3, slices)),
            pltpu.SemaphoreType.DMA((3, slices)),
        ],
        compiler_params=pltpu.CompilerParams(
            vmem_limit_bytes=60 * MIB, collective_id=cid, has_side_effects=True
        ),
        cost_estimate=pl.CostEstimate(
            flops=10**9, bytes_accessed=4 * MIB, transcendentals=0
        ),
        name=name,
    )(left, right)


def gather_body(x_ref, out_ref, send_sem, recv_sem, here_sem):
    me = lax.axis_index("tensor")
    own = x_ref.shape[0]
    greet([partner(me, b) for b in (1, 2, 4)])
    mine = pl.ds(pl.multiple_of(me * own, own), own)
    here = pltpu.make_async_copy(x_ref, out_ref.at[mine], here_sem)
    here.start()
    copy, arrived = gather_plan(x_ref, out_ref, me, own, send_sem, recv_sem)[:2]
    for k in range(5):
        copy(k).start()
    for k, following in ((0, (5, 7)), (1, (6, 8)), (2, (9,)), (3, (10,)), (5, (11,)), (6, (12,))):
        arrived(k).wait_recv()
        for f in following:
            copy(f).start()
    for k in (4, 7, 8, 9, 10, 11, 12):
        arrived(k).wait_recv()
    for k in range(GATHER_COPIES):
        copy(k).wait_send()
    here.wait()


def gather_all(value, size, cid, name):
    own, cols = value.shape
    if size != 8:
        return lax.all_gather(value, "tensor", axis=0, tiled=True)
    any_spec = pl.BlockSpec(memory_space=pl.ANY)
    return pl.pallas_call(
        gather_body,
        out_shape=jax.ShapeDtypeStruct((own * size, cols), value.dtype),
        in_specs=[any_spec],
        out_specs=any_spec,
        scratch_shapes=[
            pltpu.SemaphoreType.DMA((GATHER_COPIES,)),
            pltpu.SemaphoreType.DMA((GATHER_COPIES,)),
            pltpu.SemaphoreType.DMA,
        ],
        compiler_params=pltpu.CompilerParams(collective_id=cid, has_side_effects=True),
        cost_estimate=pl.CostEstimate(flops=0, bytes_accessed=4 * MIB, transcendentals=0),
        name=name,
    )(value)


def swap(value, axis, size, bit):
    return lax.ppermute(value, axis, [(i, i ^ bit) for i in range(size)])


def sum_all(value, axis, size):
    bit = 1
    while bit < size:
        value = value + swap(value, axis, size, bit)
        bit *= 2
    return value


def sum_everywhere(value, n_tensor, n_dp):
    me = lax.axis_index("tensor")
    bits = [1 << b for b in range(n_tensor.bit_length() - 1)]
    for bit in bits[::-1]:
        half = value.shape[1] // 2
        low, high = value[:, :half], value[:, half:]
        upper = (me // bit) % 2 == 1
        send = jnp.where(upper, low, high)
        value = jnp.where(upper, high, low) + swap(send, "tensor", n_tensor, bit)
    value = sum_all(value, "dp", n_dp)
    for bit in bits:
        got = swap(value, "tensor", n_tensor, bit)
        upper = (me // bit) % 2 == 1
        value = jnp.concatenate(
            [jnp.where(upper, got, value), jnp.where(upper, value, got)], axis=1
        )
    return value


def half_swap(values):
    pieces = []
    half = HEAD_DIM // 2
    for h in range(values.shape[1] // HEAD_DIM):
        base = h * HEAD_DIM
        pieces += [values[:, base + half : base + HEAD_DIM], values[:, base : base + half]]
    return jnp.concatenate(pieces, axis=1)


def per_device(
    block_input, segments, routes, w_query, w_key, w_value, w_output, attn_gain, query_gain, key_gain,
    moe_gain, router, w_gate, w_up, w_down, cotangent, *, n_dp, n_tensor
):
    own_rows, model_width = block_input.shape
    local_cols = w_query.shape[1]
    local_heads = local_cols // HEAD_DIM
    token_count = segments.shape[0] * segments.shape[1]
    experts = router.shape[1]
    top_count = routes.shape[1]
    hid = w_gate.shape[2]
    capacity = 5 * token_count * top_count // (4 * experts)
    me = lax.axis_index("tensor")
    rank_start = me * own_rows
    col_start = me * local_cols
    block = 256

    seg = segments.reshape(token_count)
    values16 = jnp.arange(16, dtype=jnp.int32)
    below = jnp.sum((seg[None, :] < values16[:, None]).astype(jnp.int32), axis=1)
    doc_start = jnp.sum(
        jnp.where(seg[:, None] == values16[None, :], below[None, :], 0), axis=1
    )
    positions = jnp.arange(token_count, dtype=jnp.int32) - doc_start
    lo_block = doc_start[::block] // block
    seg_col = seg[:, None]
    seg_rows = seg.reshape(token_count // block, 1, block)

    expert_ids = jnp.arange(experts, dtype=jnp.int32)
    routed = jnp.sum(
        (routes[:, :, None] == expert_ids[None, None, :]).astype(F32), axis=1
    )
    tri = (
        jnp.arange(block, dtype=jnp.int32)[:, None] > jnp.arange(block, dtype=jnp.int32)[None, :]
    ).astype(BF)
    nb = token_count // block
    routed_b = routed.reshape(nb, block, experts)
    within = jnp.einsum("ij,bje->bie", tri, routed_b.astype(BF), preferred_element_type=F32)
    sums = jnp.sum(routed_b, axis=1)
    before = jnp.sum(
        jnp.where(
            (jnp.arange(nb)[:, None] > jnp.arange(nb)[None, :])[:, :, None], sums[None, :, :], 0.0
        ),
        axis=1,
    )
    place = within + before[:, None, :]
    mask = (routed_b * (place < capacity).astype(F32)).reshape(token_count, experts)

    w_qkv = jnp.concatenate([w_query, w_key, w_value], axis=1)
    pos_col = positions.astype(F32)[:, None]
    input_own = block_input.astype(F32)
    wd_flat = w_down.reshape(experts * hid, model_width)
    reach = min(1024 // block, token_count // block)
    if n_tensor == 8:
        (
            normed, queries, keys_rot, value_low, query_unit, key_unit, scales, cos_one, sin_one,
            attended, attn_low, lse, residual, own_moe_in, full_cot,
        ) = front(
            block_input, w_output, cotangent, w_query, w_key, w_value, attn_gain, query_gain, key_gain, moe_gain,
            pos_col, seg_col, seg_rows,
            n_tensor, block, reach, 6,
        )
        query_rs, key_rs = scales[:, 0:1], scales[:, 1:2]
        cos_all = jnp.concatenate([cos_one] * local_heads, axis=1)
        sin_all = jnp.concatenate([sin_one] * local_heads, axis=1)
        lead = middle(
            own_moe_in, full_cot, mask, router, w_gate, w_up, wd_flat, n_tensor, n_dp, 1
        )
        moe_in, lead = lead[0], lead[1:]
    else:
        half = HEAD_DIM // 2
        frequency = jnp.exp(
            jnp.arange(half, dtype=F32) * (-2.0 * math.log(10000.0) / HEAD_DIM)
        )
        angles = pos_col * frequency[None, :]
        cosine, sine = jnp.cos(angles), jnp.sin(angles)
        cos_all = jnp.concatenate([cosine] * (2 * local_heads), axis=1)
        sin_all = jnp.concatenate([-sine, sine] * local_heads, axis=1)
        full_cot = lax.all_gather(cotangent, "tensor", axis=0, tiled=True)
        full_wo = lax.all_gather(w_output, "tensor", axis=0, tiled=True)
        input_wide = lax.all_gather(block_input, "tensor", axis=0, tiled=True).astype(F32)
        normed = (input_wide * rms_scale(input_wide) * attn_gain).astype(BF)
        qkv = dot_nn(normed, w_qkv)
        query_raw = qkv[:, :local_cols]
        key_raw = qkv[:, local_cols : 2 * local_cols]
        value_low = qkv[:, 2 * local_cols :].astype(BF)
        squares = jnp.stack(
            [jnp.sum(query_raw * query_raw, axis=1), jnp.sum(key_raw * key_raw, axis=1)]
        )
        squares = sum_all(squares, "tensor", n_tensor)
        scales = lax.rsqrt(squares / model_width + EPS)
        query_rs, key_rs = scales[0][:, None], scales[1][:, None]
        query_unit = query_raw * query_rs
        key_unit = key_raw * key_rs
        q_n = query_unit * query_gain
        k_n = key_unit * key_gain
        queries = (q_n * cos_all + half_swap(q_n) * sin_all).astype(BF)
        keys_rot = (k_n * cos_all + half_swap(k_n) * sin_all).astype(BF)
        attended, attn_low, lse, own_attn = attn_fwd(
            queries, keys_rot, value_low, seg_col, seg_rows, block, reach, n_tensor, 0
        )
        residual = input_own + dot_nn(own_attn, full_wo)
        own_moe_in = (residual * rms_scale(residual) * moe_gain).astype(BF)
        moe_in = lax.all_gather(own_moe_in, "tensor", axis=0, tiled=True)
        lead = expert_chunk(
            moe_in, full_cot, mask, w_gate, w_up, wd_flat, router, None, first=0, pairs=1, parts=n_dp
        )
    scale_two = rms_scale(residual)

    chunks = (1, 3, 4)
    dots = None
    reduced = []
    carried = None
    first = 0
    for count in chunks:
        res = lead if first == 0 else expert_chunk(
            moe_in, full_cot, gates, w_gate, w_up, wd_flat, router, carried,
            first=first, pairs=count, parts=n_dp,
        )
        dgu, ga, wcat, dot_c, grads = res[:5]
        if first == 0:
            xt, gates, router_probs = res[5:]
        if len(reduced) == 2:
            reduced[0], dgu = lax.optimization_barrier((reduced[0], dgu))
        carried = (xt, dgu, ga, wcat)
        dots = dot_c if dots is None else dots + dot_c
        reduced.append(lax.psum_scatter(grads, "dp", scatter_dimension=0, tiled=False))
        first += count
    moe_back = matmul_scatter(dgu, wcat, n_tensor, 2, True, "moe_back")

    own_dots = jnp.sum(
        lax.all_to_all(dots.reshape(n_tensor, own_rows, experts), "tensor", 0, 0), axis=0
    )
    own_mask = lax.dynamic_slice_in_dim(mask, rank_start, own_rows, 0)
    own_probs = lax.dynamic_slice_in_dim(router_probs, rank_start, own_rows, 0)
    prob_grads = own_dots * own_mask
    own_logit = (
        own_probs * (prob_grads - jnp.sum(own_probs * prob_grads, axis=1, keepdims=True))
    ).astype(BF)
    router_grad = dot_tn(own_logit, own_moe_in)
    moe_grad = moe_back + dot_nt(own_logit, router)

    unit_two = residual * scale_two
    moe_gain_grad = jnp.sum(moe_grad * unit_two, axis=0)
    scaled_two = moe_grad * moe_gain
    residual_grad = cotangent.astype(F32) + scale_two * (
        scaled_two - unit_two * jnp.mean(scaled_two * unit_two, axis=1, keepdims=True)
    )
    residual_low = gather_all(residual_grad.astype(BF), n_tensor, 3, "gather_residual")
    output_grad = dot_tn(residual_low, attn_low).astype(BF)
    heads_grad = dot_nt(residual_low, w_output).astype(BF)

    dq_rot, dk_rot, dv = attn_bwd(
        lo_block, queries, keys_rot, value_low, heads_grad, attended, lse, seg_col, seg_rows, block
    )
    reduced[1], dq_rot = lax.optimization_barrier((reduced[1], dq_rot))
    query_norm_grad = dq_rot * cos_all - half_swap(dq_rot) * sin_all
    key_norm_grad = dk_rot * cos_all - half_swap(dk_rot) * sin_all
    query_gain_grad = jnp.sum(query_norm_grad * query_unit, axis=0)
    key_gain_grad = jnp.sum(key_norm_grad * key_unit, axis=0)
    query_scaled = query_norm_grad * query_gain
    key_scaled = key_norm_grad * key_gain
    inner = jnp.stack(
        [jnp.sum(query_scaled * query_unit, axis=1), jnp.sum(key_scaled * key_unit, axis=1)]
    )
    inner = sum_all(inner, "tensor", n_tensor) / model_width
    query_grad_low = (query_rs * (query_scaled - query_unit * inner[0][:, None])).astype(BF)
    key_grad_low = (key_rs * (key_scaled - key_unit * inner[1][:, None])).astype(BF)
    qkv_grad = jnp.concatenate([query_grad_low, key_grad_low, dv.astype(BF)], axis=1)
    qkv_w_grad = dot_tn(normed, qkv_grad).astype(BF)
    normed_grad = matmul_scatter(qkv_grad, w_qkv, n_tensor, 4, True, "normed_back")
    ga, qkv_w_grad = lax.optimization_barrier((ga, qkv_w_grad))
    moe_out = matmul_scatter(ga, wd_flat, n_tensor, 5, False, "moe_out")
    block_output = (residual + moe_out).astype(BF)
    scale_own = rms_scale(input_own)
    unit_one = input_own * scale_own
    attn_gain_grad = jnp.sum(normed_grad * unit_one, axis=0)
    scaled_one = normed_grad * attn_gain
    grad_input = residual_grad + scale_own * (
        scaled_one - unit_one * jnp.mean(scaled_one * unit_one, axis=1, keepdims=True)
    )

    proj_grad = jnp.concatenate([qkv_w_grad, output_grad], axis=1)
    reduced[2], proj_grad, block_output, grad_input = lax.optimization_barrier(
        (reduced[2], proj_grad, block_output, grad_input)
    )
    qkv_red = lax.psum_scatter(proj_grad, "dp", scatter_dimension=0, tiled=True)
    wo_red = qkv_red[:, 3 * local_cols :].T.astype(F32)
    gains = jnp.concatenate(
        [
            router_grad,
            moe_gain_grad[None, :],
            attn_gain_grad[None, :],
            lax.dynamic_update_slice_in_dim(
                jnp.zeros((1, model_width), F32), query_gain_grad[None, :], col_start, 1
            ),
            lax.dynamic_update_slice_in_dim(
                jnp.zeros((1, model_width), F32), key_gain_grad[None, :], col_start, 1
            ),
        ],
        axis=0,
    )
    gains = sum_everywhere(gains, n_tensor, n_dp)

    ds = model_width // n_dp
    gate_out, up_out, down_out = [], [], []
    for r, count in zip(reduced, chunks):
        r = r.reshape(2 * count, 3, ds, hid)
        gate_out.append(r[:, 0])
        up_out.append(r[:, 1])
        down = r[:, 2].reshape(2 * count, ds // hid, hid, hid)
        down_out.append(down.transpose(0, 2, 1, 3).reshape(2 * count, hid, ds))
    grad_gate = jnp.concatenate(gate_out, axis=0).astype(F32)
    grad_up = jnp.concatenate(up_out, axis=0).astype(F32)
    grad_down = jnp.concatenate(down_out, axis=0).astype(F32)
    return (
        block_output,
        grad_input,
        qkv_red[:, :local_cols].astype(F32),
        qkv_red[:, local_cols : 2 * local_cols].astype(F32),
        qkv_red[:, 2 * local_cols : 3 * local_cols].astype(F32),
        wo_red,
        gains[experts + 1],
        gains[experts + 2],
        gains[experts + 3],
        gains[experts],
        gains[:experts].T,
        grad_gate,
        grad_up,
        grad_down,
    )


def solution(mesh):
    rows = P(("dp", "tensor"), None)
    cols = P(None, "tensor")
    wide = P(None, None, "tensor")
    placed = (
        rows, P("dp", None), P("dp", None), cols, cols, cols, P("tensor", None), P(), P("tensor"), P("tensor"),
        P(), P(), wide, wide, P(None, "tensor", None), rows,
    )
    outs = (
        rows, rows, P("dp", "tensor"), P("dp", "tensor"), P("dp", "tensor"), P("tensor", "dp"), P(), P(), P(), P(),
        P(), P(None, "dp", "tensor"), P(None, "dp", "tensor"), P(None, "tensor", "dp"),
    )
    return jax.shard_map(
        functools.partial(
            per_device, n_dp=mesh.shape["dp"], n_tensor=mesh.shape["tensor"]
        ),
        mesh=mesh,
        in_specs=placed,
        out_specs=outs,
        check_vma=False,
    )
```

```python
import functools
import math

import jax
import jax.numpy as jnp
from jax import lax
from jax.experimental import pallas as pl
from jax.experimental.pallas import tpu as pltpu
from jax.sharding import PartitionSpec as P

HEAD_DIM = 128
EPS = 1e-05
NEG = -1e30
MIB = 1 << 20
BF = jnp.bfloat16
F32 = jnp.float32


def rms_scale(values):
    return lax.rsqrt(jnp.mean(values * values, axis=-1, keepdims=True) + EPS)


def dot_nn(a, b):
    return lax.dot_general(a, b, (((1,), (0,)), ((), ())), preferred_element_type=F32)


def dot_nt(a, b):
    return lax.dot_general(a, b, (((1,), (1,)), ((), ())), preferred_element_type=F32)


def dot_tn(a, b):
    return lax.dot_general(a, b, (((0,), (0,)), ((), ())), preferred_element_type=F32)


def partner(me, bit):
    return me + bit * (1 - 2 * ((me // bit) % 2))


def remote(src, dst, send_sem, recv_sem, target):
    return pltpu.make_async_remote_copy(
        src_ref=src,
        dst_ref=dst,
        send_sem=send_sem,
        recv_sem=recv_sem,
        device_id={"tensor": target},
        device_id_type=pl.DeviceIdType.MESH,
    )


def greet(targets):
    barrier = pltpu.get_barrier_semaphore()
    for t in targets:
        pl.semaphore_signal(
            barrier, inc=1, device_id={"tensor": t}, device_id_type=pl.DeviceIdType.MESH
        )
    pl.semaphore_wait(barrier, len(targets))


def attn_fwd_body(
    q_ref, k_ref, v_ref, sq_ref, sk_ref, o_ref, low_ref, lse_ref, own_ref, buf, send_sem, recv_sem, here_sem,
    *, block, heads, reach, size
):
    qb = pl.program_id(0)
    me = lax.axis_index("tensor")
    scale = 1.0 / math.sqrt(HEAD_DIM)
    cols_all = heads * HEAD_DIM

    @pl.when(qb == 0)
    def _():
        greet([lax.rem(me + t, size) for t in range(1, size)])

    seg_q = sq_ref[...]
    row = qb * block + lax.broadcasted_iota(jnp.int32, (block, block), 0)
    col0 = lax.broadcasted_iota(jnp.int32, (block, block), 1)
    qs = [q_ref[:, h * HEAD_DIM : (h + 1) * HEAD_DIM] for h in range(heads)]

    def step(kb, carry):
        rows = pl.ds(pl.multiple_of(kb * block, block), block)
        allowed = (seg_q == sk_ref[kb]) & (kb * block + col0 <= row)
        out = []
        for h in range(heads):
            m, l, acc = carry[h]
            cols = slice(h * HEAD_DIM, (h + 1) * HEAD_DIM)
            s = jnp.where(allowed, dot_nt(qs[h], k_ref[rows, cols]) * scale, NEG)
            m_new = jnp.maximum(m, jnp.max(s, axis=1, keepdims=True))
            p = jnp.exp(s - m_new)
            alpha = jnp.exp(m - m_new)
            l = alpha * l + jnp.sum(p, axis=1, keepdims=True)
            acc = alpha * acc + dot_nn(p.astype(BF), v_ref[rows, cols])
            out.append((m_new, l, acc))
        return tuple(out)

    init = tuple(
        (
            jnp.full((block, 1), NEG, F32),
            jnp.zeros((block, 1), F32),
            jnp.zeros((block, HEAD_DIM), F32),
        )
        for _ in range(heads)
    )
    final = lax.fori_loop(jnp.maximum(qb - reach, 0), qb + 1, step, init)
    for h in range(heads):
        m, l, acc = final[h]
        cols = slice(h * HEAD_DIM, (h + 1) * HEAD_DIM)
        out = acc / l
        o_ref[:, cols] = out
        low_ref[:, cols] = out.astype(BF)
        buf[qb, :, cols] = out.astype(BF)
        lse_ref[:, h : h + 1] = m + jnp.log(l)

    own = own_ref.shape[0]
    per = block // own

    def rows_of(dev):
        return buf.at[dev // per, pl.ds(pl.multiple_of((dev % per) * own, own), own)]

    def land(src):
        return own_ref.at[:, pl.ds(pl.multiple_of(src * cols_all, HEAD_DIM), cols_all)]

    def send(t):
        return remote(rows_of(t), land(me), send_sem.at[t], recv_sem.at[me], t)

    for j in range(per):
        dest = qb * per + j

        @pl.when(dest != me)
        def _():
            send(dest).start()

        @pl.when(dest == me)
        def _():
            pltpu.make_async_copy(rows_of(me), land(me), here_sem).start()

    @pl.when(qb == pl.num_programs(0) - 1)
    def _():
        pltpu.make_async_copy(rows_of(me), land(me), here_sem).wait()
        for t in range(1, size):
            other = lax.rem(me + t, size)
            send(other).wait_send()
            remote(
                rows_of(other), land(other), send_sem.at[other], recv_sem.at[other], other
            ).wait_recv()


def attn_fwd(q, k, v, seg_col, seg_rows, block, reach, size, cid):
    tokens, cols = q.shape
    heads = cols // HEAD_DIM
    nb = tokens // block
    full = lambda shape: pl.BlockSpec(shape, lambda i: (0,) * len(shape))
    rowed = lambda c: pl.BlockSpec((block, c), lambda i: (i, 0))
    return pl.pallas_call(
        functools.partial(attn_fwd_body, block=block, heads=heads, reach=reach, size=size),
        out_shape=(
            jax.ShapeDtypeStruct((tokens, cols), F32),
            jax.ShapeDtypeStruct((tokens, cols), BF),
            jax.ShapeDtypeStruct((tokens, heads), F32),
            jax.ShapeDtypeStruct((tokens // size, cols * size), BF),
        ),
        grid=(nb,),
        in_specs=[
            rowed(cols),
            full((tokens, cols)),
            full((tokens, cols)),
            rowed(1),
            full((nb, 1, block)),
        ],
        out_specs=[rowed(cols), rowed(cols), rowed(heads), pl.BlockSpec(memory_space=pl.ANY)],
        scratch_shapes=[
            pltpu.VMEM((nb, block, cols), BF),
            pltpu.SemaphoreType.DMA((size,)),
            pltpu.SemaphoreType.DMA((size,)),
            pltpu.SemaphoreType.DMA,
        ],
        compiler_params=pltpu.CompilerParams(
            vmem_limit_bytes=32 * MIB, collective_id=cid, has_side_effects=True
        ),
        cost_estimate=pl.CostEstimate(
            flops=10**8, bytes_accessed=4 * MIB, transcendentals=10**5
        ),
        name="attn_fwd",
    )(q, k, v, seg_col, seg_rows)


def attn_bwd_body(
    lo_ref, q_ref, k_ref, v_ref, do_ref, o_ref, lse_ref, sq_ref, sk_ref, dq_ref, dk_ref, dv_ref, *, block, heads
):
    qb = pl.program_id(0)
    scale = 1.0 / math.sqrt(HEAD_DIM)

    @pl.when(qb == 0)
    def _():
        dk_ref[...] = jnp.zeros_like(dk_ref)
        dv_ref[...] = jnp.zeros_like(dv_ref)

    seg_q = sq_ref[...]
    row = qb * block + lax.broadcasted_iota(jnp.int32, (block, block), 0)
    col0 = lax.broadcasted_iota(jnp.int32, (block, block), 1)
    hc = [slice(h * HEAD_DIM, (h + 1) * HEAD_DIM) for h in range(heads)]
    qs = [q_ref[:, c] for c in hc]
    dos = [do_ref[:, c] for c in hc]
    lse = [lse_ref[:, h : h + 1] for h in range(heads)]
    dsum = [
        jnp.sum(dos[h].astype(F32) * o_ref[:, hc[h]], axis=1, keepdims=True) for h in range(heads)
    ]

    def step(kb, carry):
        rows = pl.ds(pl.multiple_of(kb * block, block), block)
        allowed = (seg_q == sk_ref[kb]) & (kb * block + col0 <= row)
        out = []
        for h in range(heads):
            k_blk = k_ref[rows, hc[h]]
            s = jnp.where(allowed, dot_nt(qs[h], k_blk) * scale, NEG)
            p = jnp.exp(s - lse[h])
            dp = dot_nt(dos[h], v_ref[rows, hc[h]])
            ds = (p * (dp - dsum[h])).astype(BF)
            dv_ref[rows, hc[h]] += dot_tn(p.astype(BF), dos[h])
            dk_ref[rows, hc[h]] += dot_tn(ds, qs[h]) * scale
            out.append(carry[h] + dot_nn(ds, k_blk))
        return tuple(out)

    init = tuple(jnp.zeros((block, HEAD_DIM), F32) for _ in range(heads))
    final = lax.fori_loop(lo_ref[qb], qb + 1, step, init)
    for h in range(heads):
        dq_ref[:, hc[h]] = final[h] * scale


def attn_bwd(lo, q, k, v, do, o, lse, seg_col, seg_rows, block):
    tokens, cols = q.shape
    heads = cols // HEAD_DIM
    nb = tokens // block
    full = lambda shape: pl.BlockSpec(shape, lambda i, lo: (0,) * len(shape))
    rowed = lambda c: pl.BlockSpec((block, c), lambda i, lo: (i, 0))
    return pl.pallas_call(
        functools.partial(attn_bwd_body, block=block, heads=heads),
        out_shape=tuple(jax.ShapeDtypeStruct((tokens, cols), F32) for _ in range(3)),
        grid_spec=pltpu.PrefetchScalarGridSpec(
            num_scalar_prefetch=1,
            grid=(nb,),
            in_specs=[
                rowed(cols),
                full((tokens, cols)),
                full((tokens, cols)),
                rowed(cols),
                rowed(cols),
                rowed(heads),
                rowed(1),
                full((nb, 1, block)),
            ],
            out_specs=[rowed(cols), full((tokens, cols)), full((tokens, cols))],
        ),
        compiler_params=pltpu.CompilerParams(vmem_limit_bytes=40 * MIB),
        cost_estimate=pl.CostEstimate(
            flops=10**8, bytes_accessed=4 * MIB, transcendentals=10**5
        ),
        name="attn_bwd",
    )(lo, q, k, v, do, o, lse, seg_col, seg_rows)


def expert_body(*refs, first, rows_blk, parts):
    lead = first == 0
    if lead:
        x_hbm, g_hbm, mask_ref, wg_ref, wu_ref, wd_ref, router_ref = refs[:7]
        dgu_ref, ga_ref, wcat, dots_ref, grads_ref, xt_hbm, gates_ref, probs_ref = refs[7:15]
        x_v, xt_v, g_v, sem_x, sem_t, sem_g = refs[15:]
    else:
        x_hbm, g_hbm, gates_ref, wg_ref, wu_ref, wd_ref, xt_hbm = refs[:7]
        dgu_ref, ga_ref, wcat, dots_ref, grads_ref = refs[10:15]
        x_v, xt_v, g_v, sem_x, sem_t, sem_g = refs[15:]
    p = pl.program_id(0)
    tokens, width = x_v.shape
    nblk = tokens // rows_blk
    hid = wg_ref.shape[2]
    experts = gates_ref.shape[1]
    ds = width // parts

    if lead:
        t_copy = pltpu.make_async_copy(xt_v, xt_hbm, sem_t)
    else:
        t_copy = pltpu.make_async_copy(xt_hbm, xt_v, sem_t)

    def copies(i):
        r = pl.ds(i * rows_blk, rows_blk)
        return (
            pltpu.make_async_copy(x_hbm.at[r], x_v.at[r], sem_x.at[i]),
            pltpu.make_async_copy(g_hbm.at[r], g_v.at[r], sem_g.at[i]),
        )

    @pl.when(p == 0)
    def _():
        for i in range(nblk):
            for c in copies(i):
                c.start()
        if not lead:
            t_copy.start()
        dots_ref[...] = jnp.zeros_like(dots_ref)

    wcat[:, 0:hid] = wg_ref[0]
    wcat[:, hid : 2 * hid] = wg_ref[1]
    wcat[:, 2 * hid : 3 * hid] = wu_ref[0]
    wcat[:, 3 * hid : 4 * hid] = wu_ref[1]
    lane = lax.broadcasted_iota(jnp.int32, (rows_blk, experts), 1)
    e0 = 2 * (first + p)

    def block(i, _):
        start = pl.multiple_of(i * rows_blk, rows_blk)
        r = pl.ds(start, rows_blk)

        @pl.when(p == 0)
        def _():
            for c in copies(i):
                c.wait()

        if lead:
            xt_v[:, r] = x_v[r, :].T
            logits = dot_nn(x_v[r, :], router_ref[...])
            grown = jnp.exp(logits - jnp.max(logits, axis=1, keepdims=True))
            probs = grown / jnp.sum(grown, axis=1, keepdims=True)
            probs_ref[r, :] = probs
            gates_ref[r, :] = probs * mask_ref[r, :]
        gu = dot_nn(x_v[r, :], wcat[...])
        q = dot_nt(g_v[r, :], wd_ref[...])
        gate_rows = gates_ref[r, :]
        dots = dots_ref[r, :]
        for j in range(2):
            pre = gu[:, j * hid : (j + 1) * hid]
            up = gu[:, (2 + j) * hid : (3 + j) * hid]
            back = q[:, j * hid : (j + 1) * hid]
            here = lane == e0 + j
            gate = jnp.sum(jnp.where(here, gate_rows, 0.0), axis=1, keepdims=True)
            sig = jax.nn.sigmoid(pre)
            silu = pre * sig
            act = silu * up
            dot = jnp.sum(act * back, axis=1, keepdims=True)
            dots = dots + jnp.where(here, dot, 0.0)
            scaled = gate * back
            d_up = scaled * silu
            d_gate = scaled * up * (sig + silu * (1.0 - sig))
            dgu_ref[r, j * hid : (j + 1) * hid] = d_gate.astype(BF)
            dgu_ref[r, (2 + j) * hid : (3 + j) * hid] = d_up.astype(BF)
            ga_ref[r, j * hid : (j + 1) * hid] = (gate * act).astype(BF)
        dots_ref[r, :] = dots
        return 0

    lax.fori_loop(0, nblk, block, 0)

    @pl.when(p == 0)
    def _():
        if lead:
            t_copy.start()
        else:
            t_copy.wait()

    for s in range(parts):
        gd = dot_tn(ga_ref[...], g_v[:, s * ds : (s + 1) * ds]).astype(BF)
        gw = dot_nn(xt_v[s * ds : (s + 1) * ds, :], dgu_ref[...]).astype(BF)
        for j in range(2):
            grads_ref[s, 3 * j] = gw[:, j * hid : (j + 1) * hid]
            grads_ref[s, 3 * j + 1] = gw[:, (2 + j) * hid : (3 + j) * hid]
            for c in range(ds // hid):
                grads_ref[s, 3 * j + 2, c * hid : (c + 1) * hid, :] = gd[
                    j * hid : (j + 1) * hid, c * hid : (c + 1) * hid
                ]

    if lead:

        @pl.when(p == 0)
        def _():
            t_copy.wait()


def expert_chunk(x, g, gates, wg, wu, wd, router, carried, *, first, pairs, parts):
    tokens, width = x.shape
    experts, _, hid = wg.shape
    total = experts // 2
    rows_blk = 512
    nblk = tokens // rows_blk
    ds = width // parts
    lead = first == 0
    assert not lead or pairs == 1
    any_spec = pl.BlockSpec(memory_space=pl.ANY)
    colblk = lambda rows, c: pl.BlockSpec((rows, c), lambda p: (0, first + p))
    in_specs = [
        any_spec,
        any_spec,
        pl.BlockSpec((tokens, experts), lambda p: (0, 0)),
        pl.BlockSpec((2, width, hid), lambda p: (first + p, 0, 0)),
        pl.BlockSpec((2, width, hid), lambda p: (first + p, 0, 0)),
        pl.BlockSpec((2 * hid, width), lambda p: (first + p, 0)),
    ]
    out_shape = [
        jax.ShapeDtypeStruct((tokens, total * 4 * hid), BF),
        jax.ShapeDtypeStruct((tokens, total * 2 * hid), BF),
        jax.ShapeDtypeStruct((width, total * 4 * hid), BF),
        jax.ShapeDtypeStruct((tokens, experts), F32),
        jax.ShapeDtypeStruct((parts, pairs * 6, ds, hid), BF),
    ]
    out_specs = [
        colblk(tokens, 4 * hid),
        colblk(tokens, 2 * hid),
        colblk(width, 4 * hid),
        pl.BlockSpec((tokens, experts), lambda p: (0, 0)),
        pl.BlockSpec((parts, 6, ds, hid), lambda p: (0, p, 0, 0)),
    ]
    args = [x, g, gates, wg, wu, wd]
    alias = {}
    if lead:
        args.append(router)
        in_specs.append(pl.BlockSpec(router.shape, lambda p: (0, 0)))
        narrow = jax.ShapeDtypeStruct((tokens, experts), F32)
        out_shape += [jax.ShapeDtypeStruct((width, tokens), BF), narrow, narrow]
        out_specs += [any_spec] + [pl.BlockSpec((tokens, experts), lambda p: (0, 0))] * 2
    else:
        xt, dgu, ga, wcat = carried
        args += [xt, dgu, ga, wcat]
        in_specs += [any_spec] * 4
        alias = {7: 0, 8: 1, 9: 2}
    return pl.pallas_call(
        functools.partial(expert_body, first=first, rows_blk=rows_blk, parts=parts),
        out_shape=tuple(out_shape),
        grid=(pairs,),
        in_specs=in_specs,
        out_specs=out_specs,
        scratch_shapes=[
            pltpu.VMEM((tokens, width), BF),
            pltpu.VMEM((width, tokens), BF),
            pltpu.VMEM((tokens, width), BF),
            pltpu.SemaphoreType.DMA((nblk,)),
            pltpu.SemaphoreType.DMA,
            pltpu.SemaphoreType.DMA((nblk,)),
        ],
        input_output_aliases=alias,
        compiler_params=pltpu.CompilerParams(vmem_limit_bytes=61 * MIB),
        cost_estimate=pl.CostEstimate(
            flops=10**9, bytes_accessed=4 * MIB, transcendentals=10**5
        ),
        name="expert_chunk",
    )(*args)


GATHER_COPIES = 13


def gather_plan(x_hbm, land, me, own, send_sem, recv_sem):
    half = own // 2
    pc, px, py = (partner(me, b) for b in (1, 2, 4))
    diag = partner(px, 4)

    def piece(dev, a, n):
        return land.at[pl.ds(pl.multiple_of(dev * own + a, half), n)]

    plan = [
        (me, 0, half, px),
        (me, half, half, py),
        (me, half, half, px),
        (me, 0, half, py),
        (me, 0, own, pc),
        (px, 0, half, py),
        (py, half, half, px),
        (px, 0, half, pc),
        (py, half, half, pc),
        (px, half, half, pc),
        (py, 0, half, pc),
        (diag, 0, half, pc),
        (diag, half, half, pc),
    ]
    origin = {0: px, 1: py, 2: px, 3: py, 4: pc, 5: diag, 6: diag}

    def copy(k):
        dev, a, n, target = plan[k]
        src = x_hbm.at[pl.ds(a, n)] if k < 5 else piece(dev, a, n)
        return remote(src, piece(dev, a, n), send_sem.at[k], recv_sem.at[k], target)

    def arrived(k):
        dev, a, n, target = plan[k]
        src = origin[k] if k in origin else partner(dev, 1)
        return remote(piece(src, a, n), piece(src, a, n), send_sem.at[k], recv_sem.at[k], target)

    return copy, arrived, pc, px, py, diag


def front_body(
    x_hbm, wo_hbm, g_hbm, wq_hbm, wk_hbm, wv_hbm, gain_ref, qg_ref, kg_ref, mg_ref, routes_ref, sk_ref,
    normed_hbm, *rest, size, block, reach, capacity
):
    outs, rest = rest[:14], rest[14:]
    g_all, rest = rest[0], rest[1:]
    local, rest = rest[:14], rest[14:]
    (
        q_ref, k_ref, v_ref, qu_ref, ku_ref, rs_ref, cos_ref, sin_ref, o_ref, low_ref, lse_ref, res_ref, moe_ref,
        mask_ref,
    ) = local
    (
        x_v, n_v, w_v, wo_all, own_ref, sums, sums_all, place_v,
        send_sem, recv_sem, wo_send, wo_recv, g_send, g_recv, ss_send, ss_recv, a_send, a_recv,
        w_sem, x_sem, wo_sem, g_sem, a_sem, n_sem, o_sem,
    ) = rest

    def written(i):
        return pltpu.make_async_copy(local[i], outs[i], o_sem.at[i])

    me = lax.axis_index("tensor")
    own = x_hbm.shape[0]
    width = x_hbm.shape[1]
    cols = q_ref.shape[1]
    heads = cols // HEAD_DIM
    half_dim = HEAD_DIM // 2
    weights = [
        pltpu.make_async_copy(w, w_v.at[:, pl.ds(i * cols, cols)], w_sem.at[i])
        for i, w in enumerate((wq_hbm, wk_hbm, wv_hbm))
    ]
    mine = pl.ds(pl.multiple_of(me * own, own), own)
    here = pltpu.make_async_copy(x_hbm, x_v.at[mine], x_sem)
    here.start()
    for w in weights:
        w.start()
    greet([lax.rem(me + t, size) for t in range(1, size)])
    copy, arrived, pc, px, py, diag = gather_plan(x_hbm, x_v, me, own, send_sem, recv_sem)
    wo_copy, wo_arrived = gather_plan(wo_hbm, wo_all, me, own, wo_send, wo_recv)[:2]
    for k in range(5):
        copy(k).start()
    g_copy, g_arrived = gather_plan(g_hbm, g_all, me, own, g_send, g_recv)[:2]
    wo_here = pltpu.make_async_copy(wo_hbm, wo_all.at[mine], wo_sem)
    wo_here.start()
    g_here = pltpu.make_async_copy(g_hbm, g_all.at[mine], g_sem)
    g_here.start()

    lane = lax.broadcasted_iota(jnp.int32, (own, HEAD_DIM), 1)
    power = (lane % half_dim).astype(F32) * (-2.0 * math.log(10000.0) / HEAD_DIM)
    frequency = jnp.exp(power)

    seg = jnp.concatenate([sk_ref[i] for i in range(size)], axis=0)
    first_token = jnp.zeros(seg.shape, F32)
    for value in range(1, 16):
        count = jnp.sum(jnp.where(seg < value, 1.0, 0.0))
        first_token = jnp.where(seg == value, count, first_token)
    index = lax.broadcasted_iota(jnp.int32, seg.shape, 0) * block + lax.broadcasted_iota(
        jnp.int32, seg.shape, 1
    )
    place = index.astype(F32) - first_token
    for i in range(size):
        place_v[i] = place[i : i + 1]

    def column(row):
        return jnp.broadcast_to(row, (HEAD_DIM, block)).T

    def table(i, _):
        r = pl.ds(pl.multiple_of(i * own, own), own)
        angle = column(place_v[i]) * frequency
        cos_ref[r, :] = jnp.cos(angle)
        sine = jnp.sin(angle)
        sin_ref[r, :] = jnp.where(lane < half_dim, -sine, sine)
        return 0

    lax.fori_loop(0, size, table, 0)

    experts = mask_ref.shape[1]
    expert = lax.broadcasted_iota(jnp.int32, (experts, block), 0)
    earlier = (
        lax.broadcasted_iota(jnp.int32, (block, block), 0)
        < lax.broadcasted_iota(jnp.int32, (block, block), 1)
    )
    earlier = jnp.where(earlier, 1.0, 0.0).astype(BF)
    before = jnp.zeros((experts, 1), F32)
    fill = jnp.zeros((HEAD_DIM - experts, block), F32)
    for i in range(size):
        chosen = routes_ref[:, i * block : (i + 1) * block]
        routed = jnp.zeros((experts, block), F32)
        for k in range(chosen.shape[0]):
            routed = routed + jnp.where(chosen[k : k + 1] == expert, 1.0, 0.0)
        taken = dot_nn(routed.astype(BF), earlier) + before
        before = before + jnp.sum(routed, axis=1, keepdims=True)
        kept = jnp.where(taken < capacity, routed, 0.0)
        mask_ref[i * block : (i + 1) * block, :] = jnp.concatenate([kept, fill], axis=0).T[:, :experts]
    for i in (6, 7, 13):
        written(i).start()

    def stored(dev):
        r = pl.ds(pl.multiple_of(dev * own, own), own)
        return pltpu.make_async_copy(n_v.at[r], normed_hbm.at[r], n_sem.at[dev])

    def process(dev):
        r = pl.ds(pl.multiple_of(dev * own, own), own)
        wide = x_v[r, :].astype(F32)
        scale = lax.rsqrt(jnp.mean(wide * wide, axis=1, keepdims=True) + EPS)
        normed = (wide * scale * gain_ref[...]).astype(BF)
        n_v[r, :] = normed
        stored(dev).start()
        res = dot_nn(normed, w_v[...])
        q = res[:, :cols]
        k = res[:, cols : 2 * cols]
        qu_ref[r, :] = q
        ku_ref[r, :] = k
        v_ref[r, :] = res[:, 2 * cols :].astype(BF)
        pair = jnp.where(
            lane == 0,
            jnp.sum(q * q, axis=1, keepdims=True),
            jnp.sum(k * k, axis=1, keepdims=True),
        )
        sums[dev] = pair.T[0:2, :]

    here.wait()
    for w in weights:
        w.wait()
    process(me)
    arrived(4).wait_recv()
    process(pc)
    arrived(0).wait_recv()
    copy(5).start()
    copy(7).start()
    arrived(1).wait_recv()
    copy(6).start()
    copy(8).start()
    arrived(2).wait_recv()
    copy(9).start()
    arrived(3).wait_recv()
    copy(10).start()
    for k in range(5):
        wo_copy(k).start()
    process(px)
    process(py)
    arrived(7).wait_recv()
    arrived(9).wait_recv()
    process(partner(px, 1))
    arrived(8).wait_recv()
    arrived(10).wait_recv()
    process(partner(py, 1))
    arrived(5).wait_recv()
    copy(11).start()
    arrived(6).wait_recv()
    copy(12).start()
    process(diag)
    arrived(11).wait_recv()
    arrived(12).wait_recv()
    process(partner(diag, 1))
    hand_on(wo_arrived, wo_copy, ((0, (5, 7)), (1, (6, 8))))

    def exchange(t, src):
        other = lax.rem(me + t, size)
        slot = me if src is None else other
        return remote(sums, sums_all.at[slot], ss_send.at[other], ss_recv.at[slot], other)

    for t in range(1, size):
        exchange(t, None).start()
    sums_all[me] = sums[...]
    hand_on(wo_arrived, wo_copy, ((2, (9,)), (3, (10,))))
    for k in range(5):
        g_copy(k).start()
    for t in range(1, size):
        exchange(t, 1).wait_recv()
    total = sums_all[0]
    for d in range(1, size):
        total = total + sums_all[d]
    rows_iota = lax.broadcasted_iota(jnp.int32, (HEAD_DIM, own), 0)
    for d in range(size):
        r = slice(d * own, (d + 1) * own)
        tot = total[d]
        both = jnp.where(rows_iota == 0, tot[0:1, :], tot[1:2, :])
        rs = lax.rsqrt(both / width + EPS).T
        rs_ref[r, :] = rs[:, 0:2]
        cos, sin = cos_ref[r, :], sin_ref[r, :]
        for j, (unit_ref, gain, dst) in enumerate(((qu_ref, qg_ref, q_ref), (ku_ref, kg_ref, k_ref))):
            unit = unit_ref[r, :] * rs[:, j : j + 1]
            unit_ref[r, :] = unit
            wide = unit * gain[...]
            for h in range(heads):
                c = slice(h * HEAD_DIM, (h + 1) * HEAD_DIM)
                w = wide[:, c]
                dst[r, c] = (w * cos + pltpu.roll(w, half_dim, 1) * sin).astype(BF)

    for i in range(6):
        written(i).start()
    score_scale = 1.0 / math.sqrt(HEAD_DIM)
    row0 = lax.broadcasted_iota(jnp.int32, (block, block), 0)
    col0 = lax.broadcasted_iota(jnp.int32, (block, block), 1)
    hc = [slice(h * HEAD_DIM, (h + 1) * HEAD_DIM) for h in range(heads)]

    def land(src):
        return own_ref.at[:, pl.ds(pl.multiple_of(src * cols, HEAD_DIM), cols)]

    def rows_of(dev):
        return low_ref.at[pl.ds(pl.multiple_of(dev * own, own), own)]

    def send(t):
        return remote(rows_of(t), land(me), a_send.at[t], a_recv.at[me], t)

    def query_block(qb, _):
        rq = pl.ds(pl.multiple_of(qb * block, block), block)
        seg_q = column(sk_ref[qb].astype(F32))[:, 0:1]
        qs = [q_ref[rq, c] for c in hc]

        def step(kb, carry):
            rows = pl.ds(pl.multiple_of(kb * block, block), block)
            allowed = (seg_q == sk_ref[kb].astype(F32)) & (kb * block + col0 <= qb * block + row0)
            out = []
            for h in range(heads):
                m, l, acc = carry[h]
                s = jnp.where(allowed, dot_nt(qs[h], k_ref[rows, hc[h]]) * score_scale, NEG)
                m_new = jnp.maximum(m, jnp.max(s, axis=1, keepdims=True))
                p = jnp.exp(s - m_new)
                alpha = jnp.exp(m - m_new)
                l = alpha * l + jnp.sum(p, axis=1, keepdims=True)
                acc = alpha * acc + dot_nn(p.astype(BF), v_ref[rows, hc[h]])
                out.append((m_new, l, acc))
            return tuple(out)

        init = tuple(
            (
                jnp.full((block, 1), NEG, F32),
                jnp.zeros((block, 1), F32),
                jnp.zeros((block, HEAD_DIM), F32),
            )
            for _ in range(heads)
        )
        final = lax.fori_loop(jnp.maximum(qb - reach, 0), qb + 1, step, init)
        for h in range(heads):
            m, l, acc = final[h]
            out = acc / l
            o_ref[rq, hc[h]] = out
            low_ref[rq, hc[h]] = out.astype(BF)
            lse_ref[rq, h : h + 1] = m + jnp.log(l)

        @pl.when(qb != me)
        def _():
            send(qb).start()

        @pl.when(qb == me)
        def _():
            pltpu.make_async_copy(rows_of(me), land(me), a_sem).start()

        @pl.when(qb == 3)
        def _():
            hand_on(wo_arrived, wo_copy, ((5, (11,)), (6, (12,))))

        @pl.when(qb == 5)
        def _():
            hand_on(g_arrived, g_copy, ((0, (5, 7)), (1, (6, 8))))

        return 0

    lax.fori_loop(0, size, query_block, 0)
    for i in (8, 9, 10):
        written(i).start()
    pltpu.make_async_copy(rows_of(me), land(me), a_sem).wait()
    for t in range(1, size):
        other = lax.rem(me + t, size)
        remote(rows_of(other), land(other), a_send.at[other], a_recv.at[other], other).wait_recv()
    for k in (4, 7, 8, 9, 10, 11, 12):
        wo_arrived(k).wait_recv()
    wo_here.wait()
    sl = width // 4
    total = jnp.zeros((own, 1), F32)
    for i in range(4):
        c = slice(i * sl, (i + 1) * sl)
        part = x_v[mine, c].astype(F32) + dot_nn(own_ref[...], wo_all[:, c])
        res_ref[:, c] = part
        total = total + jnp.sum(part * part, axis=1, keepdims=True)
    scale = lax.rsqrt(total / width + EPS)
    for i in range(4):
        c = slice(i * sl, (i + 1) * sl)
        moe_ref[:, c] = (res_ref[:, c] * scale * mg_ref[:, c]).astype(BF)
    for i in (11, 12):
        written(i).start()
    hand_on(g_arrived, g_copy, ((2, (9,)), (3, (10,)), (5, (11,)), (6, (12,))))
    for t in range(1, size):
        exchange(t, None).wait_send()
        send(lax.rem(me + t, size)).wait_send()
    for d in range(size):
        stored(d).wait()
    for k in (4, 7, 8, 9, 10, 11, 12):
        g_arrived(k).wait_recv()
    for k in range(GATHER_COPIES):
        copy(k).wait_send()
        wo_copy(k).wait_send()
        g_copy(k).wait_send()
    g_here.wait()
    for i in range(14):
        written(i).wait()


def hand_on(arrived, copy, steps):
    for k, following in steps:
        arrived(k).wait_recv()
        for f in following:
            copy(f).start()


def front(x, wo, g, wq, wk, wv, gain, qg, kg, mg, routes_t, seg_rows, experts, size, block, reach, capacity, cid):
    own, width = x.shape
    cols = wq.shape[1]
    tokens = own * size
    heads = cols // HEAD_DIM
    any_spec = pl.BlockSpec(memory_space=pl.ANY)
    vm = pl.BlockSpec(memory_space=pltpu.VMEM)
    arr = jax.ShapeDtypeStruct
    dma = pltpu.SemaphoreType.DMA
    kept = (
            arr((tokens, cols), BF),
            arr((tokens, cols), BF),
            arr((tokens, cols), BF),
            arr((tokens, cols), F32),
            arr((tokens, cols), F32),
            arr((tokens, 2), F32),
            arr((tokens, HEAD_DIM), F32),
            arr((tokens, HEAD_DIM), F32),
            arr((tokens, cols), F32),
            arr((tokens, cols), BF),
            arr((tokens, heads), F32),
            arr((own, width), F32),
            arr((own, width), BF),
            arr((tokens, experts), F32),
    )
    return pl.pallas_call(
        functools.partial(front_body, size=size, block=block, reach=reach, capacity=capacity),
        out_shape=(
            arr((tokens, width), BF),
            *kept,
            arr((tokens, width), BF),
        ),
        in_specs=[any_spec] * 6 + [vm] * 6,
        out_specs=[any_spec] * 16,
        scratch_shapes=[pltpu.VMEM(k.shape, k.dtype) for k in kept]
        + [
            pltpu.VMEM((tokens, width), BF),
            pltpu.VMEM((tokens, width), BF),
            pltpu.VMEM((width, 3 * cols), BF),
            pltpu.VMEM((width, width), BF),
            pltpu.VMEM((own, width), BF),
            pltpu.VMEM((size, 2, own), F32),
            pltpu.VMEM((size, size, 2, own), F32),
            pltpu.VMEM((size, 1, block), F32),
        ]
        + [dma((GATHER_COPIES,))] * 6
        + [dma((size,))] * 4
        + [
            dma((3,)),
            dma,
            dma,
            dma,
            dma,
            dma((size,)),
            dma((14,)),
        ],
        compiler_params=pltpu.CompilerParams(
            vmem_limit_bytes=58 * MIB, collective_id=cid, has_side_effects=True
        ),
        cost_estimate=pl.CostEstimate(flops=10**8, bytes_accessed=4 * MIB, transcendentals=0),
        name="front",
    )(x, wo, g, wq, wk, wv, gain[None, :], qg[None, :], kg[None, :], mg[None, :], routes_t, seg_rows)


def middle_body(
    own_hbm, g_hbm, mask_ref, router_ref, wg_ref, wu_ref, wd_ref,
    moe_hbm, dgu_hbm, ga_hbm, wcat_hbm, dots_ref, grads_ref, xt_hbm, gates_ref, probs_ref,
    x_v, xt_v, g_v, wcat, dgu_v, ga_v, send_sem, recv_sem, own_sem, g_sem, m_sem, out_sem, *, size, parts
):
    me = lax.axis_index("tensor")
    tokens, width = x_v.shape
    own = tokens // size
    hid = wg_ref.shape[2]
    experts = gates_ref.shape[1]
    ds = width // parts

    def g_copy(d):
        r = pl.ds(d * own, own)
        return pltpu.make_async_copy(g_hbm.at[r], g_v.at[r], g_sem.at[d])

    mine = pl.ds(pl.multiple_of(me * own, own), own)
    own_copy = pltpu.make_async_copy(own_hbm, x_v.at[mine], own_sem)
    own_copy.start()
    greet([partner(me, b) for b in (1, 2, 4)])
    copy, arrived, pc, px, py, diag = gather_plan(own_hbm, x_v, me, own, send_sem, recv_sem)
    for k in range(5):
        copy(k).start()
    for d in range(size):
        g_copy(d).start()

    wcat[:, 0:hid] = wg_ref[0]
    wcat[:, hid : 2 * hid] = wg_ref[1]
    wcat[:, 2 * hid : 3 * hid] = wu_ref[0]
    wcat[:, 3 * hid : 4 * hid] = wu_ref[1]
    wcat_out = pltpu.make_async_copy(wcat, wcat_hbm.at[:, pl.ds(0, 4 * hid)], out_sem.at[0])
    wcat_out.start()
    own_copy.wait()
    for d in range(size):
        g_copy(d).wait()
    lane = lax.broadcasted_iota(jnp.int32, (own, experts), 1)

    def moe_out(dev):
        r = pl.ds(pl.multiple_of(dev * own, own), own)
        return pltpu.make_async_copy(x_v.at[r], moe_hbm.at[r], m_sem.at[dev])

    def process(dev):
        r = pl.ds(pl.multiple_of(dev * own, own), own)
        moe_out(dev).start()
        xt_v[:, r] = x_v[r, :].T
        logits = dot_nt(x_v[r, :], router_ref[...])
        grown = jnp.exp(logits - jnp.max(logits, axis=1, keepdims=True))
        probs = grown / jnp.sum(grown, axis=1, keepdims=True)
        probs_ref[r, :] = probs
        gate_rows = probs * mask_ref[r, :]
        gates_ref[r, :] = gate_rows
        gu = dot_nn(x_v[r, :], wcat[...])
        q = dot_nt(g_v[r, :], wd_ref[...])
        dots = jnp.zeros((own, experts), F32)
        for j in range(2):
            pre = gu[:, j * hid : (j + 1) * hid]
            up = gu[:, (2 + j) * hid : (3 + j) * hid]
            back = q[:, j * hid : (j + 1) * hid]
            here = lane == j
            gate = jnp.sum(jnp.where(here, gate_rows, 0.0), axis=1, keepdims=True)
            sig = jax.nn.sigmoid(pre)
            silu = pre * sig
            act = silu * up
            dot = jnp.sum(act * back, axis=1, keepdims=True)
            dots = dots + jnp.where(here, dot, 0.0)
            scaled = gate * back
            d_up = scaled * silu
            d_gate = scaled * up * (sig + silu * (1.0 - sig))
            dgu_v[r, j * hid : (j + 1) * hid] = d_gate.astype(BF)
            dgu_v[r, (2 + j) * hid : (3 + j) * hid] = d_up.astype(BF)
            ga_v[r, j * hid : (j + 1) * hid] = (gate * act).astype(BF)
        dots_ref[r, :] = dots

    process(me)
    arrived(4).wait_recv()
    process(pc)
    arrived(0).wait_recv()
    copy(5).start()
    copy(7).start()
    arrived(1).wait_recv()
    copy(6).start()
    copy(8).start()
    arrived(2).wait_recv()
    copy(9).start()
    arrived(3).wait_recv()
    copy(10).start()
    process(px)
    process(py)
    arrived(7).wait_recv()
    arrived(9).wait_recv()
    process(partner(px, 1))
    arrived(8).wait_recv()
    arrived(10).wait_recv()
    process(partner(py, 1))
    arrived(5).wait_recv()
    copy(11).start()
    arrived(6).wait_recv()
    copy(12).start()
    process(diag)
    arrived(11).wait_recv()
    arrived(12).wait_recv()
    process(partner(diag, 1))

    outs = [
        pltpu.make_async_copy(dgu_v, dgu_hbm.at[:, pl.ds(0, 4 * hid)], out_sem.at[1]),
        pltpu.make_async_copy(ga_v, ga_hbm.at[:, pl.ds(0, 2 * hid)], out_sem.at[2]),
        pltpu.make_async_copy(xt_v, xt_hbm, out_sem.at[3]),
    ]
    for o in outs:
        o.start()
    for s in range(parts):
        gd = dot_tn(ga_v[...], g_v[:, s * ds : (s + 1) * ds]).astype(BF)
        gw = dot_nn(xt_v[s * ds : (s + 1) * ds, :], dgu_v[...]).astype(BF)
        for j in range(2):
            grads_ref[s, 3 * j] = gw[:, j * hid : (j + 1) * hid]
            grads_ref[s, 3 * j + 1] = gw[:, (2 + j) * hid : (3 + j) * hid]
            for c in range(ds // hid):
                grads_ref[s, 3 * j + 2, c * hid : (c + 1) * hid, :] = gd[
                    j * hid : (j + 1) * hid, c * hid : (c + 1) * hid
                ]
    wcat_out.wait()
    for o in outs:
        o.wait()
    for d in range(size):
        moe_out(d).wait()
    for k in range(GATHER_COPIES):
        copy(k).wait_send()


def middle(own_rows, g, mask, router, wg, wu, wd, size, parts, cid):
    own, width = own_rows.shape
    tokens = own * size
    experts, _, hid = wg.shape
    total = experts // 2
    ds = width // parts
    any_spec = pl.BlockSpec(memory_space=pl.ANY)
    vm = pl.BlockSpec(memory_space=pltpu.VMEM)
    first = lambda shape: pl.BlockSpec(shape, lambda i: (0,) * len(shape))
    arr = jax.ShapeDtypeStruct
    dma = pltpu.SemaphoreType.DMA
    narrow = arr((tokens, experts), F32)
    return pl.pallas_call(
        functools.partial(middle_body, size=size, parts=parts),
        out_shape=(
            arr((tokens, width), BF),
            arr((tokens, total * 4 * hid), BF),
            arr((tokens, total * 2 * hid), BF),
            arr((width, total * 4 * hid), BF),
            narrow,
            arr((parts, 6, ds, hid), BF),
            arr((width, tokens), BF),
            narrow,
            narrow,
        ),
        grid=(1,),
        in_specs=[
            any_spec,
            any_spec,
            first((tokens, experts)),
            first(router.shape),
            first((2, width, hid)),
            first((2, width, hid)),
            first((2 * hid, width)),
        ],
        out_specs=[
            any_spec,
            any_spec,
            any_spec,
            any_spec,
            first((tokens, experts)),
            first((parts, 6, ds, hid)),
            any_spec,
            first((tokens, experts)),
            first((tokens, experts)),
        ],
        scratch_shapes=[
            pltpu.VMEM((tokens, width), BF),
            pltpu.VMEM((width, tokens), BF),
            pltpu.VMEM((tokens, width), BF),
            pltpu.VMEM((width, 4 * hid), BF),
            pltpu.VMEM((tokens, 4 * hid), BF),
            pltpu.VMEM((tokens, 2 * hid), BF),
            dma((GATHER_COPIES,)),
            dma((GATHER_COPIES,)),
            dma,
            dma((size,)),
            dma((size,)),
            dma((4,)),
        ],
        compiler_params=pltpu.CompilerParams(
            vmem_limit_bytes=62 * MIB, collective_id=cid, has_side_effects=True
        ),
        cost_estimate=pl.CostEstimate(flops=10**9, bytes_accessed=4 * MIB, transcendentals=0),
        name="middle",
    )(own_rows, g, mask, router, wg, wu, wd)


def matmul_scatter_body(
    l_hbm, r_hbm, out_ref, l_v, r_v, part, got1, got2, got3, sem_l, sem_r, send_sem, recv_sem,
    *, size, slices, nt
):
    me = lax.axis_index("tensor")
    tokens = l_v.shape[0]
    own = tokens // size
    sn = out_ref.shape[1] // slices
    mine = [(me // b) % 2 for b in (1, 2, 4)]
    group = 2

    def l_copy(i):
        r = pl.ds(i * own * group, own * group)
        return pltpu.make_async_copy(l_hbm.at[r], l_v.at[r], sem_l.at[i])

    def r_copy(s):
        c = pl.ds(s * sn, sn)
        if nt:
            return pltpu.make_async_copy(r_hbm.at[c], r_v.at[c], sem_r.at[s])
        return pltpu.make_async_copy(r_hbm.at[:, c], r_v.at[:, c], sem_r.at[s])

    r_copy(0).start()
    for i in range(size // group):
        l_copy(i).start()
    for s in range(1, slices):
        r_copy(s).start()
    greet([partner(me, b) for b in (1, 2, 4)])

    def hop(s, stage):
        a, b = (1, 2) if s % 2 == 0 else (2, 1)
        if stage == 0:
            src, dst, bit = part.at[s, 1 - mine[0]], got1.at[s], 1
        elif stage == 1:
            src, dst, bit = part.at[s, mine[0], pl.ds(2 * (1 - mine[a]), 2)], got2.at[s], 1 << a
        else:
            src, dst, bit = part.at[s, mine[0], 2 * mine[a] + 1 - mine[b]], got3.at[s], 1 << b
        return remote(src, dst, send_sem.at[stage, s], recv_sem.at[stage, s], partner(me, bit))

    def compute(s):
        r_copy(s).wait()

        def rows(i, _):
            if s == 0:
                l_copy(i).wait()
            r = pl.ds(pl.multiple_of(i * own * group, own * group), own * group)
            if nt:
                res = dot_nt(l_v[r, :], r_v[s * sn : (s + 1) * sn, :])
            else:
                res = dot_nn(l_v[r, :], r_v[:, s * sn : (s + 1) * sn])
            res = res.astype(BF)
            x, y = i % 2, i // 2
            pos = 2 * x + y if s % 2 == 0 else 2 * y + x
            for c in range(2):
                part[s, c, pos] = res[c * own : (c + 1) * own]
            return 0

        lax.fori_loop(0, size // group, rows, 0)
        hop(s, 0).start()

    def first(s):
        hop(s, 0).wait_recv()
        part[s, mine[0]] = (part[s, mine[0]].astype(F32) + got1[s].astype(F32)).astype(BF)
        hop(s, 1).start()

    def second(s):
        a = 1 if s % 2 == 0 else 2
        hop(s, 1).wait_recv()
        ix = pl.ds(2 * mine[a], 2)
        part[s, mine[0], ix] = (part[s, mine[0], ix].astype(F32) + got2[s].astype(F32)).astype(BF)
        hop(s, 2).start()

    def third(s):
        a, b = (1, 2) if s % 2 == 0 else (2, 1)
        hop(s, 2).wait_recv()
        out_ref[:, s * sn : (s + 1) * sn] = part[s, mine[0], 2 * mine[a] + mine[b]].astype(
            F32
        ) + got3[s].astype(F32)

    for t in range(slices + 5):
        if t < slices:
            compute(t)
        if 0 <= t - 1 < slices:
            first(t - 1)
        if 0 <= t - 3 < slices:
            second(t - 3)
        if 0 <= t - 5 < slices:
            third(t - 5)
    for s in range(slices):
        for stage in range(3):
            hop(s, stage).wait_send()


def matmul_scatter(left, right, size, cid, nt, name):
    tokens, depth = left.shape
    width = right.shape[0] if nt else right.shape[1]
    own = tokens // size
    if size != 8:
        part = (dot_nt if nt else dot_nn)(left, right).astype(BF)
        return lax.psum_scatter(part, "tensor", scatter_dimension=0, tiled=True).astype(F32)
    slices = 8
    sn = width // slices
    any_spec = pl.BlockSpec(memory_space=pl.ANY)
    return pl.pallas_call(
        functools.partial(matmul_scatter_body, size=size, slices=slices, nt=nt),
        out_shape=jax.ShapeDtypeStruct((own, width), F32),
        in_specs=[any_spec, any_spec],
        out_specs=pl.BlockSpec(memory_space=pltpu.VMEM),
        scratch_shapes=[
            pltpu.VMEM(left.shape, BF),
            pltpu.VMEM(right.shape, BF),
            pltpu.VMEM((slices, 2, size // 2, own, sn), BF),
            pltpu.VMEM((slices, size // 2, own, sn), BF),
            pltpu.VMEM((slices, size // 4, own, sn), BF),
            pltpu.VMEM((slices, own, sn), BF),
            pltpu.SemaphoreType.DMA((size // 2,)),
            pltpu.SemaphoreType.DMA((slices,)),
            pltpu.SemaphoreType.DMA((3, slices)),
            pltpu.SemaphoreType.DMA((3, slices)),
        ],
        compiler_params=pltpu.CompilerParams(
            vmem_limit_bytes=60 * MIB, collective_id=cid, has_side_effects=True
        ),
        cost_estimate=pl.CostEstimate(
            flops=10**9, bytes_accessed=4 * MIB, transcendentals=0
        ),
        name=name,
    )(left, right)


def gather_body(x_ref, out_ref, send_sem, recv_sem, here_sem):
    me = lax.axis_index("tensor")
    own = x_ref.shape[0]
    greet([partner(me, b) for b in (1, 2, 4)])
    mine = pl.ds(pl.multiple_of(me * own, own), own)
    here = pltpu.make_async_copy(x_ref, out_ref.at[mine], here_sem)
    here.start()
    copy, arrived = gather_plan(x_ref, out_ref, me, own, send_sem, recv_sem)[:2]
    for k in range(5):
        copy(k).start()
    for k, following in ((0, (5, 7)), (1, (6, 8)), (2, (9,)), (3, (10,)), (5, (11,)), (6, (12,))):
        arrived(k).wait_recv()
        for f in following:
            copy(f).start()
    for k in (4, 7, 8, 9, 10, 11, 12):
        arrived(k).wait_recv()
    for k in range(GATHER_COPIES):
        copy(k).wait_send()
    here.wait()


def gather_all(value, size, cid, name):
    own, cols = value.shape
    if size != 8:
        return lax.all_gather(value, "tensor", axis=0, tiled=True)
    any_spec = pl.BlockSpec(memory_space=pl.ANY)
    return pl.pallas_call(
        gather_body,
        out_shape=jax.ShapeDtypeStruct((own * size, cols), value.dtype),
        in_specs=[any_spec],
        out_specs=any_spec,
        scratch_shapes=[
            pltpu.SemaphoreType.DMA((GATHER_COPIES,)),
            pltpu.SemaphoreType.DMA((GATHER_COPIES,)),
            pltpu.SemaphoreType.DMA,
        ],
        compiler_params=pltpu.CompilerParams(collective_id=cid, has_side_effects=True),
        cost_estimate=pl.CostEstimate(flops=0, bytes_accessed=4 * MIB, transcendentals=0),
        name=name,
    )(value)


def swap(value, axis, size, bit):
    return lax.ppermute(value, axis, [(i, i ^ bit) for i in range(size)])


def sum_all(value, axis, size):
    bit = 1
    while bit < size:
        value = value + swap(value, axis, size, bit)
        bit *= 2
    return value


def sum_everywhere(value, n_tensor, n_dp):
    me = lax.axis_index("tensor")
    bits = [1 << b for b in range(n_tensor.bit_length() - 1)]
    for bit in bits[::-1]:
        half = value.shape[1] // 2
        low, high = value[:, :half], value[:, half:]
        upper = (me // bit) % 2 == 1
        send = jnp.where(upper, low, high)
        value = jnp.where(upper, high, low) + swap(send, "tensor", n_tensor, bit)
    value = sum_all(value, "dp", n_dp)
    for bit in bits:
        got = swap(value, "tensor", n_tensor, bit)
        upper = (me // bit) % 2 == 1
        value = jnp.concatenate(
            [jnp.where(upper, got, value), jnp.where(upper, value, got)], axis=1
        )
    return value


def half_swap(values):
    pieces = []
    half = HEAD_DIM // 2
    for h in range(values.shape[1] // HEAD_DIM):
        base = h * HEAD_DIM
        pieces += [values[:, base + half : base + HEAD_DIM], values[:, base : base + half]]
    return jnp.concatenate(pieces, axis=1)


def document_blocks(segments, block):
    seg = segments.reshape(-1)
    tokens = seg.shape[0]
    values16 = jnp.arange(16, dtype=jnp.int32)
    below = jnp.sum((seg[None, :] < values16[:, None]).astype(jnp.int32), axis=1)
    doc_start = jnp.sum(
        jnp.where(seg[:, None] == values16[None, :], below[None, :], 0), axis=1
    )
    positions = jnp.arange(tokens, dtype=jnp.int32) - doc_start
    return (
        seg[:, None],
        seg.reshape(tokens // block, 1, block),
        doc_start[::block] // block,
        positions.astype(F32)[:, None],
    )


def routing_mask(routes, experts, capacity, block):
    tokens = routes.shape[0]
    expert_ids = jnp.arange(experts, dtype=jnp.int32)
    routed = jnp.sum(
        (routes[:, :, None] == expert_ids[None, None, :]).astype(F32), axis=1
    )
    tri = (
        jnp.arange(block, dtype=jnp.int32)[:, None] > jnp.arange(block, dtype=jnp.int32)[None, :]
    ).astype(BF)
    nb = tokens // block
    routed_b = routed.reshape(nb, block, experts)
    within = jnp.einsum("ij,bje->bie", tri, routed_b.astype(BF), preferred_element_type=F32)
    sums = jnp.sum(routed_b, axis=1)
    before = jnp.sum(
        jnp.where(
            (jnp.arange(nb)[:, None] > jnp.arange(nb)[None, :])[:, :, None], sums[None, :, :], 0.0
        ),
        axis=1,
    )
    place = within + before[:, None, :]
    return (routed_b * (place < capacity).astype(F32)).reshape(tokens, experts)


def per_device(
    block_input, segments, routes, w_query, w_key, w_value, w_output, attn_gain, query_gain, key_gain,
    moe_gain, router, w_gate, w_up, w_down, cotangent, *, n_dp, n_tensor
):
    own_rows, model_width = block_input.shape
    local_cols = w_query.shape[1]
    local_heads = local_cols // HEAD_DIM
    token_count = segments.shape[0] * segments.shape[1]
    experts = router.shape[1]
    top_count = routes.shape[1]
    hid = w_gate.shape[2]
    capacity = 5 * token_count * top_count // (4 * experts)
    me = lax.axis_index("tensor")
    rank_start = me * own_rows
    col_start = me * local_cols
    block = 256

    w_qkv = jnp.concatenate([w_query, w_key, w_value], axis=1)
    input_own = block_input.astype(F32)
    wd_flat = w_down.reshape(experts * hid, model_width)
    reach = min(1024 // block, token_count // block)
    if n_tensor == 8:
        (
            normed, queries, keys_rot, value_low, query_unit, key_unit, scales, cos_one, sin_one,
            attended, attn_low, lse, residual, own_moe_in, mask, full_cot,
        ) = front(
            block_input, w_output, cotangent, w_query, w_key, w_value, attn_gain, query_gain, key_gain, moe_gain,
            routes.T, segments.reshape(token_count // block, 1, block),
            experts, n_tensor, block, reach, capacity, 6,
        )
        segments, own_moe_in = lax.optimization_barrier((segments, own_moe_in))
        seg_col, seg_rows, lo_block = document_blocks(segments, block)[:3]
        query_rs, key_rs = scales[:, 0:1], scales[:, 1:2]
        cos_all = jnp.concatenate([cos_one] * local_heads, axis=1)
        sin_all = jnp.concatenate([sin_one] * local_heads, axis=1)
        lead = middle(
            own_moe_in, full_cot, mask, router.T, w_gate, w_up, wd_flat, n_tensor, n_dp, 1
        )
        moe_in, lead = lead[0], lead[1:]
    else:
        seg_col, seg_rows, lo_block, pos_col = document_blocks(segments, block)
        mask = routing_mask(routes, experts, capacity, block)
        half = HEAD_DIM // 2
        frequency = jnp.exp(
            jnp.arange(half, dtype=F32) * (-2.0 * math.log(10000.0) / HEAD_DIM)
        )
        angles = pos_col * frequency[None, :]
        cosine, sine = jnp.cos(angles), jnp.sin(angles)
        cos_all = jnp.concatenate([cosine] * (2 * local_heads), axis=1)
        sin_all = jnp.concatenate([-sine, sine] * local_heads, axis=1)
        full_cot = lax.all_gather(cotangent, "tensor", axis=0, tiled=True)
        full_wo = lax.all_gather(w_output, "tensor", axis=0, tiled=True)
        input_wide = lax.all_gather(block_input, "tensor", axis=0, tiled=True).astype(F32)
        normed = (input_wide * rms_scale(input_wide) * attn_gain).astype(BF)
        qkv = dot_nn(normed, w_qkv)
        query_raw = qkv[:, :local_cols]
        key_raw = qkv[:, local_cols : 2 * local_cols]
        value_low = qkv[:, 2 * local_cols :].astype(BF)
        squares = jnp.stack(
            [jnp.sum(query_raw * query_raw, axis=1), jnp.sum(key_raw * key_raw, axis=1)]
        )
        squares = sum_all(squares, "tensor", n_tensor)
        scales = lax.rsqrt(squares / model_width + EPS)
        query_rs, key_rs = scales[0][:, None], scales[1][:, None]
        query_unit = query_raw * query_rs
        key_unit = key_raw * key_rs
        q_n = query_unit * query_gain
        k_n = key_unit * key_gain
        queries = (q_n * cos_all + half_swap(q_n) * sin_all).astype(BF)
        keys_rot = (k_n * cos_all + half_swap(k_n) * sin_all).astype(BF)
        attended, attn_low, lse, own_attn = attn_fwd(
            queries, keys_rot, value_low, seg_col, seg_rows, block, reach, n_tensor, 0
        )
        residual = input_own + dot_nn(own_attn, full_wo)
        own_moe_in = (residual * rms_scale(residual) * moe_gain).astype(BF)
        moe_in = lax.all_gather(own_moe_in, "tensor", axis=0, tiled=True)
        lead = expert_chunk(
            moe_in, full_cot, mask, w_gate, w_up, wd_flat, router, None, first=0, pairs=1, parts=n_dp
        )
    scale_two = rms_scale(residual)

    chunks = (1, 3, 4)
    dots = None
    reduced = []
    carried = None
    first = 0
    for count in chunks:
        res = lead if first == 0 else expert_chunk(
            moe_in, full_cot, gates, w_gate, w_up, wd_flat, router, carried,
            first=first, pairs=count, parts=n_dp,
        )
        dgu, ga, wcat, dot_c, grads = res[:5]
        if first == 0:
            xt, gates, router_probs = res[5:]
        if len(reduced) == 2:
            reduced[0], dgu = lax.optimization_barrier((reduced[0], dgu))
        carried = (xt, dgu, ga, wcat)
        dots = dot_c if dots is None else dots + dot_c
        reduced.append(lax.psum_scatter(grads, "dp", scatter_dimension=0, tiled=False))
        first += count
    moe_back = matmul_scatter(dgu, wcat, n_tensor, 2, True, "moe_back")

    own_dots = jnp.sum(
        lax.all_to_all(dots.reshape(n_tensor, own_rows, experts), "tensor", 0, 0), axis=0
    )
    own_mask = lax.dynamic_slice_in_dim(mask, rank_start, own_rows, 0)
    own_probs = lax.dynamic_slice_in_dim(router_probs, rank_start, own_rows, 0)
    prob_grads = own_dots * own_mask
    own_logit = (
        own_probs * (prob_grads - jnp.sum(own_probs * prob_grads, axis=1, keepdims=True))
    ).astype(BF)
    router_grad = dot_tn(own_logit, own_moe_in)
    moe_grad = moe_back + dot_nt(own_logit, router)

    unit_two = residual * scale_two
    moe_gain_grad = jnp.sum(moe_grad * unit_two, axis=0)
    scaled_two = moe_grad * moe_gain
    residual_grad = cotangent.astype(F32) + scale_two * (
        scaled_two - unit_two * jnp.mean(scaled_two * unit_two, axis=1, keepdims=True)
    )
    residual_low = gather_all(residual_grad.astype(BF), n_tensor, 3, "gather_residual")
    output_grad = dot_tn(residual_low, attn_low).astype(BF)
    heads_grad = dot_nt(residual_low, w_output).astype(BF)

    dq_rot, dk_rot, dv = attn_bwd(
        lo_block, queries, keys_rot, value_low, heads_grad, attended, lse, seg_col, seg_rows, block
    )
    reduced[1], dq_rot = lax.optimization_barrier((reduced[1], dq_rot))
    query_norm_grad = dq_rot * cos_all - half_swap(dq_rot) * sin_all
    key_norm_grad = dk_rot * cos_all - half_swap(dk_rot) * sin_all
    query_gain_grad = jnp.sum(query_norm_grad * query_unit, axis=0)
    key_gain_grad = jnp.sum(key_norm_grad * key_unit, axis=0)
    query_scaled = query_norm_grad * query_gain
    key_scaled = key_norm_grad * key_gain
    inner = jnp.stack(
        [jnp.sum(query_scaled * query_unit, axis=1), jnp.sum(key_scaled * key_unit, axis=1)]
    )
    inner = sum_all(inner, "tensor", n_tensor) / model_width
    query_grad_low = (query_rs * (query_scaled - query_unit * inner[0][:, None])).astype(BF)
    key_grad_low = (key_rs * (key_scaled - key_unit * inner[1][:, None])).astype(BF)
    qkv_grad = jnp.concatenate([query_grad_low, key_grad_low, dv.astype(BF)], axis=1)
    qkv_w_grad = dot_tn(normed, qkv_grad).astype(BF)
    normed_grad = matmul_scatter(qkv_grad, w_qkv, n_tensor, 4, True, "normed_back")
    ga, qkv_w_grad = lax.optimization_barrier((ga, qkv_w_grad))
    moe_out = matmul_scatter(ga, wd_flat, n_tensor, 5, False, "moe_out")
    block_output = (residual + moe_out).astype(BF)
    scale_own = rms_scale(input_own)
    unit_one = input_own * scale_own
    attn_gain_grad = jnp.sum(normed_grad * unit_one, axis=0)
    scaled_one = normed_grad * attn_gain
    grad_input = residual_grad + scale_own * (
        scaled_one - unit_one * jnp.mean(scaled_one * unit_one, axis=1, keepdims=True)
    )

    proj_grad = jnp.concatenate([qkv_w_grad, output_grad], axis=1)
    reduced[2], proj_grad, block_output, grad_input = lax.optimization_barrier(
        (reduced[2], proj_grad, block_output, grad_input)
    )
    qkv_red = lax.psum_scatter(proj_grad, "dp", scatter_dimension=0, tiled=True)
    wo_red = qkv_red[:, 3 * local_cols :].T.astype(F32)
    gains = jnp.concatenate(
        [
            router_grad,
            moe_gain_grad[None, :],
            attn_gain_grad[None, :],
            lax.dynamic_update_slice_in_dim(
                jnp.zeros((1, model_width), F32), query_gain_grad[None, :], col_start, 1
            ),
            lax.dynamic_update_slice_in_dim(
                jnp.zeros((1, model_width), F32), key_gain_grad[None, :], col_start, 1
            ),
        ],
        axis=0,
    )
    gains = sum_everywhere(gains, n_tensor, n_dp)

    ds = model_width // n_dp
    gate_out, up_out, down_out = [], [], []
    for r, count in zip(reduced, chunks):
        r = r.reshape(2 * count, 3, ds, hid)
        gate_out.append(r[:, 0])
        up_out.append(r[:, 1])
        down = r[:, 2].reshape(2 * count, ds // hid, hid, hid)
        down_out.append(down.transpose(0, 2, 1, 3).reshape(2 * count, hid, ds))
    grad_gate = jnp.concatenate(gate_out, axis=0).astype(F32)
    grad_up = jnp.concatenate(up_out, axis=0).astype(F32)
    grad_down = jnp.concatenate(down_out, axis=0).astype(F32)
    return (
        block_output,
        grad_input,
        qkv_red[:, :local_cols].astype(F32),
        qkv_red[:, local_cols : 2 * local_cols].astype(F32),
        qkv_red[:, 2 * local_cols : 3 * local_cols].astype(F32),
        wo_red,
        gains[experts + 1],
        gains[experts + 2],
        gains[experts + 3],
        gains[experts],
        gains[:experts].T,
        grad_gate,
        grad_up,
        grad_down,
    )


def solution(mesh):
    rows = P(("dp", "tensor"), None)
    cols = P(None, "tensor")
    wide = P(None, None, "tensor")
    placed = (
        rows, P("dp", None), P("dp", None), cols, cols, cols, P("tensor", None), P(), P("tensor"), P("tensor"),
        P(), P(), wide, wide, P(None, "tensor", None), rows,
    )
    outs = (
        rows, rows, P("dp", "tensor"), P("dp", "tensor"), P("dp", "tensor"), P("tensor", "dp"), P(), P(), P(), P(),
        P(), P(None, "dp", "tensor"), P(None, "dp", "tensor"), P(None, "tensor", "dp"),
    )
    return jax.shard_map(
        functools.partial(
            per_device, n_dp=mesh.shape["dp"], n_tensor=mesh.shape["tensor"]
        ),
        mesh=mesh,
        in_specs=placed,
        out_specs=outs,
        check_vma=False,
    )
```

```python
import functools
import math

import jax
import jax.numpy as jnp
from jax import lax
from jax.experimental import pallas as pl
from jax.experimental.pallas import tpu as pltpu
from jax.sharding import PartitionSpec as P

HEAD_DIM = 128
EPS = 1e-05
NEG = -1e30
MIB = 1 << 20
BF = jnp.bfloat16
F32 = jnp.float32


def rms_scale(values):
    return lax.rsqrt(jnp.mean(values * values, axis=-1, keepdims=True) + EPS)


def dot_nn(a, b):
    return lax.dot_general(a, b, (((1,), (0,)), ((), ())), preferred_element_type=F32)


def dot_nt(a, b):
    return lax.dot_general(a, b, (((1,), (1,)), ((), ())), preferred_element_type=F32)


def dot_tn(a, b):
    return lax.dot_general(a, b, (((0,), (0,)), ((), ())), preferred_element_type=F32)


def partner(me, bit):
    return me + bit * (1 - 2 * ((me // bit) % 2))


def remote(src, dst, send_sem, recv_sem, target):
    return pltpu.make_async_remote_copy(
        src_ref=src,
        dst_ref=dst,
        send_sem=send_sem,
        recv_sem=recv_sem,
        device_id={"tensor": target},
        device_id_type=pl.DeviceIdType.MESH,
    )


def greet(targets):
    barrier = pltpu.get_barrier_semaphore()
    for t in targets:
        pl.semaphore_signal(
            barrier, inc=1, device_id={"tensor": t}, device_id_type=pl.DeviceIdType.MESH
        )
    pl.semaphore_wait(barrier, len(targets))


def attn_fwd_body(
    q_ref, k_ref, v_ref, sq_ref, sk_ref, o_ref, low_ref, lse_ref, own_ref, buf, send_sem, recv_sem, here_sem,
    *, block, heads, reach, size
):
    qb = pl.program_id(0)
    me = lax.axis_index("tensor")
    scale = 1.0 / math.sqrt(HEAD_DIM)
    cols_all = heads * HEAD_DIM

    @pl.when(qb == 0)
    def _():
        greet([lax.rem(me + t, size) for t in range(1, size)])

    seg_q = sq_ref[...]
    row = qb * block + lax.broadcasted_iota(jnp.int32, (block, block), 0)
    col0 = lax.broadcasted_iota(jnp.int32, (block, block), 1)
    qs = [q_ref[:, h * HEAD_DIM : (h + 1) * HEAD_DIM] for h in range(heads)]

    def step(kb, carry):
        rows = pl.ds(pl.multiple_of(kb * block, block), block)
        allowed = (seg_q == sk_ref[kb]) & (kb * block + col0 <= row)
        out = []
        for h in range(heads):
            m, l, acc = carry[h]
            cols = slice(h * HEAD_DIM, (h + 1) * HEAD_DIM)
            s = jnp.where(allowed, dot_nt(qs[h], k_ref[rows, cols]) * scale, NEG)
            m_new = jnp.maximum(m, jnp.max(s, axis=1, keepdims=True))
            p = jnp.exp(s - m_new)
            alpha = jnp.exp(m - m_new)
            l = alpha * l + jnp.sum(p, axis=1, keepdims=True)
            acc = alpha * acc + dot_nn(p.astype(BF), v_ref[rows, cols])
            out.append((m_new, l, acc))
        return tuple(out)

    init = tuple(
        (
            jnp.full((block, 1), NEG, F32),
            jnp.zeros((block, 1), F32),
            jnp.zeros((block, HEAD_DIM), F32),
        )
        for _ in range(heads)
    )
    final = lax.fori_loop(jnp.maximum(qb - reach, 0), qb + 1, step, init)
    for h in range(heads):
        m, l, acc = final[h]
        cols = slice(h * HEAD_DIM, (h + 1) * HEAD_DIM)
        out = acc / l
        o_ref[:, cols] = out
        low_ref[:, cols] = out.astype(BF)
        buf[qb, :, cols] = out.astype(BF)
        lse_ref[:, h : h + 1] = m + jnp.log(l)

    own = own_ref.shape[0]
    per = block // own

    def rows_of(dev):
        return buf.at[dev // per, pl.ds(pl.multiple_of((dev % per) * own, own), own)]

    def land(src):
        return own_ref.at[:, pl.ds(pl.multiple_of(src * cols_all, HEAD_DIM), cols_all)]

    def send(t):
        return remote(rows_of(t), land(me), send_sem.at[t], recv_sem.at[me], t)

    for j in range(per):
        dest = qb * per + j

        @pl.when(dest != me)
        def _():
            send(dest).start()

        @pl.when(dest == me)
        def _():
            pltpu.make_async_copy(rows_of(me), land(me), here_sem).start()

    @pl.when(qb == pl.num_programs(0) - 1)
    def _():
        pltpu.make_async_copy(rows_of(me), land(me), here_sem).wait()
        for t in range(1, size):
            other = lax.rem(me + t, size)
            send(other).wait_send()
            remote(
                rows_of(other), land(other), send_sem.at[other], recv_sem.at[other], other
            ).wait_recv()


def attn_fwd(q, k, v, seg_col, seg_rows, block, reach, size, cid):
    tokens, cols = q.shape
    heads = cols // HEAD_DIM
    nb = tokens // block
    full = lambda shape: pl.BlockSpec(shape, lambda i: (0,) * len(shape))
    rowed = lambda c: pl.BlockSpec((block, c), lambda i: (i, 0))
    return pl.pallas_call(
        functools.partial(attn_fwd_body, block=block, heads=heads, reach=reach, size=size),
        out_shape=(
            jax.ShapeDtypeStruct((tokens, cols), F32),
            jax.ShapeDtypeStruct((tokens, cols), BF),
            jax.ShapeDtypeStruct((tokens, heads), F32),
            jax.ShapeDtypeStruct((tokens // size, cols * size), BF),
        ),
        grid=(nb,),
        in_specs=[
            rowed(cols),
            full((tokens, cols)),
            full((tokens, cols)),
            rowed(1),
            full((nb, 1, block)),
        ],
        out_specs=[rowed(cols), rowed(cols), rowed(heads), pl.BlockSpec(memory_space=pl.ANY)],
        scratch_shapes=[
            pltpu.VMEM((nb, block, cols), BF),
            pltpu.SemaphoreType.DMA((size,)),
            pltpu.SemaphoreType.DMA((size,)),
            pltpu.SemaphoreType.DMA,
        ],
        compiler_params=pltpu.CompilerParams(
            vmem_limit_bytes=32 * MIB, collective_id=cid, has_side_effects=True
        ),
        cost_estimate=pl.CostEstimate(
            flops=10**8, bytes_accessed=4 * MIB, transcendentals=10**5
        ),
        name="attn_fwd",
    )(q, k, v, seg_col, seg_rows)


def attn_bwd_body(
    lo_ref, q_ref, k_ref, v_ref, do_ref, o_ref, lse_ref, sq_ref, sk_ref, dq_ref, dk_ref, dv_ref, *, block, heads
):
    qb = pl.program_id(0)
    scale = 1.0 / math.sqrt(HEAD_DIM)

    @pl.when(qb == 0)
    def _():
        dk_ref[...] = jnp.zeros_like(dk_ref)
        dv_ref[...] = jnp.zeros_like(dv_ref)

    seg_q = sq_ref[...]
    row = qb * block + lax.broadcasted_iota(jnp.int32, (block, block), 0)
    col0 = lax.broadcasted_iota(jnp.int32, (block, block), 1)
    hc = [slice(h * HEAD_DIM, (h + 1) * HEAD_DIM) for h in range(heads)]
    qs = [q_ref[:, c] for c in hc]
    dos = [do_ref[:, c] for c in hc]
    lse = [lse_ref[:, h : h + 1] for h in range(heads)]
    dsum = [
        jnp.sum(dos[h].astype(F32) * o_ref[:, hc[h]], axis=1, keepdims=True) for h in range(heads)
    ]

    def step(kb, carry):
        rows = pl.ds(pl.multiple_of(kb * block, block), block)
        allowed = (seg_q == sk_ref[kb]) & (kb * block + col0 <= row)
        out = []
        for h in range(heads):
            k_blk = k_ref[rows, hc[h]]
            s = jnp.where(allowed, dot_nt(qs[h], k_blk) * scale, NEG)
            p = jnp.exp(s - lse[h])
            dp = dot_nt(dos[h], v_ref[rows, hc[h]])
            ds = (p * (dp - dsum[h])).astype(BF)
            dv_ref[rows, hc[h]] += dot_tn(p.astype(BF), dos[h])
            dk_ref[rows, hc[h]] += dot_tn(ds, qs[h]) * scale
            out.append(carry[h] + dot_nn(ds, k_blk))
        return tuple(out)

    init = tuple(jnp.zeros((block, HEAD_DIM), F32) for _ in range(heads))
    final = lax.fori_loop(lo_ref[qb], qb + 1, step, init)
    for h in range(heads):
        dq_ref[:, hc[h]] = final[h] * scale


def attn_bwd(lo, q, k, v, do, o, lse, seg_col, seg_rows, block):
    tokens, cols = q.shape
    heads = cols // HEAD_DIM
    nb = tokens // block
    full = lambda shape: pl.BlockSpec(shape, lambda i, lo: (0,) * len(shape))
    rowed = lambda c: pl.BlockSpec((block, c), lambda i, lo: (i, 0))
    return pl.pallas_call(
        functools.partial(attn_bwd_body, block=block, heads=heads),
        out_shape=tuple(jax.ShapeDtypeStruct((tokens, cols), F32) for _ in range(3)),
        grid_spec=pltpu.PrefetchScalarGridSpec(
            num_scalar_prefetch=1,
            grid=(nb,),
            in_specs=[
                rowed(cols),
                full((tokens, cols)),
                full((tokens, cols)),
                rowed(cols),
                rowed(cols),
                rowed(heads),
                rowed(1),
                full((nb, 1, block)),
            ],
            out_specs=[rowed(cols), full((tokens, cols)), full((tokens, cols))],
        ),
        compiler_params=pltpu.CompilerParams(vmem_limit_bytes=40 * MIB),
        cost_estimate=pl.CostEstimate(
            flops=10**8, bytes_accessed=4 * MIB, transcendentals=10**5
        ),
        name="attn_bwd",
    )(lo, q, k, v, do, o, lse, seg_col, seg_rows)


def expert_body(*refs, first, rows_blk, parts):
    lead = first == 0
    if lead:
        x_hbm, g_hbm, mask_ref, wg_ref, wu_ref, wd_ref, router_ref = refs[:7]
        dgu_ref, ga_ref, wcat, dots_ref, grads_ref, xt_hbm, gates_ref, probs_ref = refs[7:15]
        x_v, xt_v, g_v, sem_x, sem_t, sem_g = refs[15:]
    else:
        x_hbm, g_hbm, gates_ref, wg_ref, wu_ref, wd_ref, xt_hbm = refs[:7]
        dgu_ref, ga_ref, wcat, dots_ref, grads_ref = refs[10:15]
        x_v, xt_v, g_v, sem_x, sem_t, sem_g = refs[15:]
    p = pl.program_id(0)
    tokens, width = x_v.shape
    nblk = tokens // rows_blk
    hid = wg_ref.shape[2]
    experts = gates_ref.shape[1]
    ds = width // parts

    if lead:
        t_copy = pltpu.make_async_copy(xt_v, xt_hbm, sem_t)
    else:
        t_copy = pltpu.make_async_copy(xt_hbm, xt_v, sem_t)

    def copies(i):
        r = pl.ds(i * rows_blk, rows_blk)
        return (
            pltpu.make_async_copy(x_hbm.at[r], x_v.at[r], sem_x.at[i]),
            pltpu.make_async_copy(g_hbm.at[r], g_v.at[r], sem_g.at[i]),
        )

    @pl.when(p == 0)
    def _():
        for i in range(nblk):
            for c in copies(i):
                c.start()
        if not lead:
            t_copy.start()
        dots_ref[...] = jnp.zeros_like(dots_ref)

    wcat[:, 0:hid] = wg_ref[0]
    wcat[:, hid : 2 * hid] = wg_ref[1]
    wcat[:, 2 * hid : 3 * hid] = wu_ref[0]
    wcat[:, 3 * hid : 4 * hid] = wu_ref[1]
    lane = lax.broadcasted_iota(jnp.int32, (rows_blk, experts), 1)
    e0 = 2 * (first + p)

    def block(i, _):
        start = pl.multiple_of(i * rows_blk, rows_blk)
        r = pl.ds(start, rows_blk)

        @pl.when(p == 0)
        def _():
            for c in copies(i):
                c.wait()

        if lead:
            xt_v[:, r] = x_v[r, :].T
            logits = dot_nn(x_v[r, :], router_ref[...])
            grown = jnp.exp(logits - jnp.max(logits, axis=1, keepdims=True))
            probs = grown / jnp.sum(grown, axis=1, keepdims=True)
            probs_ref[r, :] = probs
            gates_ref[r, :] = probs * mask_ref[r, :]
        gu = dot_nn(x_v[r, :], wcat[...])
        q = dot_nt(g_v[r, :], wd_ref[...])
        gate_rows = gates_ref[r, :]
        dots = dots_ref[r, :]
        for j in range(2):
            pre = gu[:, j * hid : (j + 1) * hid]
            up = gu[:, (2 + j) * hid : (3 + j) * hid]
            back = q[:, j * hid : (j + 1) * hid]
            here = lane == e0 + j
            gate = jnp.sum(jnp.where(here, gate_rows, 0.0), axis=1, keepdims=True)
            sig = jax.nn.sigmoid(pre)
            silu = pre * sig
            act = silu * up
            dot = jnp.sum(act * back, axis=1, keepdims=True)
            dots = dots + jnp.where(here, dot, 0.0)
            scaled = gate * back
            d_up = scaled * silu
            d_gate = scaled * up * (sig + silu * (1.0 - sig))
            dgu_ref[r, j * hid : (j + 1) * hid] = d_gate.astype(BF)
            dgu_ref[r, (2 + j) * hid : (3 + j) * hid] = d_up.astype(BF)
            ga_ref[r, j * hid : (j + 1) * hid] = (gate * act).astype(BF)
        dots_ref[r, :] = dots
        return 0

    lax.fori_loop(0, nblk, block, 0)

    @pl.when(p == 0)
    def _():
        if lead:
            t_copy.start()
        else:
            t_copy.wait()

    for s in range(parts):
        gd = dot_tn(ga_ref[...], g_v[:, s * ds : (s + 1) * ds]).astype(BF)
        gw = dot_nn(xt_v[s * ds : (s + 1) * ds, :], dgu_ref[...]).astype(BF)
        for j in range(2):
            grads_ref[s, 3 * j] = gw[:, j * hid : (j + 1) * hid]
            grads_ref[s, 3 * j + 1] = gw[:, (2 + j) * hid : (3 + j) * hid]
            for c in range(ds // hid):
                grads_ref[s, 3 * j + 2, c * hid : (c + 1) * hid, :] = gd[
                    j * hid : (j + 1) * hid, c * hid : (c + 1) * hid
                ]

    if lead:

        @pl.when(p == 0)
        def _():
            t_copy.wait()


def expert_chunk(x, g, gates, wg, wu, wd, router, carried, *, first, pairs, parts):
    tokens, width = x.shape
    experts, _, hid = wg.shape
    total = experts // 2
    rows_blk = 512
    nblk = tokens // rows_blk
    ds = width // parts
    lead = first == 0
    assert not lead or pairs == 1
    any_spec = pl.BlockSpec(memory_space=pl.ANY)
    colblk = lambda rows, c: pl.BlockSpec((rows, c), lambda p: (0, first + p))
    in_specs = [
        any_spec,
        any_spec,
        pl.BlockSpec((tokens, experts), lambda p: (0, 0)),
        pl.BlockSpec((2, width, hid), lambda p: (first + p, 0, 0)),
        pl.BlockSpec((2, width, hid), lambda p: (first + p, 0, 0)),
        pl.BlockSpec((2 * hid, width), lambda p: (first + p, 0)),
    ]
    out_shape = [
        jax.ShapeDtypeStruct((tokens, total * 4 * hid), BF),
        jax.ShapeDtypeStruct((tokens, total * 2 * hid), BF),
        jax.ShapeDtypeStruct((width, total * 4 * hid), BF),
        jax.ShapeDtypeStruct((tokens, experts), F32),
        jax.ShapeDtypeStruct((parts, pairs * 6, ds, hid), BF),
    ]
    out_specs = [
        colblk(tokens, 4 * hid),
        colblk(tokens, 2 * hid),
        colblk(width, 4 * hid),
        pl.BlockSpec((tokens, experts), lambda p: (0, 0)),
        pl.BlockSpec((parts, 6, ds, hid), lambda p: (0, p, 0, 0)),
    ]
    args = [x, g, gates, wg, wu, wd]
    alias = {}
    if lead:
        args.append(router)
        in_specs.append(pl.BlockSpec(router.shape, lambda p: (0, 0)))
        narrow = jax.ShapeDtypeStruct((tokens, experts), F32)
        out_shape += [jax.ShapeDtypeStruct((width, tokens), BF), narrow, narrow]
        out_specs += [any_spec] + [pl.BlockSpec((tokens, experts), lambda p: (0, 0))] * 2
    else:
        xt, dgu, ga, wcat = carried
        args += [xt, dgu, ga, wcat]
        in_specs += [any_spec] * 4
        alias = {7: 0, 8: 1, 9: 2}
    return pl.pallas_call(
        functools.partial(expert_body, first=first, rows_blk=rows_blk, parts=parts),
        out_shape=tuple(out_shape),
        grid=(pairs,),
        in_specs=in_specs,
        out_specs=out_specs,
        scratch_shapes=[
            pltpu.VMEM((tokens, width), BF),
            pltpu.VMEM((width, tokens), BF),
            pltpu.VMEM((tokens, width), BF),
            pltpu.SemaphoreType.DMA((nblk,)),
            pltpu.SemaphoreType.DMA,
            pltpu.SemaphoreType.DMA((nblk,)),
        ],
        input_output_aliases=alias,
        compiler_params=pltpu.CompilerParams(vmem_limit_bytes=61 * MIB),
        cost_estimate=pl.CostEstimate(
            flops=10**9, bytes_accessed=4 * MIB, transcendentals=10**5
        ),
        name="expert_chunk",
    )(*args)


GATHER_COPIES = 13


def gather_plan(x_hbm, land, me, own, send_sem, recv_sem):
    half = own // 2
    pc, px, py = (partner(me, b) for b in (1, 2, 4))
    diag = partner(px, 4)

    def piece(dev, a, n):
        return land.at[pl.ds(pl.multiple_of(dev * own + a, half), n)]

    plan = [
        (me, 0, half, px),
        (me, half, half, py),
        (me, half, half, px),
        (me, 0, half, py),
        (me, 0, own, pc),
        (px, 0, half, py),
        (py, half, half, px),
        (px, 0, half, pc),
        (py, half, half, pc),
        (px, half, half, pc),
        (py, 0, half, pc),
        (diag, 0, half, pc),
        (diag, half, half, pc),
    ]
    origin = {0: px, 1: py, 2: px, 3: py, 4: pc, 5: diag, 6: diag}

    def copy(k):
        dev, a, n, target = plan[k]
        src = x_hbm.at[pl.ds(a, n)] if k < 5 else piece(dev, a, n)
        return remote(src, piece(dev, a, n), send_sem.at[k], recv_sem.at[k], target)

    def arrived(k):
        dev, a, n, target = plan[k]
        src = origin[k] if k in origin else partner(dev, 1)
        return remote(piece(src, a, n), piece(src, a, n), send_sem.at[k], recv_sem.at[k], target)

    return copy, arrived, pc, px, py, diag


def front_body(
    x_hbm, wo_hbm, g_hbm, wq_hbm, wk_hbm, wv_hbm, gain_ref, qg_ref, kg_ref, mg_ref, routes_ref, sk_ref,
    normed_hbm, *rest, size, block, reach, capacity
):
    outs, rest = rest[:14], rest[14:]
    g_all, rest = rest[0], rest[1:]
    local, rest = rest[:14], rest[14:]
    (
        q_ref, k_ref, v_ref, qu_ref, ku_ref, rs_ref, cos_ref, sin_ref, o_ref, low_ref, lse_ref, res_ref, moe_ref,
        mask_ref,
    ) = local
    (
        x_v, n_v, w_v, wo_all, own_ref, sums, sums_all, place_v,
        send_sem, recv_sem, wo_send, wo_recv, g_send, g_recv, ss_send, ss_recv, a_send, a_recv,
        w_sem, x_sem, wo_sem, g_sem, a_sem, n_sem, o_sem,
    ) = rest

    def written(i):
        return pltpu.make_async_copy(local[i], outs[i], o_sem.at[i])

    me = lax.axis_index("tensor")
    own = x_hbm.shape[0]
    width = x_hbm.shape[1]
    cols = q_ref.shape[1]
    heads = cols // HEAD_DIM
    half_dim = HEAD_DIM // 2
    weights = [
        pltpu.make_async_copy(w, w_v.at[:, pl.ds(i * cols, cols)], w_sem.at[i])
        for i, w in enumerate((wq_hbm, wk_hbm, wv_hbm))
    ]
    mine = pl.ds(pl.multiple_of(me * own, own), own)
    here = pltpu.make_async_copy(x_hbm, x_v.at[mine], x_sem)
    here.start()
    for w in weights:
        w.start()
    greet([lax.rem(me + t, size) for t in range(1, size)])
    copy, arrived, pc, px, py, diag = gather_plan(x_hbm, x_v, me, own, send_sem, recv_sem)
    wo_copy, wo_arrived = gather_plan(wo_hbm, wo_all, me, own, wo_send, wo_recv)[:2]
    for k in range(5):
        copy(k).start()
    g_copy, g_arrived = gather_plan(g_hbm, g_all, me, own, g_send, g_recv)[:2]
    wo_here = pltpu.make_async_copy(wo_hbm, wo_all.at[mine], wo_sem)
    wo_here.start()
    g_here = pltpu.make_async_copy(g_hbm, g_all.at[mine], g_sem)
    g_here.start()

    lane = lax.broadcasted_iota(jnp.int32, (own, HEAD_DIM), 1)
    power = (lane % half_dim).astype(F32) * (-2.0 * math.log(10000.0) / HEAD_DIM)
    frequency = jnp.exp(power)

    seg = jnp.concatenate([sk_ref[i] for i in range(size)], axis=0)
    first_token = jnp.zeros(seg.shape, F32)
    for value in range(1, 16):
        count = jnp.sum(jnp.where(seg < value, 1.0, 0.0))
        first_token = jnp.where(seg == value, count, first_token)
    index = lax.broadcasted_iota(jnp.int32, seg.shape, 0) * block + lax.broadcasted_iota(
        jnp.int32, seg.shape, 1
    )
    place = index.astype(F32) - first_token
    for i in range(size):
        place_v[i] = place[i : i + 1]

    def column(row):
        return jnp.broadcast_to(row, (HEAD_DIM, block)).T

    def table(i, _):
        r = pl.ds(pl.multiple_of(i * own, own), own)
        angle = column(place_v[i]) * frequency
        cos_ref[r, :] = jnp.cos(angle)
        sine = jnp.sin(angle)
        sin_ref[r, :] = jnp.where(lane < half_dim, -sine, sine)
        return 0

    lax.fori_loop(0, size, table, 0)

    experts = mask_ref.shape[1]
    expert = lax.broadcasted_iota(jnp.int32, (experts, block), 0)
    earlier = (
        lax.broadcasted_iota(jnp.int32, (block, block), 0)
        < lax.broadcasted_iota(jnp.int32, (block, block), 1)
    )
    earlier = jnp.where(earlier, 1.0, 0.0).astype(BF)
    before = jnp.zeros((experts, 1), F32)
    fill = jnp.zeros((HEAD_DIM - experts, block), F32)
    for i in range(size):
        chosen = routes_ref[:, i * block : (i + 1) * block]
        routed = jnp.zeros((experts, block), F32)
        for k in range(chosen.shape[0]):
            routed = routed + jnp.where(chosen[k : k + 1] == expert, 1.0, 0.0)
        taken = dot_nn(routed.astype(BF), earlier) + before
        before = before + jnp.sum(routed, axis=1, keepdims=True)
        kept = jnp.where(taken < capacity, routed, 0.0)
        mask_ref[i * block : (i + 1) * block, :] = jnp.concatenate([kept, fill], axis=0).T[:, :experts]
    for i in (6, 7, 13):
        written(i).start()

    def stored(dev):
        r = pl.ds(pl.multiple_of(dev * own, own), own)
        return pltpu.make_async_copy(n_v.at[r], normed_hbm.at[r], n_sem.at[dev])

    def process(dev):
        r = pl.ds(pl.multiple_of(dev * own, own), own)
        wide = x_v[r, :].astype(F32)
        scale = lax.rsqrt(jnp.mean(wide * wide, axis=1, keepdims=True) + EPS)
        normed = (wide * scale * gain_ref[...]).astype(BF)
        n_v[r, :] = normed
        stored(dev).start()
        res = dot_nn(normed, w_v[...])
        q = res[:, :cols]
        k = res[:, cols : 2 * cols]
        qu_ref[r, :] = q
        ku_ref[r, :] = k
        v_ref[r, :] = res[:, 2 * cols :].astype(BF)
        pair = jnp.where(
            lane == 0,
            jnp.sum(q * q, axis=1, keepdims=True),
            jnp.sum(k * k, axis=1, keepdims=True),
        )
        sums[dev] = pair.T[0:2, :]

    here.wait()
    for w in weights:
        w.wait()
    process(me)
    arrived(4).wait_recv()
    process(pc)
    arrived(0).wait_recv()
    copy(5).start()
    copy(7).start()
    arrived(1).wait_recv()
    copy(6).start()
    copy(8).start()
    arrived(2).wait_recv()
    copy(9).start()
    arrived(3).wait_recv()
    copy(10).start()
    for k in range(5):
        wo_copy(k).start()
    process(px)
    process(py)
    arrived(7).wait_recv()
    arrived(9).wait_recv()
    process(partner(px, 1))
    arrived(8).wait_recv()
    arrived(10).wait_recv()
    process(partner(py, 1))
    arrived(5).wait_recv()
    copy(11).start()
    arrived(6).wait_recv()
    copy(12).start()
    process(diag)
    arrived(11).wait_recv()
    arrived(12).wait_recv()
    process(partner(diag, 1))
    hand_on(wo_arrived, wo_copy, ((0, (5, 7)), (1, (6, 8))))

    def exchange(t, src):
        other = lax.rem(me + t, size)
        slot = me if src is None else other
        return remote(sums, sums_all.at[slot], ss_send.at[other], ss_recv.at[slot], other)

    for t in range(1, size):
        exchange(t, None).start()
    sums_all[me] = sums[...]
    hand_on(wo_arrived, wo_copy, ((2, (9,)), (3, (10,))))
    for k in range(5):
        g_copy(k).start()
    for t in range(1, size):
        exchange(t, 1).wait_recv()
    total = sums_all[0]
    for d in range(1, size):
        total = total + sums_all[d]
    rows_iota = lax.broadcasted_iota(jnp.int32, (HEAD_DIM, own), 0)
    for d in range(size):
        r = slice(d * own, (d + 1) * own)
        tot = total[d]
        both = jnp.where(rows_iota == 0, tot[0:1, :], tot[1:2, :])
        rs = lax.rsqrt(both / width + EPS).T
        rs_ref[r, :] = rs[:, 0:2]
        cos, sin = cos_ref[r, :], sin_ref[r, :]
        for j, (unit_ref, gain, dst) in enumerate(((qu_ref, qg_ref, q_ref), (ku_ref, kg_ref, k_ref))):
            unit = unit_ref[r, :] * rs[:, j : j + 1]
            unit_ref[r, :] = unit
            wide = unit * gain[...]
            for h in range(heads):
                c = slice(h * HEAD_DIM, (h + 1) * HEAD_DIM)
                w = wide[:, c]
                dst[r, c] = (w * cos + pltpu.roll(w, half_dim, 1) * sin).astype(BF)

    for i in range(6):
        written(i).start()
    score_scale = 1.0 / math.sqrt(HEAD_DIM)
    row0 = lax.broadcasted_iota(jnp.int32, (block, block), 0)
    col0 = lax.broadcasted_iota(jnp.int32, (block, block), 1)
    hc = [slice(h * HEAD_DIM, (h + 1) * HEAD_DIM) for h in range(heads)]

    def land(src):
        return own_ref.at[:, pl.ds(pl.multiple_of(src * cols, HEAD_DIM), cols)]

    def rows_of(dev):
        return low_ref.at[pl.ds(pl.multiple_of(dev * own, own), own)]

    def send(t):
        return remote(rows_of(t), land(me), a_send.at[t], a_recv.at[me], t)

    def query_block(qb, _):
        rq = pl.ds(pl.multiple_of(qb * block, block), block)
        seg_q = column(sk_ref[qb].astype(F32))[:, 0:1]
        qs = [q_ref[rq, c] for c in hc]

        def step(kb, carry):
            rows = pl.ds(pl.multiple_of(kb * block, block), block)
            allowed = (seg_q == sk_ref[kb].astype(F32)) & (kb * block + col0 <= qb * block + row0)
            out = []
            for h in range(heads):
                m, l, acc = carry[h]
                s = jnp.where(allowed, dot_nt(qs[h], k_ref[rows, hc[h]]) * score_scale, NEG)
                m_new = jnp.maximum(m, jnp.max(s, axis=1, keepdims=True))
                p = jnp.exp(s - m_new)
                alpha = jnp.exp(m - m_new)
                l = alpha * l + jnp.sum(p, axis=1, keepdims=True)
                acc = alpha * acc + dot_nn(p.astype(BF), v_ref[rows, hc[h]])
                out.append((m_new, l, acc))
            return tuple(out)

        init = tuple(
            (
                jnp.full((block, 1), NEG, F32),
                jnp.zeros((block, 1), F32),
                jnp.zeros((block, HEAD_DIM), F32),
            )
            for _ in range(heads)
        )
        final = lax.fori_loop(jnp.maximum(qb - reach, 0), qb + 1, step, init)
        for h in range(heads):
            m, l, acc = final[h]
            out = acc / l
            o_ref[rq, hc[h]] = out
            low_ref[rq, hc[h]] = out.astype(BF)
            lse_ref[rq, h : h + 1] = m + jnp.log(l)

        @pl.when(qb != me)
        def _():
            send(qb).start()

        @pl.when(qb == me)
        def _():
            pltpu.make_async_copy(rows_of(me), land(me), a_sem).start()

        @pl.when(qb == 3)
        def _():
            hand_on(wo_arrived, wo_copy, ((5, (11,)), (6, (12,))))

        @pl.when(qb == 5)
        def _():
            hand_on(g_arrived, g_copy, ((0, (5, 7)), (1, (6, 8))))

        return 0

    lax.fori_loop(0, size, query_block, 0)
    for i in (8, 9, 10):
        written(i).start()
    pltpu.make_async_copy(rows_of(me), land(me), a_sem).wait()
    for t in range(1, size):
        other = lax.rem(me + t, size)
        remote(rows_of(other), land(other), a_send.at[other], a_recv.at[other], other).wait_recv()
    for k in (4, 7, 8, 9, 10, 11, 12):
        wo_arrived(k).wait_recv()
    wo_here.wait()
    sl = width // 4
    total = jnp.zeros((own, 1), F32)
    for i in range(4):
        c = slice(i * sl, (i + 1) * sl)
        part = x_v[mine, c].astype(F32) + dot_nn(own_ref[...], wo_all[:, c])
        res_ref[:, c] = part
        total = total + jnp.sum(part * part, axis=1, keepdims=True)
    scale = lax.rsqrt(total / width + EPS)
    for i in range(4):
        c = slice(i * sl, (i + 1) * sl)
        moe_ref[:, c] = (res_ref[:, c] * scale * mg_ref[:, c]).astype(BF)
    for i in (11, 12):
        written(i).start()
    hand_on(g_arrived, g_copy, ((2, (9,)), (3, (10,)), (5, (11,)), (6, (12,))))
    for t in range(1, size):
        exchange(t, None).wait_send()
        send(lax.rem(me + t, size)).wait_send()
    for d in range(size):
        stored(d).wait()
    for k in (4, 7, 8, 9, 10, 11, 12):
        g_arrived(k).wait_recv()
    for k in range(GATHER_COPIES):
        copy(k).wait_send()
        wo_copy(k).wait_send()
        g_copy(k).wait_send()
    g_here.wait()
    for i in range(14):
        written(i).wait()


def hand_on(arrived, copy, steps):
    for k, following in steps:
        arrived(k).wait_recv()
        for f in following:
            copy(f).start()


def front(x, wo, g, wq, wk, wv, gain, qg, kg, mg, routes_t, seg_rows, experts, size, block, reach, capacity, cid):
    own, width = x.shape
    cols = wq.shape[1]
    tokens = own * size
    heads = cols // HEAD_DIM
    any_spec = pl.BlockSpec(memory_space=pl.ANY)
    vm = pl.BlockSpec(memory_space=pltpu.VMEM)
    arr = jax.ShapeDtypeStruct
    dma = pltpu.SemaphoreType.DMA
    kept = (
            arr((tokens, cols), BF),
            arr((tokens, cols), BF),
            arr((tokens, cols), BF),
            arr((tokens, cols), F32),
            arr((tokens, cols), F32),
            arr((tokens, 2), F32),
            arr((tokens, HEAD_DIM), F32),
            arr((tokens, HEAD_DIM), F32),
            arr((tokens, cols), F32),
            arr((tokens, cols), BF),
            arr((tokens, heads), F32),
            arr((own, width), F32),
            arr((own, width), BF),
            arr((tokens, experts), F32),
    )
    return pl.pallas_call(
        functools.partial(front_body, size=size, block=block, reach=reach, capacity=capacity),
        out_shape=(
            arr((tokens, width), BF),
            *kept,
            arr((tokens, width), BF),
        ),
        in_specs=[any_spec] * 6 + [vm] * 6,
        out_specs=[any_spec] * 16,
        scratch_shapes=[pltpu.VMEM(k.shape, k.dtype) for k in kept]
        + [
            pltpu.VMEM((tokens, width), BF),
            pltpu.VMEM((tokens, width), BF),
            pltpu.VMEM((width, 3 * cols), BF),
            pltpu.VMEM((width, width), BF),
            pltpu.VMEM((own, width), BF),
            pltpu.VMEM((size, 2, own), F32),
            pltpu.VMEM((size, size, 2, own), F32),
            pltpu.VMEM((size, 1, block), F32),
        ]
        + [dma((GATHER_COPIES,))] * 6
        + [dma((size,))] * 4
        + [
            dma((3,)),
            dma,
            dma,
            dma,
            dma,
            dma((size,)),
            dma((14,)),
        ],
        compiler_params=pltpu.CompilerParams(
            vmem_limit_bytes=58 * MIB, collective_id=cid, has_side_effects=True
        ),
        cost_estimate=pl.CostEstimate(flops=10**8, bytes_accessed=4 * MIB, transcendentals=0),
        name="front",
    )(x, wo, g, wq, wk, wv, gain[None, :], qg[None, :], kg[None, :], mg[None, :], routes_t, seg_rows)


def middle_body(
    own_hbm, g_hbm, mask_ref, router_ref, wg_ref, wu_ref, wd_ref,
    moe_hbm, dgu_hbm, ga_hbm, wcat_hbm, dots_hbm, grads_hbm, xt_hbm, gates_hbm, probs_hbm,
    x_v, xt_v, g_v, wcat, dgu_v, ga_v, dots_ref, grads_ref, gates_ref, probs_ref, part_sem, send_sem, recv_sem, own_sem, g_sem, m_sem, out_sem, *, size, parts
):
    me = lax.axis_index("tensor")
    tokens, width = x_v.shape
    own = tokens // size
    hid = wg_ref.shape[2]
    experts = gates_ref.shape[1]
    ds = width // parts

    def g_copy(d):
        r = pl.ds(d * own, own)
        return pltpu.make_async_copy(g_hbm.at[r], g_v.at[r], g_sem.at[d])

    mine = pl.ds(pl.multiple_of(me * own, own), own)
    own_copy = pltpu.make_async_copy(own_hbm, x_v.at[mine], own_sem)
    own_copy.start()
    greet([partner(me, b) for b in (1, 2, 4)])
    copy, arrived, pc, px, py, diag = gather_plan(own_hbm, x_v, me, own, send_sem, recv_sem)
    for k in range(5):
        copy(k).start()
    for d in range(size):
        g_copy(d).start()

    wcat[:, 0:hid] = wg_ref[0]
    wcat[:, hid : 2 * hid] = wg_ref[1]
    wcat[:, 2 * hid : 3 * hid] = wu_ref[0]
    wcat[:, 3 * hid : 4 * hid] = wu_ref[1]
    wcat_out = pltpu.make_async_copy(wcat, wcat_hbm.at[:, pl.ds(0, 4 * hid)], out_sem.at[0])
    wcat_out.start()
    own_copy.wait()
    for d in range(size):
        g_copy(d).wait()
    lane = lax.broadcasted_iota(jnp.int32, (own, experts), 1)

    def moe_out(dev):
        r = pl.ds(pl.multiple_of(dev * own, own), own)
        return pltpu.make_async_copy(x_v.at[r], moe_hbm.at[r], m_sem.at[dev])

    def process(dev):
        r = pl.ds(pl.multiple_of(dev * own, own), own)
        moe_out(dev).start()
        xt_v[:, r] = x_v[r, :].T
        logits = dot_nt(x_v[r, :], router_ref[...])
        grown = jnp.exp(logits - jnp.max(logits, axis=1, keepdims=True))
        probs = grown / jnp.sum(grown, axis=1, keepdims=True)
        probs_ref[r, :] = probs
        gate_rows = probs * mask_ref[r, :]
        gates_ref[r, :] = gate_rows
        gu = dot_nn(x_v[r, :], wcat[...])
        q = dot_nt(g_v[r, :], wd_ref[...])
        dots = jnp.zeros((own, experts), F32)
        for j in range(2):
            pre = gu[:, j * hid : (j + 1) * hid]
            up = gu[:, (2 + j) * hid : (3 + j) * hid]
            back = q[:, j * hid : (j + 1) * hid]
            here = lane == j
            gate = jnp.sum(jnp.where(here, gate_rows, 0.0), axis=1, keepdims=True)
            sig = jax.nn.sigmoid(pre)
            silu = pre * sig
            act = silu * up
            dot = jnp.sum(act * back, axis=1, keepdims=True)
            dots = dots + jnp.where(here, dot, 0.0)
            scaled = gate * back
            d_up = scaled * silu
            d_gate = scaled * up * (sig + silu * (1.0 - sig))
            dgu_v[r, j * hid : (j + 1) * hid] = d_gate.astype(BF)
            dgu_v[r, (2 + j) * hid : (3 + j) * hid] = d_up.astype(BF)
            ga_v[r, j * hid : (j + 1) * hid] = (gate * act).astype(BF)
        dots_ref[r, :] = dots

    process(me)
    arrived(4).wait_recv()
    process(pc)
    arrived(0).wait_recv()
    copy(5).start()
    copy(7).start()
    arrived(1).wait_recv()
    copy(6).start()
    copy(8).start()
    arrived(2).wait_recv()
    copy(9).start()
    arrived(3).wait_recv()
    copy(10).start()
    process(px)
    process(py)
    arrived(7).wait_recv()
    arrived(9).wait_recv()
    process(partner(px, 1))
    arrived(8).wait_recv()
    arrived(10).wait_recv()
    process(partner(py, 1))
    arrived(5).wait_recv()
    copy(11).start()
    arrived(6).wait_recv()
    copy(12).start()
    process(diag)
    arrived(11).wait_recv()
    arrived(12).wait_recv()
    process(partner(diag, 1))

    outs = [
        pltpu.make_async_copy(dgu_v, dgu_hbm.at[:, pl.ds(0, 4 * hid)], out_sem.at[1]),
        pltpu.make_async_copy(ga_v, ga_hbm.at[:, pl.ds(0, 2 * hid)], out_sem.at[2]),
        pltpu.make_async_copy(xt_v, xt_hbm, out_sem.at[3]),
        pltpu.make_async_copy(dots_ref, dots_hbm, out_sem.at[4]),
        pltpu.make_async_copy(gates_ref, gates_hbm, out_sem.at[5]),
        pltpu.make_async_copy(probs_ref, probs_hbm, out_sem.at[6]),
    ]
    for o in outs:
        o.start()
    for s in range(parts):
        gd = dot_tn(ga_v[...], g_v[:, s * ds : (s + 1) * ds]).astype(BF)
        gw = dot_nn(xt_v[s * ds : (s + 1) * ds, :], dgu_v[...]).astype(BF)
        for j in range(2):
            grads_ref[s, 3 * j] = gw[:, j * hid : (j + 1) * hid]
            grads_ref[s, 3 * j + 1] = gw[:, (2 + j) * hid : (3 + j) * hid]
            for c in range(ds // hid):
                grads_ref[s, 3 * j + 2, c * hid : (c + 1) * hid, :] = gd[
                    j * hid : (j + 1) * hid, c * hid : (c + 1) * hid
                ]
        part_out = pltpu.make_async_copy(grads_ref.at[s], grads_hbm.at[s], part_sem.at[s])
        part_out.start()
        outs.append(part_out)
    wcat_out.wait()
    for o in outs:
        o.wait()
    for d in range(size):
        moe_out(d).wait()
    for k in range(GATHER_COPIES):
        copy(k).wait_send()


def middle(own_rows, g, mask, router, wg, wu, wd, size, parts, cid):
    own, width = own_rows.shape
    tokens = own * size
    experts, _, hid = wg.shape
    total = experts // 2
    ds = width // parts
    any_spec = pl.BlockSpec(memory_space=pl.ANY)
    vm = pl.BlockSpec(memory_space=pltpu.VMEM)
    first = lambda shape: pl.BlockSpec(shape, lambda i: (0,) * len(shape))
    arr = jax.ShapeDtypeStruct
    dma = pltpu.SemaphoreType.DMA
    narrow = arr((tokens, experts), F32)
    return pl.pallas_call(
        functools.partial(middle_body, size=size, parts=parts),
        out_shape=(
            arr((tokens, width), BF),
            arr((tokens, total * 4 * hid), BF),
            arr((tokens, total * 2 * hid), BF),
            arr((width, total * 4 * hid), BF),
            narrow,
            arr((parts, 6, ds, hid), BF),
            arr((width, tokens), BF),
            narrow,
            narrow,
        ),
        grid=(1,),
        in_specs=[
            any_spec,
            any_spec,
            first((tokens, experts)),
            first(router.shape),
            first((2, width, hid)),
            first((2, width, hid)),
            first((2 * hid, width)),
        ],
        out_specs=[any_spec] * 9,
        scratch_shapes=[
            pltpu.VMEM((tokens, width), BF),
            pltpu.VMEM((width, tokens), BF),
            pltpu.VMEM((tokens, width), BF),
            pltpu.VMEM((width, 4 * hid), BF),
            pltpu.VMEM((tokens, 4 * hid), BF),
            pltpu.VMEM((tokens, 2 * hid), BF),
            pltpu.VMEM((tokens, experts), F32),
            pltpu.VMEM((parts, 6, ds, hid), BF),
            pltpu.VMEM((tokens, experts), F32),
            pltpu.VMEM((tokens, experts), F32),
            dma((parts,)),
            dma((GATHER_COPIES,)),
            dma((GATHER_COPIES,)),
            dma,
            dma((size,)),
            dma((size,)),
            dma((7,)),
        ],
        compiler_params=pltpu.CompilerParams(
            vmem_limit_bytes=62 * MIB, collective_id=cid, has_side_effects=True
        ),
        cost_estimate=pl.CostEstimate(flops=10**9, bytes_accessed=4 * MIB, transcendentals=0),
        name="middle",
    )(own_rows, g, mask, router, wg, wu, wd)


def matmul_scatter_body(
    l_hbm, r_hbm, out_ref, l_v, r_v, part, got1, got2, got3, sem_l, sem_r, send_sem, recv_sem,
    *, size, slices, nt
):
    me = lax.axis_index("tensor")
    tokens = l_v.shape[0]
    own = tokens // size
    sn = out_ref.shape[1] // slices
    mine = [(me // b) % 2 for b in (1, 2, 4)]
    group = 2

    def l_copy(i):
        r = pl.ds(i * own * group, own * group)
        return pltpu.make_async_copy(l_hbm.at[r], l_v.at[r], sem_l.at[i])

    def r_copy(s):
        c = pl.ds(s * sn, sn)
        if nt:
            return pltpu.make_async_copy(r_hbm.at[c], r_v.at[c], sem_r.at[s])
        return pltpu.make_async_copy(r_hbm.at[:, c], r_v.at[:, c], sem_r.at[s])

    r_copy(0).start()
    for i in range(size // group):
        l_copy(i).start()
    for s in range(1, slices):
        r_copy(s).start()
    greet([partner(me, b) for b in (1, 2, 4)])

    def hop(s, stage):
        a, b = (1, 2) if s % 2 == 0 else (2, 1)
        if stage == 0:
            src, dst, bit = part.at[s, 1 - mine[0]], got1.at[s], 1
        elif stage == 1:
            src, dst, bit = part.at[s, mine[0], pl.ds(2 * (1 - mine[a]), 2)], got2.at[s], 1 << a
        else:
            src, dst, bit = part.at[s, mine[0], 2 * mine[a] + 1 - mine[b]], got3.at[s], 1 << b
        return remote(src, dst, send_sem.at[stage, s], recv_sem.at[stage, s], partner(me, bit))

    def compute(s):
        r_copy(s).wait()

        def rows(i, _):
            if s == 0:
                l_copy(i).wait()
            r = pl.ds(pl.multiple_of(i * own * group, own * group), own * group)
            if nt:
                res = dot_nt(l_v[r, :], r_v[s * sn : (s + 1) * sn, :])
            else:
                res = dot_nn(l_v[r, :], r_v[:, s * sn : (s + 1) * sn])
            res = res.astype(BF)
            x, y = i % 2, i // 2
            pos = 2 * x + y if s % 2 == 0 else 2 * y + x
            for c in range(2):
                part[s, c, pos] = res[c * own : (c + 1) * own]
            return 0

        lax.fori_loop(0, size // group, rows, 0)
        hop(s, 0).start()

    def first(s):
        hop(s, 0).wait_recv()
        part[s, mine[0]] = (part[s, mine[0]].astype(F32) + got1[s].astype(F32)).astype(BF)
        hop(s, 1).start()

    def second(s):
        a = 1 if s % 2 == 0 else 2
        hop(s, 1).wait_recv()
        ix = pl.ds(2 * mine[a], 2)
        part[s, mine[0], ix] = (part[s, mine[0], ix].astype(F32) + got2[s].astype(F32)).astype(BF)
        hop(s, 2).start()

    def third(s):
        a, b = (1, 2) if s % 2 == 0 else (2, 1)
        hop(s, 2).wait_recv()
        out_ref[:, s * sn : (s + 1) * sn] = part[s, mine[0], 2 * mine[a] + mine[b]].astype(
            F32
        ) + got3[s].astype(F32)

    for t in range(slices + 5):
        if t < slices:
            compute(t)
        if 0 <= t - 1 < slices:
            first(t - 1)
        if 0 <= t - 3 < slices:
            second(t - 3)
        if 0 <= t - 5 < slices:
            third(t - 5)
    for s in range(slices):
        for stage in range(3):
            hop(s, stage).wait_send()


def matmul_scatter(left, right, size, cid, nt, name):
    tokens, depth = left.shape
    width = right.shape[0] if nt else right.shape[1]
    own = tokens // size
    if size != 8:
        part = (dot_nt if nt else dot_nn)(left, right).astype(BF)
        return lax.psum_scatter(part, "tensor", scatter_dimension=0, tiled=True).astype(F32)
    slices = 8
    sn = width // slices
    any_spec = pl.BlockSpec(memory_space=pl.ANY)
    return pl.pallas_call(
        functools.partial(matmul_scatter_body, size=size, slices=slices, nt=nt),
        out_shape=jax.ShapeDtypeStruct((own, width), F32),
        in_specs=[any_spec, any_spec],
        out_specs=pl.BlockSpec(memory_space=pltpu.VMEM),
        scratch_shapes=[
            pltpu.VMEM(left.shape, BF),
            pltpu.VMEM(right.shape, BF),
            pltpu.VMEM((slices, 2, size // 2, own, sn), BF),
            pltpu.VMEM((slices, size // 2, own, sn), BF),
            pltpu.VMEM((slices, size // 4, own, sn), BF),
            pltpu.VMEM((slices, own, sn), BF),
            pltpu.SemaphoreType.DMA((size // 2,)),
            pltpu.SemaphoreType.DMA((slices,)),
            pltpu.SemaphoreType.DMA((3, slices)),
            pltpu.SemaphoreType.DMA((3, slices)),
        ],
        compiler_params=pltpu.CompilerParams(
            vmem_limit_bytes=60 * MIB, collective_id=cid, has_side_effects=True
        ),
        cost_estimate=pl.CostEstimate(
            flops=10**9, bytes_accessed=4 * MIB, transcendentals=0
        ),
        name=name,
    )(left, right)


def gather_body(x_ref, out_ref, send_sem, recv_sem, here_sem):
    me = lax.axis_index("tensor")
    own = x_ref.shape[0]
    greet([partner(me, b) for b in (1, 2, 4)])
    mine = pl.ds(pl.multiple_of(me * own, own), own)
    here = pltpu.make_async_copy(x_ref, out_ref.at[mine], here_sem)
    here.start()
    copy, arrived = gather_plan(x_ref, out_ref, me, own, send_sem, recv_sem)[:2]
    for k in range(5):
        copy(k).start()
    for k, following in ((0, (5, 7)), (1, (6, 8)), (2, (9,)), (3, (10,)), (5, (11,)), (6, (12,))):
        arrived(k).wait_recv()
        for f in following:
            copy(f).start()
    for k in (4, 7, 8, 9, 10, 11, 12):
        arrived(k).wait_recv()
    for k in range(GATHER_COPIES):
        copy(k).wait_send()
    here.wait()


def gather_all(value, size, cid, name):
    own, cols = value.shape
    if size != 8:
        return lax.all_gather(value, "tensor", axis=0, tiled=True)
    any_spec = pl.BlockSpec(memory_space=pl.ANY)
    return pl.pallas_call(
        gather_body,
        out_shape=jax.ShapeDtypeStruct((own * size, cols), value.dtype),
        in_specs=[any_spec],
        out_specs=any_spec,
        scratch_shapes=[
            pltpu.SemaphoreType.DMA((GATHER_COPIES,)),
            pltpu.SemaphoreType.DMA((GATHER_COPIES,)),
            pltpu.SemaphoreType.DMA,
        ],
        compiler_params=pltpu.CompilerParams(collective_id=cid, has_side_effects=True),
        cost_estimate=pl.CostEstimate(flops=0, bytes_accessed=4 * MIB, transcendentals=0),
        name=name,
    )(value)


def swap(value, axis, size, bit):
    return lax.ppermute(value, axis, [(i, i ^ bit) for i in range(size)])


def sum_all(value, axis, size):
    bit = 1
    while bit < size:
        value = value + swap(value, axis, size, bit)
        bit *= 2
    return value


def sum_everywhere(value, n_tensor, n_dp):
    me = lax.axis_index("tensor")
    bits = [1 << b for b in range(n_tensor.bit_length() - 1)]
    for bit in bits[::-1]:
        half = value.shape[1] // 2
        low, high = value[:, :half], value[:, half:]
        upper = (me // bit) % 2 == 1
        send = jnp.where(upper, low, high)
        value = jnp.where(upper, high, low) + swap(send, "tensor", n_tensor, bit)
    value = sum_all(value, "dp", n_dp)
    for bit in bits:
        got = swap(value, "tensor", n_tensor, bit)
        upper = (me // bit) % 2 == 1
        value = jnp.concatenate(
            [jnp.where(upper, got, value), jnp.where(upper, value, got)], axis=1
        )
    return value


def half_swap(values):
    pieces = []
    half = HEAD_DIM // 2
    for h in range(values.shape[1] // HEAD_DIM):
        base = h * HEAD_DIM
        pieces += [values[:, base + half : base + HEAD_DIM], values[:, base : base + half]]
    return jnp.concatenate(pieces, axis=1)


def document_blocks(segments, block):
    seg = segments.reshape(-1)
    tokens = seg.shape[0]
    values16 = jnp.arange(16, dtype=jnp.int32)
    below = jnp.sum((seg[None, :] < values16[:, None]).astype(jnp.int32), axis=1)
    doc_start = jnp.sum(
        jnp.where(seg[:, None] == values16[None, :], below[None, :], 0), axis=1
    )
    positions = jnp.arange(tokens, dtype=jnp.int32) - doc_start
    return (
        seg[:, None],
        seg.reshape(tokens // block, 1, block),
        doc_start[::block] // block,
        positions.astype(F32)[:, None],
    )


def routing_mask(routes, experts, capacity, block):
    tokens = routes.shape[0]
    expert_ids = jnp.arange(experts, dtype=jnp.int32)
    routed = jnp.sum(
        (routes[:, :, None] == expert_ids[None, None, :]).astype(F32), axis=1
    )
    tri = (
        jnp.arange(block, dtype=jnp.int32)[:, None] > jnp.arange(block, dtype=jnp.int32)[None, :]
    ).astype(BF)
    nb = tokens // block
    routed_b = routed.reshape(nb, block, experts)
    within = jnp.einsum("ij,bje->bie", tri, routed_b.astype(BF), preferred_element_type=F32)
    sums = jnp.sum(routed_b, axis=1)
    before = jnp.sum(
        jnp.where(
            (jnp.arange(nb)[:, None] > jnp.arange(nb)[None, :])[:, :, None], sums[None, :, :], 0.0
        ),
        axis=1,
    )
    place = within + before[:, None, :]
    return (routed_b * (place < capacity).astype(F32)).reshape(tokens, experts)


def per_device(
    block_input, segments, routes, w_query, w_key, w_value, w_output, attn_gain, query_gain, key_gain,
    moe_gain, router, w_gate, w_up, w_down, cotangent, *, n_dp, n_tensor
):
    own_rows, model_width = block_input.shape
    local_cols = w_query.shape[1]
    local_heads = local_cols // HEAD_DIM
    token_count = segments.shape[0] * segments.shape[1]
    experts = router.shape[1]
    top_count = routes.shape[1]
    hid = w_gate.shape[2]
    capacity = 5 * token_count * top_count // (4 * experts)
    me = lax.axis_index("tensor")
    rank_start = me * own_rows
    col_start = me * local_cols
    block = 256

    w_qkv = jnp.concatenate([w_query, w_key, w_value], axis=1)
    input_own = block_input.astype(F32)
    wd_flat = w_down.reshape(experts * hid, model_width)
    reach = min(1024 // block, token_count // block)
    if n_tensor == 8:
        (
            normed, queries, keys_rot, value_low, query_unit, key_unit, scales, cos_one, sin_one,
            attended, attn_low, lse, residual, own_moe_in, mask, full_cot,
        ) = front(
            block_input, w_output, cotangent, w_query, w_key, w_value, attn_gain, query_gain, key_gain, moe_gain,
            routes.T, segments.reshape(token_count // block, 1, block),
            experts, n_tensor, block, reach, capacity, 6,
        )
        segments, own_moe_in = lax.optimization_barrier((segments, own_moe_in))
        seg_col, seg_rows, lo_block = document_blocks(segments, block)[:3]
        query_rs, key_rs = scales[:, 0:1], scales[:, 1:2]
        cos_all = jnp.concatenate([cos_one] * local_heads, axis=1)
        sin_all = jnp.concatenate([sin_one] * local_heads, axis=1)
        lead = middle(
            own_moe_in, full_cot, mask, router.T, w_gate, w_up, wd_flat, n_tensor, n_dp, 1
        )
        moe_in, lead = lead[0], lead[1:]
    else:
        seg_col, seg_rows, lo_block, pos_col = document_blocks(segments, block)
        mask = routing_mask(routes, experts, capacity, block)
        half = HEAD_DIM // 2
        frequency = jnp.exp(
            jnp.arange(half, dtype=F32) * (-2.0 * math.log(10000.0) / HEAD_DIM)
        )
        angles = pos_col * frequency[None, :]
        cosine, sine = jnp.cos(angles), jnp.sin(angles)
        cos_all = jnp.concatenate([cosine] * (2 * local_heads), axis=1)
        sin_all = jnp.concatenate([-sine, sine] * local_heads, axis=1)
        full_cot = lax.all_gather(cotangent, "tensor", axis=0, tiled=True)
        full_wo = lax.all_gather(w_output, "tensor", axis=0, tiled=True)
        input_wide = lax.all_gather(block_input, "tensor", axis=0, tiled=True).astype(F32)
        normed = (input_wide * rms_scale(input_wide) * attn_gain).astype(BF)
        qkv = dot_nn(normed, w_qkv)
        query_raw = qkv[:, :local_cols]
        key_raw = qkv[:, local_cols : 2 * local_cols]
        value_low = qkv[:, 2 * local_cols :].astype(BF)
        squares = jnp.stack(
            [jnp.sum(query_raw * query_raw, axis=1), jnp.sum(key_raw * key_raw, axis=1)]
        )
        squares = sum_all(squares, "tensor", n_tensor)
        scales = lax.rsqrt(squares / model_width + EPS)
        query_rs, key_rs = scales[0][:, None], scales[1][:, None]
        query_unit = query_raw * query_rs
        key_unit = key_raw * key_rs
        q_n = query_unit * query_gain
        k_n = key_unit * key_gain
        queries = (q_n * cos_all + half_swap(q_n) * sin_all).astype(BF)
        keys_rot = (k_n * cos_all + half_swap(k_n) * sin_all).astype(BF)
        attended, attn_low, lse, own_attn = attn_fwd(
            queries, keys_rot, value_low, seg_col, seg_rows, block, reach, n_tensor, 0
        )
        residual = input_own + dot_nn(own_attn, full_wo)
        own_moe_in = (residual * rms_scale(residual) * moe_gain).astype(BF)
        moe_in = lax.all_gather(own_moe_in, "tensor", axis=0, tiled=True)
        lead = expert_chunk(
            moe_in, full_cot, mask, w_gate, w_up, wd_flat, router, None, first=0, pairs=1, parts=n_dp
        )
    scale_two = rms_scale(residual)

    chunks = (1, 3, 4)
    dots = None
    reduced = []
    carried = None
    first = 0
    for count in chunks:
        res = lead if first == 0 else expert_chunk(
            moe_in, full_cot, gates, w_gate, w_up, wd_flat, router, carried,
            first=first, pairs=count, parts=n_dp,
        )
        dgu, ga, wcat, dot_c, grads = res[:5]
        if first == 0:
            xt, gates, router_probs = res[5:]
        if len(reduced) == 2:
            reduced[0], dgu = lax.optimization_barrier((reduced[0], dgu))
        carried = (xt, dgu, ga, wcat)
        dots = dot_c if dots is None else dots + dot_c
        reduced.append(lax.psum_scatter(grads, "dp", scatter_dimension=0, tiled=False))
        first += count
    moe_back = matmul_scatter(dgu, wcat, n_tensor, 2, True, "moe_back")

    own_dots = jnp.sum(
        lax.all_to_all(dots.reshape(n_tensor, own_rows, experts), "tensor", 0, 0), axis=0
    )
    own_mask = lax.dynamic_slice_in_dim(mask, rank_start, own_rows, 0)
    own_probs = lax.dynamic_slice_in_dim(router_probs, rank_start, own_rows, 0)
    prob_grads = own_dots * own_mask
    own_logit = (
        own_probs * (prob_grads - jnp.sum(own_probs * prob_grads, axis=1, keepdims=True))
    ).astype(BF)
    router_grad = dot_tn(own_logit, own_moe_in)
    moe_grad = moe_back + dot_nt(own_logit, router)

    unit_two = residual * scale_two
    moe_gain_grad = jnp.sum(moe_grad * unit_two, axis=0)
    scaled_two = moe_grad * moe_gain
    residual_grad = cotangent.astype(F32) + scale_two * (
        scaled_two - unit_two * jnp.mean(scaled_two * unit_two, axis=1, keepdims=True)
    )
    residual_low = gather_all(residual_grad.astype(BF), n_tensor, 3, "gather_residual")
    output_grad = dot_tn(residual_low, attn_low).astype(BF)
    heads_grad = dot_nt(residual_low, w_output).astype(BF)

    dq_rot, dk_rot, dv = attn_bwd(
        lo_block, queries, keys_rot, value_low, heads_grad, attended, lse, seg_col, seg_rows, block
    )
    reduced[1], dq_rot = lax.optimization_barrier((reduced[1], dq_rot))
    query_norm_grad = dq_rot * cos_all - half_swap(dq_rot) * sin_all
    key_norm_grad = dk_rot * cos_all - half_swap(dk_rot) * sin_all
    query_gain_grad = jnp.sum(query_norm_grad * query_unit, axis=0)
    key_gain_grad = jnp.sum(key_norm_grad * key_unit, axis=0)
    query_scaled = query_norm_grad * query_gain
    key_scaled = key_norm_grad * key_gain
    inner = jnp.stack(
        [jnp.sum(query_scaled * query_unit, axis=1), jnp.sum(key_scaled * key_unit, axis=1)]
    )
    inner = sum_all(inner, "tensor", n_tensor) / model_width
    query_grad_low = (query_rs * (query_scaled - query_unit * inner[0][:, None])).astype(BF)
    key_grad_low = (key_rs * (key_scaled - key_unit * inner[1][:, None])).astype(BF)
    qkv_grad = jnp.concatenate([query_grad_low, key_grad_low, dv.astype(BF)], axis=1)
    qkv_w_grad = dot_tn(normed, qkv_grad).astype(BF)
    normed_grad = matmul_scatter(qkv_grad, w_qkv, n_tensor, 4, True, "normed_back")
    ga, qkv_w_grad = lax.optimization_barrier((ga, qkv_w_grad))
    moe_out = matmul_scatter(ga, wd_flat, n_tensor, 5, False, "moe_out")
    block_output = (residual + moe_out).astype(BF)
    scale_own = rms_scale(input_own)
    unit_one = input_own * scale_own
    attn_gain_grad = jnp.sum(normed_grad * unit_one, axis=0)
    scaled_one = normed_grad * attn_gain
    grad_input = residual_grad + scale_own * (
        scaled_one - unit_one * jnp.mean(scaled_one * unit_one, axis=1, keepdims=True)
    )

    proj_grad = jnp.concatenate([qkv_w_grad, output_grad], axis=1)
    reduced[2], proj_grad, block_output, grad_input = lax.optimization_barrier(
        (reduced[2], proj_grad, block_output, grad_input)
    )
    qkv_red = lax.psum_scatter(proj_grad, "dp", scatter_dimension=0, tiled=True)
    wo_red = qkv_red[:, 3 * local_cols :].T.astype(F32)
    gains = jnp.concatenate(
        [
            router_grad,
            moe_gain_grad[None, :],
            attn_gain_grad[None, :],
            lax.dynamic_update_slice_in_dim(
                jnp.zeros((1, model_width), F32), query_gain_grad[None, :], col_start, 1
            ),
            lax.dynamic_update_slice_in_dim(
                jnp.zeros((1, model_width), F32), key_gain_grad[None, :], col_start, 1
            ),
        ],
        axis=0,
    )
    gains = sum_everywhere(gains, n_tensor, n_dp)

    ds = model_width // n_dp
    gate_out, up_out, down_out = [], [], []
    for r, count in zip(reduced, chunks):
        r = r.reshape(2 * count, 3, ds, hid)
        gate_out.append(r[:, 0])
        up_out.append(r[:, 1])
        down = r[:, 2].reshape(2 * count, ds // hid, hid, hid)
        down_out.append(down.transpose(0, 2, 1, 3).reshape(2 * count, hid, ds))
    grad_gate = jnp.concatenate(gate_out, axis=0).astype(F32)
    grad_up = jnp.concatenate(up_out, axis=0).astype(F32)
    grad_down = jnp.concatenate(down_out, axis=0).astype(F32)
    return (
        block_output,
        grad_input,
        qkv_red[:, :local_cols].astype(F32),
        qkv_red[:, local_cols : 2 * local_cols].astype(F32),
        qkv_red[:, 2 * local_cols : 3 * local_cols].astype(F32),
        wo_red,
        gains[experts + 1],
        gains[experts + 2],
        gains[experts + 3],
        gains[experts],
        gains[:experts].T,
        grad_gate,
        grad_up,
        grad_down,
    )


def solution(mesh):
    rows = P(("dp", "tensor"), None)
    cols = P(None, "tensor")
    wide = P(None, None, "tensor")
    placed = (
        rows, P("dp", None), P("dp", None), cols, cols, cols, P("tensor", None), P(), P("tensor"), P("tensor"),
        P(), P(), wide, wide, P(None, "tensor", None), rows,
    )
    outs = (
        rows, rows, P("dp", "tensor"), P("dp", "tensor"), P("dp", "tensor"), P("tensor", "dp"), P(), P(), P(), P(),
        P(), P(None, "dp", "tensor"), P(None, "dp", "tensor"), P(None, "tensor", "dp"),
    )
    return jax.shard_map(
        functools.partial(
            per_device, n_dp=mesh.shape["dp"], n_tensor=mesh.shape["tensor"]
        ),
        mesh=mesh,
        in_specs=placed,
        out_specs=outs,
        check_vma=False,
    )
```
